32 devices in a mesh: wide: 8 (over z, y), narrow: 4 (over x, core).
Axes of the slice: x: 2, y: 2, z: 4, core: 2. Of those that a mesh axis runs over, the one named last changes fastest.
Arguments:
- populations: float32 [19, 16, 128, 512], P(None, 'wide', None, 'narrow'), may hold values from 0 to 1, as said below
- conformation: float32 [6, 16, 128, 512], P(None, 'wide', None, 'narrow'), may hold values from -0.3 to 3, as said below
Outputs:
- read: float32 [19, 16, 128, 512], P(None, 'wide', None, 'narrow')
- new_conformation: float32 [6, 16, 128, 512], P(None, 'wide', None, 'narrow')
The draws below stay inside these ranges and needn't reach their ends.
Inputs may be any that keep to these rules, and one draw needn't show every extreme that they name: Every population is positive, and the populations of a cell sum to between 0.6 and 1.4. Each cell's conformation tensor is symmetric and diagonally dominant with positive diagonal, its trace at most 9.
All inputs are finite; a program needn't handle non-finite values.
Results may differ from the reference program's by a relative error of at most 0.00002.
Values sent between devices are 32-bit elements; how exact they have to be, the bound alone decides.
No kernel may reach another device: no remote copies, remote signals or barrier semaphores. Data moves between devices by JAX's collectives and lax.ppermute only.
A program may use at most 192 MiB of HBM per device.

```python
import jax
import jax.numpy as jnp

NY = 128
NX = 16
NZ = 512


VELOCITIES = ((0, 0, 0), (1, 0, 0), (-1, 0, 0), (0, 1, 0), (0, -1, 0), (0, 0, 1), (0, 0, -1), (1, 1, 0), (-1, -1, 0), (1, -1, 0), (-1, 1, 0), (1, 0, 1), (-1, 0, -1), (1, 0, -1), (-1, 0, 1), (0, 1, 1), (0, -1, -1), (0, 1, -1), (0, -1, 1))


LATTICE_WEIGHTS = (1.0 / 3.0,) + (1.0 / 18.0,) * 6 + (1.0 / 36.0,) * 12


def draw_populations(key, part):
    key_dens, key_velo, key_noise = jax.random.split(jax.random.fold_in(key, 11), 3)
    cells = (NX, NY, NZ)
    density = jax.random.uniform(key_dens, cells, jnp.float32, 0.85, 1.15)
    velocity = jax.random.uniform(key_velo, (3,) + cells, jnp.float32, -0.08, 0.08)
    noise = 0.05 * jnp.clip(jax.random.normal(key_noise, (19,) + cells, jnp.float32), -3.0, 3.0)
    speed_sq = velocity[0] * velocity[0] + velocity[1] * velocity[1] + velocity[2] * velocity[2]
    parts = []
    for number in range(19):
        vec = VELOCITIES[number]
        along = vec[0] * velocity[0] + vec[1] * velocity[1] + vec[2] * velocity[2]
        equil = density * (1.0 + 3.0 * along + 4.5 * along * along - 1.5 * speed_sq)
        parts.append(LATTICE_WEIGHTS[number] * (equil + noise[number]))
    return jnp.stack(parts).astype(jnp.float32)


def draw_conformation(key, part):
    key_diag, key_off = jax.random.split(jax.random.fold_in(key, 23), 2)
    cells = (NX, NY, NZ)
    diagonal = jax.random.uniform(key_diag, (3,) + cells, jnp.float32, 0.6, 2.5)
    offdiag = jax.random.uniform(key_off, (3,) + cells, jnp.float32, -0.3, 0.3)
    return jnp.concatenate([diagonal, offdiag], axis=0).astype(jnp.float32)


def setup_inputs(seed: int = 0) -> dict:
    streams_of = jax.random.split(jax.random.key(seed), 3)
    return {
        "populations": draw_populations(jax.random.fold_in(streams_of[2], 71), 0),
        "conformation": draw_conformation(jax.random.fold_in(streams_of[2], 71), 0),
    }


VELOCITIES = ((0, 0, 0), (1, 0, 0), (-1, 0, 0), (0, 1, 0), (0, -1, 0), (0, 0, 1), (0, 0, -1),
              (1, 1, 0), (-1, -1, 0), (1, -1, 0), (-1, 1, 0), (1, 0, 1), (-1, 0, -1), (1, 0, -1),
              (-1, 0, 1), (0, 1, 1), (0, -1, -1), (0, 1, -1), (0, -1, 1))
LATTICE_WEIGHTS = (1.0 / 3.0,) + (1.0 / 18.0,) * 6 + (1.0 / 36.0,) * 12
OPPOSITE = (0, 2, 1, 4, 3, 6, 5, 8, 7, 10, 9, 12, 11, 14, 13, 16, 15, 18, 17)
SYMMETRIC_INDEX = ((0, 3, 4), (3, 1, 5), (4, 5, 2))
COMPONENT_PAIRS = ((0, 0), (1, 1), (2, 2), (0, 1), (0, 2), (1, 2))
SOLVENT_TIME = 0.8
RELAX_TIME = 20.0
POLYMER_VISC = 1.0
EXTENSION_SQ = 100.0
DIFFUSIVITY = 0.05
DRIVE_FORCE = 1e-5


def wall_pad(field, odd):
    lower = field[:, :, :1]
    upper = field[:, :, -1:]
    if odd:
        lower, upper = -lower, -upper
    return jnp.concatenate([lower, field, upper], axis=2)


def gradients(padded, odd):
    centre = padded[:, 1:-1, :, 1:-1]
    walled = wall_pad(centre, odd)
    along_x = 0.5 * (padded[:, 2:, :, 1:-1] - padded[:, :-2, :, 1:-1])
    along_y = 0.5 * (walled[:, :, 2:] - walled[:, :, :-2])
    along_z = 0.5 * (padded[:, 1:-1, :, 2:] - padded[:, 1:-1, :, :-2])
    return along_x, along_y, along_z


def laplacian(padded):
    centre = padded[:, 1:-1, :, 1:-1]
    walled = wall_pad(centre, False)
    total = padded[:, 2:, :, 1:-1] + padded[:, :-2, :, 1:-1]
    total = total + walled[:, :, 2:] + walled[:, :, :-2]
    total = total + padded[:, 1:-1, :, 2:] + padded[:, 1:-1, :, :-2]
    return total - 6.0 * centre


def peterlin_of(conform):
    trace = conform[0] + conform[1] + conform[2]
    return (EXTENSION_SQ - 3.0) / (EXTENSION_SQ - trace)


def relaxed_part(conform, peterlin):
    parts = []
    for number in range(6):
        term = peterlin * conform[number]
        if number < 3:
            term = term - 1.0
        parts.append(term)
    return jnp.stack(parts)


def polymer_force(padded_conf):
    stress = (POLYMER_VISC / RELAX_TIME) * relaxed_part(padded_conf, peterlin_of(padded_conf))
    along_x, along_y, along_z = gradients(stress, False)
    parts = []
    for first in range(3):
        row = SYMMETRIC_INDEX[first]
        term = along_x[row[0]] + along_y[row[1]] + along_z[row[2]]
        if first == 0:
            term = term + DRIVE_FORCE
        parts.append(term)
    return jnp.stack(parts)


def moments(popul, force):
    density = jnp.sum(popul, axis=0)
    parts = []
    for axis_num in range(3):
        moment = jnp.zeros_like(density)
        for number in range(19):
            weight_c = VELOCITIES[number][axis_num]
            if weight_c == 1:
                moment = moment + popul[number]
            elif weight_c == -1:
                moment = moment - popul[number]
        parts.append((moment + 0.5 * force[axis_num]) / density)
    return density, jnp.stack(parts)


def conform_update(padded_conf, velocity, padded_velocity):
    conform = padded_conf[:, 1:-1, :, 1:-1]
    grad_c = gradients(padded_conf, False)
    grad_v = gradients(padded_velocity, True)
    advect = velocity[0] * grad_c[0] + velocity[1] * grad_c[1] + velocity[2] * grad_c[2]
    stretch_list = []
    for first, second in COMPONENT_PAIRS:
        term = jnp.zeros_like(conform[0])
        for inner in range(3):
            term = term + conform[SYMMETRIC_INDEX[first][inner]] * grad_v[inner][second]
            term = term + grad_v[inner][first] * conform[SYMMETRIC_INDEX[inner][second]]
        stretch_list.append(term)
    stretch = jnp.stack(stretch_list)
    relax = relaxed_part(conform, peterlin_of(conform)) / RELAX_TIME
    return conform - advect + stretch - relax + DIFFUSIVITY * laplacian(padded_conf)


def collide(popul, density, velocity, force):
    speed_sq = velocity[0] * velocity[0] + velocity[1] * velocity[1] + velocity[2] * velocity[2]
    factor = 1.0 - 0.5 / SOLVENT_TIME
    parts = []
    for number in range(19):
        vec = VELOCITIES[number]
        weight = LATTICE_WEIGHTS[number]
        along = vec[0] * velocity[0] + vec[1] * velocity[1] + vec[2] * velocity[2]
        equil = weight * density * (1.0 + 3.0 * along + 4.5 * along * along - 1.5 * speed_sq)
        push = 0.0
        for axis_num in range(3):
            push = push + 3.0 * (vec[axis_num] - velocity[axis_num]) * force[axis_num]
            push = push + 9.0 * along * vec[axis_num] * force[axis_num]
        parts.append(popul[number] - (popul[number] - equil) / SOLVENT_TIME + factor * weight * push)
    return jnp.stack(parts)


def wall_walk(shifted, bounced, step_y):
    if step_y == 1:
        return jnp.concatenate([bounced[:, :1], shifted[:, :-1]], axis=1)
    if step_y == -1:
        return jnp.concatenate([shifted[:, 1:], bounced[:, -1:]], axis=1)
    return shifted


def wrap_pad(field, width):
    return jnp.pad(field, ((0, 0), (width, width), (0, 0), (width, width)), mode="wrap")


def reference(populations, conformation):
    padded_conf = wrap_pad(conformation, 1)
    force = polymer_force(padded_conf)
    density, velocity = moments(populations, force)
    padded_velocity = wrap_pad(velocity, 1)
    new_conformation = conform_update(padded_conf, velocity, padded_velocity)
    post = collide(populations, density, velocity, force)
    parts = []
    for number in range(19):
        vec = VELOCITIES[number]
        shifted = jnp.roll(post[number], (vec[0], vec[2]), axis=(0, 2))
        parts.append(wall_walk(shifted, post[OPPOSITE[number]], vec[1]))
    return jnp.stack(parts), new_conformation
```

```python
import functools

import jax
import jax.numpy as jnp
from jax import lax
from jax.experimental import pallas as pl
from jax.experimental.pallas import tpu as pltpu
from jax.sharding import PartitionSpec as P

VELOCITIES = (
    (0, 0, 0),
    (1, 0, 0),
    (-1, 0, 0),
    (0, 1, 0),
    (0, -1, 0),
    (0, 0, 1),
    (0, 0, -1),
    (1, 1, 0),
    (-1, -1, 0),
    (1, -1, 0),
    (-1, 1, 0),
    (1, 0, 1),
    (-1, 0, -1),
    (1, 0, -1),
    (-1, 0, 1),
    (0, 1, 1),
    (0, -1, -1),
    (0, 1, -1),
    (0, -1, 1),
)
LATTICE_WEIGHTS = (1.0 / 3.0,) + (1.0 / 18.0,) * 6 + (1.0 / 36.0,) * 12
OPPOSITE = (0, 2, 1, 4, 3, 6, 5, 8, 7, 10, 9, 12, 11, 14, 13, 16, 15, 18, 17)
SYMMETRIC_INDEX = ((0, 3, 4), (3, 1, 5), (4, 5, 2))
COMPONENT_PAIRS = ((0, 0), (1, 1), (2, 2), (0, 1), (0, 2), (1, 2))
SOLVENT_TIME = 0.8
RELAX_TIME = 20.0
POLYMER_VISC = 1.0
EXTENSION_SQ = 100.0
DIFFUSIVITY = 0.05
DRIVE_FORCE = 1e-05
STRESS_SCALE = POLYMER_VISC / RELAX_TIME

SLOT_SHIFTS = ((0, 0), (1, 0), (-1, 0), (0, 1), (0, -1))
PLUS = tuple(VELOCITIES.index((1, cy, cz)) for cy, cz in SLOT_SHIFTS)
MINUS = tuple(VELOCITIES.index((-1, cy, cz)) for cy, cz in SLOT_SHIFTS)
Z_UP = tuple(VELOCITIES.index(v) for v in ((0, 0, 1), (0, 1, 1), (0, -1, 1), (1, 0, 1), (-1, 0, 1)))
Z_DOWN = tuple(
    VELOCITIES.index(v) for v in ((0, 0, -1), (0, 1, -1), (0, -1, -1), (1, 0, -1), (-1, 0, -1))
)
ROWS = 8
F32 = jnp.float32
VMEM = pltpu.VMEM


def vmem_spec():
    return pl.BlockSpec(memory_space=pltpu.VMEM)


def any_spec():
    return pl.BlockSpec(memory_space=pl.ANY)


def params():
    return pltpu.CompilerParams(vmem_limit_bytes=48 << 20)


def lanes_of(like):
    return lax.broadcasted_iota(jnp.int32, like.shape, 1)


def rolled(value, shift, axis=1):
    shift = shift % value.shape[axis]
    return value if shift == 0 else pltpu.roll(value, shift, axis)


def pack_columns(values, source, packed=None, base=0):
    lane = lanes_of(values[0])
    if packed is None:
        packed = jnp.zeros_like(values[0])
    for number, value in enumerate(values, base):
        packed = jnp.where(lane == number, rolled(value, number - source), packed)
    return packed


def for_rows(total, body):
    def step(number, carry):
        body(pl.multiple_of(number * ROWS, ROWS))
        return carry

    lax.fori_loop(0, total // ROWS, step, 0)


def peterlin_of(c_xx, c_yy, c_zz):
    return (EXTENSION_SQ - 3.0) / (EXTENSION_SQ - (c_xx + c_yy + c_zz))


def edge_kernel(far_ref, conf_ref, up_ref, down_ref, far_out):
    height, width = conf_ref.shape[2:]
    far = far_ref[0]

    def rows(start):
        at = pl.ds(start, ROWS)
        values = [conf_ref[f, p, at, :] for p in range(2) for f in range(6)]
        up_ref[at, :] = pack_columns(values, width - 1)
        down_ref[at, :] = pack_columns(values, 0)
        for f in range(6):
            far_out[f, at, :] = conf_ref[f, far, at, :]

    for_rows(height, rows)


def edges(far, conform):
    height, width = conform.shape[2:]
    tile = jax.ShapeDtypeStruct((height, width), F32)
    return pl.pallas_call(
        edge_kernel,
        out_shape=(tile, tile, jax.ShapeDtypeStruct((6, height, width), F32)),
        in_specs=[pl.BlockSpec(memory_space=pltpu.SMEM), vmem_spec()],
        out_specs=(vmem_spec(), vmem_spec(), vmem_spec()),
        compiler_params=params(),
        name="edges",
    )(far, conform)


def prepare_kernel(conf_ref, popul_ref, low_ref, high_ref, pre_ref, tall):
    height, width = conf_ref.shape[2:]

    def stress(fields, at_of):
        trace_parts = [at_of(f) for f in range(3)]
        peterlin = STRESS_SCALE * peterlin_of(*trace_parts)
        out = {}
        for f in fields:
            value = trace_parts[f] if f < 3 else at_of(f)
            out[f] = peterlin * value - (STRESS_SCALE if f < 3 else 0.0)
        return out

    for p in range(2):
        sign = 2 * p - 1

        def first(start, p=p, sign=sign):
            at = pl.ds(start, ROWS)
            own = stress(range(6), lambda f: conf_ref[f, p, at, :])
            other = stress((0, 3, 4), lambda f: conf_ref[f, 1 - p, at, :])
            low_pack = low_ref[at, :]
            high_pack = high_ref[at, :]
            low = stress((2, 4, 5), lambda f: rolled(low_pack, -(6 * p + f)))
            high = stress((2, 4, 5), lambda f: rolled(high_pack, width - 1 - (6 * p + f)))
            lane = lanes_of(low_pack)
            for number, f in enumerate((3, 1, 5)):
                tall[number, p, pl.ds(start + 8, ROWS), :] = own[f]
            for number in range(3):
                across = SYMMETRIC_INDEX[number][2]
                below = jnp.where(lane == 0, low[across], rolled(own[across], 1))
                above = jnp.where(lane == width - 1, high[across], rolled(own[across], -1))
                term = 0.5 * (above - below) - (0.5 * sign) * other[SYMMETRIC_INDEX[number][0]]
                if number == 0:
                    term = term + DRIVE_FORCE
                pre_ref[number, p, at, :] = term
            values = [popul_ref[i, p, at, :] for i in range(19)]
            density = values[0]
            for i in range(1, 19):
                density = density + values[i]
            pre_ref[3, p, at, :] = density
            for axis in range(3):
                moment = None
                for i in range(19):
                    if VELOCITIES[i][axis] == 1:
                        moment = values[i] if moment is None else moment + values[i]
                for i in range(19):
                    if VELOCITIES[i][axis] == -1:
                        moment = moment - values[i]
                pre_ref[4 + axis, p, at, :] = moment

        for_rows(height, first)
        for number in range(3):
            tall[number, p, 7:8, :] = tall[number, p, 8:9, :]
            tall[number, p, height + 8 : height + 9, :] = tall[number, p, height + 7 : height + 8, :]

        def second(start, p=p):
            at = pl.ds(start, ROWS)
            for number in range(3):
                above = tall[number, p, pl.ds(start + 9, ROWS), :]
                below = tall[number, p, pl.ds(start + 7, ROWS), :]
                pre_ref[number, p, at, :] = pre_ref[number, p, at, :] + 0.5 * (above - below)

        for_rows(height, second)


def prepare(conform, popul, low, high):
    height, width = conform.shape[2:]
    return pl.pallas_call(
        prepare_kernel,
        out_shape=jax.ShapeDtypeStruct((7, 2, height, width), F32),
        in_specs=[vmem_spec()] * 4,
        out_specs=vmem_spec(),
        scratch_shapes=[VMEM((3, 2, height + 16, width), F32)],
        compiler_params=params(),
        name="prepare",
    )(conform, popul, low, high)


def collide_kernel(second, plane_ref, popul_ref, pre_ref, halo_ref, *refs):
    if second:
        _, up_in, down_in, post_ref, message_ref, up_ref, down_ref = refs
    else:
        post_ref, message_ref, up_ref, down_ref = refs
    height, width = halo_ref.shape[1:]
    plane = plane_ref[0]
    outward_plus = plane == 1
    half_sign = jnp.where(outward_plus, 0.5, -0.5).astype(F32)
    factor = 1.0 - 0.5 / SOLVENT_TIME
    keep = 1.0 - 1.0 / SOLVENT_TIME
    base = 8 if second else 0

    def rows(start):
        at = pl.ds(start, ROWS)
        halo = [halo_ref[f, at, :] for f in range(5)]
        peterlin = STRESS_SCALE * peterlin_of(halo[0], halo[1], halo[2])
        stress = (peterlin * halo[0] - STRESS_SCALE, peterlin * halo[3], peterlin * halo[4])
        force = [pre_ref[a, 0, at, :] + half_sign * stress[a] for a in range(3)]
        density = pre_ref[3, 0, at, :]
        inverse = 1.0 / density
        velocity = [(pre_ref[4 + a, 0, at, :] + 0.5 * force[a]) * inverse for a in range(3)]
        speed_sq = (
            velocity[0] * velocity[0] + velocity[1] * velocity[1] + velocity[2] * velocity[2]
        )
        push = velocity[0] * force[0] + velocity[1] * force[1] + velocity[2] * force[2]
        rate = density * (1.0 / SOLVENT_TIME)
        common = rate * (1.0 - 1.5 * speed_sq) - (3.0 * factor) * push
        flow = [rate * velocity[a] for a in range(3)]
        drag = [factor * force[a] for a in range(3)]
        post = [None] * 19
        post[0] = keep * popul_ref[0, 0, at, :] + LATTICE_WEIGHTS[0] * common

        def along(vec, parts):
            total = None
            for axis in range(3):
                if vec[axis] == 1:
                    total = parts[axis] if total is None else total + parts[axis]
                elif vec[axis] == -1:
                    total = total - parts[axis]
            return total

        for i in range(1, 19, 2):
            vec = VELOCITIES[i]
            weight = LATTICE_WEIGHTS[i]
            c_u = along(vec, velocity)
            c_flow = along(vec, flow)
            c_drag = along(vec, drag)
            total = c_flow + c_drag
            even = weight * common + (4.5 * weight) * (c_u * (total + c_drag))
            odd = (3.0 * weight) * total
            post[i] = keep * popul_ref[i, 0, at, :] + (even + odd)
            post[i + 1] = keep * popul_ref[i + 1, 0, at, :] + (even - odd)
        for i in range(19):
            post_ref[i, 0, at, :] = post[i]
        for a in range(3):
            message_ref[a, at, :] = velocity[a]
        for slot in range(5):
            message_ref[3 + slot, at, :] = jnp.where(
                outward_plus, post[PLUS[slot]], post[MINUS[slot]]
            )
        up = up_in[at, :] if second else None
        down = down_in[at, :] if second else None
        up_ref[at, :] = pack_columns(
            velocity + [post[i] for i in Z_UP], width - 1, up, base
        )
        down_ref[at, :] = pack_columns(velocity + [post[i] for i in Z_DOWN], 0, down, base)

    for_rows(height, rows)


def collide(plane, popul, pre, halo, earlier=None):
    height, width = popul.shape[2:]
    block = min(32, height)
    second = earlier is not None
    tile = jax.ShapeDtypeStruct((height, width), F32)
    tile_spec = pl.BlockSpec((block, width), lambda g, s: (g, 0))

    def plane_spec(count):
        return pl.BlockSpec((count, 1, block, width), lambda g, s: (0, s[0], g, 0))

    in_specs = [
        plane_spec(19),
        plane_spec(7),
        pl.BlockSpec((6, block, width), lambda g, s: (0, g, 0)),
    ]
    operands = [plane, popul, pre, halo]
    aliases = {}
    if second:
        in_specs += [any_spec(), tile_spec, tile_spec]
        operands += list(earlier)
        aliases = {4: 0}
    return pl.pallas_call(
        functools.partial(collide_kernel, second),
        grid_spec=pltpu.PrefetchScalarGridSpec(
            num_scalar_prefetch=1,
            grid=(height // block,),
            in_specs=in_specs,
            out_specs=(
                plane_spec(19),
                pl.BlockSpec((8, block, width), lambda g, s: (0, g, 0)),
                tile_spec,
                tile_spec,
            ),
        ),
        out_shape=(
            jax.ShapeDtypeStruct(popul.shape, F32),
            jax.ShapeDtypeStruct((8, height, width), F32),
            tile,
            tile,
        ),
        input_output_aliases=aliases,
        compiler_params=params(),
        name="collide_odd" if second else "collide_even",
    )(*operands)


def corner_kernel(low_ref, high_ref, even_ref, odd_ref):
    low = low_ref[...].T
    high = high_ref[...].T
    even_ref[0:8, :] = low[0:8]
    even_ref[8:16, :] = high[0:8]
    odd_ref[0:8, :] = low[8:16]
    odd_ref[8:16, :] = high[8:16]


def corners(low, high):
    height = low.shape[0]
    out = jax.ShapeDtypeStruct((16, height), F32)
    return pl.pallas_call(
        corner_kernel,
        out_shape=(out, out),
        in_specs=[vmem_spec()] * 2,
        out_specs=(vmem_spec(), vmem_spec()),
        compiler_params=params(),
        name="corners",
    )(low, high)


def inner_kernel(
    planes_ref,
    conf_ref,
    halo_e,
    halo_o,
    conf_low,
    conf_high,
    low_ref,
    high_ref,
    post_ref,
    velo_e,
    velo_o,
    read_ref,
    part_ref,
    conf_tall,
    velo_tall,
    halo,
):
    height, width = conf_ref.shape[2:]
    planes = (planes_ref[0], planes_ref[1])
    for face, (velo, half) in enumerate(((velo_e, halo_e), (velo_o, halo_o))):
        p = planes[face]
        for a in range(3):
            velo_tall[a, p, 8 : 8 + height, :] = velo[a]
            velo_tall[a, p, 7:8, :] = -velo[a, 0:1, :]
            velo_tall[a, p, height + 8 : height + 9, :] = -velo[a, height - 1 : height, :]
        for f in range(6):
            halo[p, f] = half[f]
    for p in range(2):
        for f in range(6):
            conf_tall[f, p, 8 : 8 + height, :] = conf_ref[f, p]
            conf_tall[f, p, 7:8, :] = conf_ref[f, p, 0:1, :]
            conf_tall[f, p, height + 8 : height + 9, :] = conf_ref[f, p, height - 1 : height, :]

    even_first = planes[0] == 0

    def lane_of(p, field):
        return (field, 8 + field) if p == 0 else (8 + field, field)

    def edge_value(pack, p, field, target):
        when_first, otherwise = lane_of(p, field)
        return jnp.where(
            even_first, rolled(pack, target - when_first), rolled(pack, target - otherwise)
        )

    for p in range(2):
        sign = 2 * p - 1

        def rows(start, p=p, sign=sign):
            at = pl.ds(start, ROWS)
            upper = pl.ds(start + 9, ROWS)
            lower = pl.ds(start + 7, ROWS)
            cl_pack = conf_low[at, :]
            ch_pack = conf_high[at, :]
            l_pack = low_ref[at, :]
            h_pack = high_ref[at, :]
            lane = lanes_of(cl_pack)
            first = lane == 0
            final = lane == width - 1
            velocity = [velo_tall[a, p, pl.ds(start + 8, ROWS), :] for a in range(3)]
            grad = [[None] * 3 for _ in range(3)]
            for a in range(3):
                grad[0][a] = (-0.5 * sign) * velo_tall[a, 1 - p, pl.ds(start + 8, ROWS), :]
                grad[1][a] = 0.5 * (velo_tall[a, p, upper, :] - velo_tall[a, p, lower, :])
                above = jnp.where(
                    final, edge_value(h_pack, p, a, width - 1), rolled(velocity[a], -1)
                )
                below = jnp.where(first, edge_value(l_pack, p, a, 0), rolled(velocity[a], 1))
                grad[2][a] = 0.5 * (above - below)
            own = [conf_ref[f, p, at, :] for f in range(6)]
            peterlin = (1.0 / RELAX_TIME) * peterlin_of(own[0], own[1], own[2])
            for f in range(6):
                i, j = COMPONENT_PAIRS[f]
                x_in = conf_ref[f, 1 - p, at, :]
                x_out = halo[p, f, at, :]
                y_up = conf_tall[f, p, upper, :]
                y_low = conf_tall[f, p, lower, :]
                lane_number = 6 * p + f
                z_up = jnp.where(
                    final, rolled(ch_pack, width - 1 - lane_number), rolled(own[f], -1)
                )
                z_low = jnp.where(first, rolled(cl_pack, -lane_number), rolled(own[f], 1))
                around = (x_in + x_out) + (y_up + y_low) + (z_up + z_low)
                advect = (
                    (sign * velocity[0]) * (x_out - x_in)
                    + velocity[1] * (y_up - y_low)
                    + velocity[2] * (z_up - z_low)
                )
                stretch = None
                for k in range(3):
                    term = own[SYMMETRIC_INDEX[i][k]] * grad[k][j]
                    if i != j:
                        term = term + grad[k][i] * own[SYMMETRIC_INDEX[k][j]]
                    stretch = term if stretch is None else stretch + term
                if i == j:
                    stretch = 2.0 * stretch
                relax = peterlin * own[f]
                if f < 3:
                    relax = relax - 1.0 / RELAX_TIME
                part_ref[f, p, at, :] = (
                    own[f]
                    - 0.5 * advect
                    + stretch
                    - relax
                    + DIFFUSIVITY * (around - 6.0 * own[f])
                )

        for_rows(height, rows)

    full_low = low_ref[...]
    full_high = high_ref[...]
    lane = lanes_of(full_low)
    for i in range(19):
        step_x, step_y, step_z = VELOCITIES[i]
        for p in range(2):
            q = p - step_x
            if q not in (0, 1):
                continue
            value = post_ref[i, q]
            if step_z == 1:
                edge = edge_value(full_low, q, 3 + Z_UP.index(i), 0)
                value = jnp.where(lane == 0, edge, rolled(value, 1))
            elif step_z == -1:
                edge = edge_value(full_high, q, 3 + Z_DOWN.index(i), width - 1)
                value = jnp.where(lane == width - 1, edge, rolled(value, -1))
            back = OPPOSITE[i]
            if step_y == 1:
                read_ref[i, p, 1:height, :] = value[: height - 1]
                read_ref[i, p, 0:1, :] = post_ref[back, p, 0:1, :]
            elif step_y == -1:
                read_ref[i, p, 0 : height - 1, :] = value[1:]
                read_ref[i, p, height - 1 : height, :] = post_ref[back, p, height - 1 : height, :]
            else:
                read_ref[i, p] = value


def inner(planes, conform, halo_e, halo_o, conf_low, conf_high, low, high, post, velo_e, velo_o):
    height, width = conform.shape[2:]
    velo_spec = pl.BlockSpec((3, height, width), lambda g: (0, 0, 0))
    whole = lambda shape: pl.BlockSpec(shape, lambda g: (0,) * len(shape))
    return pl.pallas_call(
        inner_kernel,
        grid=(1,),
        out_shape=(
            jax.ShapeDtypeStruct(post.shape, F32),
            jax.ShapeDtypeStruct(conform.shape, F32),
        ),
        in_specs=[
            pl.BlockSpec(memory_space=pltpu.SMEM),
            whole(conform.shape),
            whole(halo_e.shape),
            whole(halo_o.shape),
            whole(conf_low.shape),
            whole(conf_low.shape),
            whole(conf_low.shape),
            whole(conf_low.shape),
            whole(post.shape),
            velo_spec,
            velo_spec,
        ],
        out_specs=(whole(post.shape), whole(conform.shape)),
        scratch_shapes=[
            VMEM((6, 2, height + 16, width), F32),
            VMEM((3, 2, height + 16, width), F32),
            VMEM((2, 6, height, width), F32),
        ],
        compiler_params=params(),
        name="inner",
    )(planes, conform, halo_e, halo_o, conf_low, conf_high, low, high, post, velo_e, velo_o)


def finish_kernel(
    second,
    plane_ref,
    part_ref,
    conf_ref,
    got_ref,
    bottom_ref,
    top_ref,
    corner_ref,
    *refs,
):
    if second:
        _, _, read_ref, new_ref, read_tile, new_tile, sems = refs
    else:
        _, read_ref, new_ref, read_tile, new_tile, sems = refs
    height, width = got_ref.shape[1:]
    plane = plane_ref[0]
    half_sign = jnp.where(plane == 1, 0.5, -0.5).astype(F32)
    copies = []

    def send(slot):
        target = jnp.where(plane == 1, MINUS[slot], PLUS[slot])
        copy = pltpu.make_async_copy(
            read_tile.at[slot], read_ref.at[target, plane], sems.at[slot]
        )
        copy.start()
        copies.append(copy)

    lane = lax.broadcasted_iota(jnp.int32, (height, width), 1)
    low = jnp.broadcast_to(corner_ref[pl.ds(6 + plane, 1), :], (width, height)).T
    high = jnp.broadcast_to(corner_ref[pl.ds(14 + plane, 1), :], (width, height)).T
    read_tile[0] = got_ref[3]
    send(0)
    read_tile[1, 1:height, :] = got_ref[4, 0 : height - 1, :]
    read_tile[1, 0:1, :] = bottom_ref[0, 0:1, :]
    send(1)
    read_tile[2, 0 : height - 1, :] = got_ref[5, 1:height, :]
    read_tile[2, height - 1 : height, :] = top_ref[0, 7:8, :]
    send(2)
    read_tile[3] = jnp.where(lane == 0, low, rolled(got_ref[6], 1))
    send(3)
    read_tile[4] = jnp.where(lane == width - 1, high, rolled(got_ref[7], -1))
    send(4)

    def rows(start):
        at = pl.ds(start, ROWS)
        slope = [half_sign * got_ref[a, at, :] for a in range(3)]
        row = [conf_ref[f, 0, at, :] for f in (0, 3, 4)]
        for f in range(6):
            i, j = COMPONENT_PAIRS[f]
            if i == j:
                term = 2.0 * (row[i] * slope[j])
            else:
                term = row[i] * slope[j] + slope[i] * row[j]
            new_tile[f, at, :] = part_ref[f, 0, at, :] + term

    for_rows(height, rows)
    for f in range(6):
        copy = pltpu.make_async_copy(new_tile.at[f], new_ref.at[f, plane], sems.at[5 + f])
        copy.start()
        copies.append(copy)
    for copy in copies:
        copy.wait()


def finish(plane, part, conform, got, sent, corner, read, new=None):
    height, width = conform.shape[2:]
    second = new is not None
    plane_spec = pl.BlockSpec((6, 1, height, width), lambda g, s: (0, s[0], 0, 0))
    in_specs = [
        plane_spec,
        plane_spec,
        pl.BlockSpec((8, height, width), lambda g, s: (0, 0, 0)),
        pl.BlockSpec((1, 8, width), lambda g, s: (5, 0, 0)),
        pl.BlockSpec((1, 8, width), lambda g, s: (4, height // 8 - 1, 0)),
        pl.BlockSpec((16, height), lambda g, s: (0, 0)),
        any_spec(),
    ]
    operands = [plane, part, conform, got, sent, sent, corner, read]
    aliases = {7: 0}
    if second:
        in_specs.append(any_spec())
        operands.append(new)
        aliases[8] = 1
    return pl.pallas_call(
        functools.partial(finish_kernel, second),
        grid_spec=pltpu.PrefetchScalarGridSpec(
            num_scalar_prefetch=1,
            grid=(1,),
            in_specs=in_specs,
            out_specs=(any_spec(), any_spec()),
            scratch_shapes=[
                VMEM((5, height, width), F32),
                VMEM((6, height, width), F32),
                pltpu.SemaphoreType.DMA((11,)),
            ],
        ),
        out_shape=(
            jax.ShapeDtypeStruct(read.shape, F32),
            jax.ShapeDtypeStruct(conform.shape, F32),
        ),
        input_output_aliases=aliases,
        compiler_params=params(),
        name="finish_odd" if second else "finish_even",
    )(*operands)


def body(popul, conform):
    wide = lax.axis_size("wide")
    narrow = lax.axis_size("narrow")
    odd = lax.rem(lax.axis_index("wide"), 2)
    plane_e = (1 - odd).astype(jnp.int32).reshape(1)
    plane_o = odd.astype(jnp.int32).reshape(1)
    even_pairs = [(i, i ^ 1) for i in range(wide)]
    odd_pairs = [(i, (i + 1) % wide if i % 2 else (i - 1) % wide) for i in range(wide)]
    up = [(i, (i + 1) % narrow) for i in range(narrow)]
    down = [(j, i) for i, j in up]

    near = lax.dynamic_index_in_dim(conform, plane_e[0], axis=1, keepdims=False)
    halo_e = lax.ppermute(near, "wide", even_pairs)
    conf_up, conf_down, far = edges(plane_o, conform)
    halo_o = lax.ppermute(far, "wide", odd_pairs)
    conf_low = lax.ppermute(conf_up, "narrow", up)
    conf_high = lax.ppermute(conf_down, "narrow", down)
    pre = prepare(conform, popul, conf_low, conf_high)
    post, sent_e, z_up, z_down = collide(plane_e, popul, pre, halo_e)
    got_e = lax.ppermute(sent_e, "wide", even_pairs)
    post, sent_o, z_up, z_down = collide(plane_o, popul, pre, halo_o, (post, z_up, z_down))
    got_o = lax.ppermute(sent_o, "wide", odd_pairs)
    low = lax.ppermute(z_up, "narrow", up)
    high = lax.ppermute(z_down, "narrow", down)
    corner_e, corner_o = corners(low, high)
    corner_e = lax.ppermute(corner_e, "wide", even_pairs)
    corner_o = lax.ppermute(corner_o, "wide", odd_pairs)
    read, part = inner(
        jnp.concatenate([plane_e, plane_o]),
        conform,
        halo_e,
        halo_o,
        conf_low,
        conf_high,
        low,
        high,
        post,
        sent_e,
        sent_o,
    )
    read, new = finish(plane_e, part, conform, got_e, sent_e, corner_e, read)
    return finish(plane_o, part, conform, got_o, sent_o, corner_o, read, new)


def solution(mesh):
    placed = P(None, "wide", None, "narrow")
    return jax.shard_map(
        body, mesh=mesh, in_specs=(placed, placed), out_specs=(placed, placed), check_vma=False
    )
```

```python
import functools

import jax
import jax.numpy as jnp
from jax import lax
from jax.experimental import pallas as pl
from jax.experimental.pallas import tpu as pltpu
from jax.sharding import PartitionSpec as P

VELOCITIES = (
    (0, 0, 0),
    (1, 0, 0),
    (-1, 0, 0),
    (0, 1, 0),
    (0, -1, 0),
    (0, 0, 1),
    (0, 0, -1),
    (1, 1, 0),
    (-1, -1, 0),
    (1, -1, 0),
    (-1, 1, 0),
    (1, 0, 1),
    (-1, 0, -1),
    (1, 0, -1),
    (-1, 0, 1),
    (0, 1, 1),
    (0, -1, -1),
    (0, 1, -1),
    (0, -1, 1),
)
LATTICE_WEIGHTS = (1.0 / 3.0,) + (1.0 / 18.0,) * 6 + (1.0 / 36.0,) * 12
OPPOSITE = (0, 2, 1, 4, 3, 6, 5, 8, 7, 10, 9, 12, 11, 14, 13, 16, 15, 18, 17)
SYMMETRIC_INDEX = ((0, 3, 4), (3, 1, 5), (4, 5, 2))
COMPONENT_PAIRS = ((0, 0), (1, 1), (2, 2), (0, 1), (0, 2), (1, 2))
SOLVENT_TIME = 0.8
RELAX_TIME = 20.0
POLYMER_VISC = 1.0
EXTENSION_SQ = 100.0
DIFFUSIVITY = 0.05
DRIVE_FORCE = 1e-05
STRESS_SCALE = POLYMER_VISC / RELAX_TIME

SLOT_SHIFTS = ((0, 0), (1, 0), (-1, 0), (0, 1), (0, -1))
PLUS = tuple(VELOCITIES.index((1, cy, cz)) for cy, cz in SLOT_SHIFTS)
MINUS = tuple(VELOCITIES.index((-1, cy, cz)) for cy, cz in SLOT_SHIFTS)
Z_UP = tuple(VELOCITIES.index(v) for v in ((0, 0, 1), (0, 1, 1), (0, -1, 1), (1, 0, 1), (-1, 0, 1)))
Z_DOWN = tuple(
    VELOCITIES.index(v) for v in ((0, 0, -1), (0, 1, -1), (0, -1, -1), (1, 0, -1), (-1, 0, -1))
)
ROWS = 32
F32 = jnp.float32
VMEM = pltpu.VMEM


def vmem_spec():
    return pl.BlockSpec(memory_space=pltpu.VMEM)


def any_spec():
    return pl.BlockSpec(memory_space=pl.ANY)


def params():
    return pltpu.CompilerParams(vmem_limit_bytes=12 << 20)


def lanes_of(like):
    return lax.broadcasted_iota(jnp.int32, like.shape, 1)


def rolled(value, shift, axis=1):
    shift = shift % value.shape[axis]
    return value if shift == 0 else pltpu.roll(value, shift, axis)


def pack_columns(values, source, packed=None, base=0):
    lane = lanes_of(values[0])
    if packed is None:
        packed = jnp.zeros_like(values[0])
    for number, value in enumerate(values, base):
        packed = jnp.where(lane == number, rolled(value, number - source), packed)
    return packed


def for_rows(total, body):
    def step(number, carry):
        body(pl.multiple_of(number * ROWS, ROWS))
        return carry

    lax.fori_loop(0, total // ROWS, step, 0)


def peterlin_of(c_xx, c_yy, c_zz):
    return (EXTENSION_SQ - 3.0) / (EXTENSION_SQ - (c_xx + c_yy + c_zz))


def load_kernel(near_plane, conf_hbm, conf_ref, near_ref, sems):
    near = near_plane[0]
    copies = [
        pltpu.make_async_copy(conf_hbm.at[:, near], near_ref, sems.at[0]),
        pltpu.make_async_copy(conf_hbm, conf_ref, sems.at[1]),
    ]
    for copy in copies:
        copy.start()
    for copy in copies:
        copy.wait()


def load(near_plane, conform):
    shape = conform.shape
    return pl.pallas_call(
        load_kernel,
        out_shape=(
            jax.ShapeDtypeStruct(shape, F32),
            jax.ShapeDtypeStruct((shape[0],) + shape[2:], F32),
        ),
        in_specs=[pl.BlockSpec(memory_space=pltpu.SMEM), any_spec()],
        out_specs=(vmem_spec(), vmem_spec()),
        scratch_shapes=[pltpu.SemaphoreType.DMA((2,))],
        compiler_params=params(),
        name="load",
    )(near_plane, conform)


def edge_kernel(conf_ref, up_ref, down_ref):
    height, width = conf_ref.shape[2:]

    def rows(start):
        at = pl.ds(start, ROWS)
        values = [conf_ref[f, p, at, :] for p in range(2) for f in range(6)]
        up_ref[at, :] = pack_columns(values, width - 1)
        down_ref[at, :] = pack_columns(values, 0)

    for_rows(height, rows)


def edges(conform):
    height, width = conform.shape[2:]
    tile = jax.ShapeDtypeStruct((height, width), F32)
    return pl.pallas_call(
        edge_kernel,
        out_shape=(tile, tile),
        in_specs=[vmem_spec()],
        out_specs=(vmem_spec(), vmem_spec()),
        compiler_params=params(),
        name="edges",
    )(conform)


def moments_kernel(far_plane, popul_hbm, conf_ref, _, popul_ref, sums_ref, far_ref, sems):
    height = conf_ref.shape[2]
    copies = []
    for p in range(2):
        copies.append(pltpu.make_async_copy(popul_hbm.at[:, p], popul_ref.at[:, p], sems.at[p]))
        copies[-1].start()
    far = far_plane[0]
    for f in range(6):
        far_ref[f] = conf_ref[f, far]
    for p in range(2):
        copies[p].wait()

        def rows(start, p=p):
            at = pl.ds(start, ROWS)
            values = [popul_ref[i, p, at, :] for i in range(19)]
            density = values[0]
            for i in range(1, 19):
                density = density + values[i]
            sums_ref[0, p, at, :] = density
            for axis in range(3):
                moment = None
                for i in range(19):
                    if VELOCITIES[i][axis] == 1:
                        moment = values[i] if moment is None else moment + values[i]
                for i in range(19):
                    if VELOCITIES[i][axis] == -1:
                        moment = moment - values[i]
                sums_ref[1 + axis, p, at, :] = moment

        for_rows(height, rows)


def moments(far_plane, popul, conform, after):
    shape = conform.shape
    return pl.pallas_call(
        moments_kernel,
        out_shape=(
            jax.ShapeDtypeStruct(popul.shape, F32),
            jax.ShapeDtypeStruct((4,) + shape[1:], F32),
            jax.ShapeDtypeStruct((shape[0],) + shape[2:], F32),
        ),
        in_specs=[pl.BlockSpec(memory_space=pltpu.SMEM), any_spec(), vmem_spec(), any_spec()],
        out_specs=(vmem_spec(),) * 3,
        scratch_shapes=[pltpu.SemaphoreType.DMA((2,))],
        compiler_params=params(),
        name="moments",
    )(far_plane, popul, conform, after)


def prepare_kernel(conf_ref, low_ref, high_ref, pre_ref, tall):
    height, width = conf_ref.shape[2:]

    def stress(fields, at_of):
        trace_parts = [at_of(f) for f in range(3)]
        peterlin = STRESS_SCALE * peterlin_of(*trace_parts)
        out = {}
        for f in fields:
            value = trace_parts[f] if f < 3 else at_of(f)
            out[f] = peterlin * value - (STRESS_SCALE if f < 3 else 0.0)
        return out

    for p in range(2):
        sign = 2 * p - 1

        def first(start, p=p, sign=sign):
            at = pl.ds(start, ROWS)
            own = stress(range(6), lambda f: conf_ref[f, p, at, :])
            other = stress((0, 3, 4), lambda f: conf_ref[f, 1 - p, at, :])
            low_pack = low_ref[at, :]
            high_pack = high_ref[at, :]
            low = stress((2, 4, 5), lambda f: rolled(low_pack, -(6 * p + f)))
            high = stress((2, 4, 5), lambda f: rolled(high_pack, width - 1 - (6 * p + f)))
            lane = lanes_of(low_pack)
            for number, f in enumerate((3, 1, 5)):
                tall[number, p, pl.ds(start + 8, ROWS), :] = own[f]
            for number in range(3):
                across = SYMMETRIC_INDEX[number][2]
                below = jnp.where(lane == 0, low[across], rolled(own[across], 1))
                above = jnp.where(lane == width - 1, high[across], rolled(own[across], -1))
                term = 0.5 * (above - below) - (0.5 * sign) * other[SYMMETRIC_INDEX[number][0]]
                if number == 0:
                    term = term + DRIVE_FORCE
                pre_ref[number, p, at, :] = term

        for_rows(height, first)
        for number in range(3):
            tall[number, p, 7:8, :] = tall[number, p, 8:9, :]
            tall[number, p, height + 8 : height + 9, :] = tall[number, p, height + 7 : height + 8, :]

        def second(start, p=p):
            at = pl.ds(start, ROWS)
            for number in range(3):
                above = tall[number, p, pl.ds(start + 9, ROWS), :]
                below = tall[number, p, pl.ds(start + 7, ROWS), :]
                pre_ref[number, p, at, :] = pre_ref[number, p, at, :] + 0.5 * (above - below)

        for_rows(height, second)


def prepare(conform, low, high):
    height, width = conform.shape[2:]
    return pl.pallas_call(
        prepare_kernel,
        out_shape=jax.ShapeDtypeStruct((3, 2, height, width), F32),
        in_specs=[vmem_spec()] * 3,
        out_specs=vmem_spec(),
        scratch_shapes=[VMEM((3, 2, height + 16, width), F32)],
        compiler_params=params(),
        name="prepare",
    )(conform, low, high)


def collide_kernel(second, plane_ref, popul_ref, sums_ref, pre_ref, halo_ref, *refs):
    if second:
        _, up_in, down_in, post_ref, message_ref, up_ref, down_ref = refs
    else:
        post_ref, message_ref, up_ref, down_ref = refs
    height, width = halo_ref.shape[1:]
    plane = plane_ref[0]
    outward_plus = plane == 1
    half_sign = jnp.where(outward_plus, 0.5, -0.5).astype(F32)
    factor = 1.0 - 0.5 / SOLVENT_TIME
    keep = 1.0 - 1.0 / SOLVENT_TIME
    base = 8 if second else 0

    def rows(start):
        at = pl.ds(start, ROWS)
        halo = [halo_ref[f, at, :] for f in range(5)]
        peterlin = STRESS_SCALE * peterlin_of(halo[0], halo[1], halo[2])
        stress = (peterlin * halo[0] - STRESS_SCALE, peterlin * halo[3], peterlin * halo[4])
        force = [pre_ref[a, plane, at, :] + half_sign * stress[a] for a in range(3)]
        density = sums_ref[0, plane, at, :]
        inverse = 1.0 / density
        velocity = [(sums_ref[1 + a, plane, at, :] + 0.5 * force[a]) * inverse for a in range(3)]
        speed_sq = (
            velocity[0] * velocity[0] + velocity[1] * velocity[1] + velocity[2] * velocity[2]
        )
        push = velocity[0] * force[0] + velocity[1] * force[1] + velocity[2] * force[2]
        rate = density * (1.0 / SOLVENT_TIME)
        common = rate * (1.0 - 1.5 * speed_sq) - (3.0 * factor) * push
        flow = [rate * velocity[a] for a in range(3)]
        drag = [factor * force[a] for a in range(3)]
        post = [None] * 19
        post[0] = keep * popul_ref[0, plane, at, :] + LATTICE_WEIGHTS[0] * common

        def along(vec, parts):
            total = None
            for axis in range(3):
                if vec[axis] == 1:
                    total = parts[axis] if total is None else total + parts[axis]
                elif vec[axis] == -1:
                    total = total - parts[axis]
            return total

        for i in range(1, 19, 2):
            vec = VELOCITIES[i]
            weight = LATTICE_WEIGHTS[i]
            c_u = along(vec, velocity)
            c_flow = along(vec, flow)
            c_drag = along(vec, drag)
            total = c_flow + c_drag
            even = weight * common + (4.5 * weight) * (c_u * (total + c_drag))
            odd = (3.0 * weight) * total
            post[i] = keep * popul_ref[i, plane, at, :] + (even + odd)
            post[i + 1] = keep * popul_ref[i + 1, plane, at, :] + (even - odd)
        for i in range(19):
            post_ref[i, plane, at, :] = post[i]
        for a in range(3):
            message_ref[a, at, :] = velocity[a]
        for slot in range(5):
            message_ref[3 + slot, at, :] = jnp.where(
                outward_plus, post[PLUS[slot]], post[MINUS[slot]]
            )
        up = up_in[at, :] if second else None
        down = down_in[at, :] if second else None
        up_ref[at, :] = pack_columns(
            velocity + [post[i] for i in Z_UP], width - 1, up, base
        )
        down_ref[at, :] = pack_columns(velocity + [post[i] for i in Z_DOWN], 0, down, base)

    for_rows(height, rows)


def collide(plane, popul, sums, pre, halo, earlier=None):
    height, width = popul.shape[2:]
    second = earlier is not None
    tile = jax.ShapeDtypeStruct((height, width), F32)
    operands = [plane, popul, sums, pre, halo] + (list(earlier) if second else [])
    return pl.pallas_call(
        functools.partial(collide_kernel, second),
        in_specs=[pl.BlockSpec(memory_space=pltpu.SMEM)] + [vmem_spec()] * (len(operands) - 1),
        out_specs=(vmem_spec(),) * 4,
        out_shape=(
            jax.ShapeDtypeStruct(popul.shape, F32),
            jax.ShapeDtypeStruct((8, height, width), F32),
            tile,
            tile,
        ),
        input_output_aliases={5: 0} if second else {},
        compiler_params=params(),
        name="collide_odd" if second else "collide_even",
    )(*operands)


def corner_kernel(low_ref, high_ref, even_ref, odd_ref):
    low = low_ref[...].T
    high = high_ref[...].T
    even_ref[0:8, :] = low[0:8]
    even_ref[8:16, :] = high[0:8]
    odd_ref[0:8, :] = low[8:16]
    odd_ref[8:16, :] = high[8:16]


def corners(low, high):
    height = low.shape[0]
    out = jax.ShapeDtypeStruct((16, height), F32)
    return pl.pallas_call(
        corner_kernel,
        out_shape=(out, out),
        in_specs=[vmem_spec()] * 2,
        out_specs=(vmem_spec(), vmem_spec()),
        compiler_params=params(),
        name="corners",
    )(low, high)


def inner_kernel(
    planes_ref,
    conf_ref,
    halo_e,
    halo_o,
    conf_low,
    conf_high,
    low_ref,
    high_ref,
    post_ref,
    velo_e,
    velo_o,
    read_ref,
    part_ref,
    conf_tall,
    velo_tall,
    halo,
    shifted,
    sems,
):
    height, width = conf_ref.shape[2:]
    planes = (planes_ref[0], planes_ref[1])
    for face, (velo, half) in enumerate(((velo_e, halo_e), (velo_o, halo_o))):
        p = planes[face]
        for a in range(3):
            velo_tall[a, p, 8 : 8 + height, :] = velo[a]
            velo_tall[a, p, 7:8, :] = -velo[a, 0:1, :]
            velo_tall[a, p, height + 8 : height + 9, :] = -velo[a, height - 1 : height, :]
        for f in range(6):
            halo[p, f] = half[f]
    for p in range(2):
        for f in range(6):
            conf_tall[f, p, 8 : 8 + height, :] = conf_ref[f, p]
            conf_tall[f, p, 7:8, :] = conf_ref[f, p, 0:1, :]
            conf_tall[f, p, height + 8 : height + 9, :] = conf_ref[f, p, height - 1 : height, :]

    even_first = planes[0] == 0

    def lane_of(p, field):
        return (field, 8 + field) if p == 0 else (8 + field, field)

    def edge_value(pack, p, field, target):
        when_first, otherwise = lane_of(p, field)
        return jnp.where(
            even_first, rolled(pack, target - when_first), rolled(pack, target - otherwise)
        )

    copies = []
    full_low = low_ref[...]
    full_high = high_ref[...]
    lane = lanes_of(full_low)
    for i in range(19):
        step_x, step_y, step_z = VELOCITIES[i]
        for p in range(2):
            q = p - step_x
            if q not in (0, 1):
                continue
            tile = post_ref.at[i, q]
            if step_y or step_z:
                value = post_ref[i, q]
                if step_z == 1:
                    edge = edge_value(full_low, q, 3 + Z_UP.index(i), 0)
                    value = jnp.where(lane == 0, edge, rolled(value, 1))
                elif step_z == -1:
                    edge = edge_value(full_high, q, 3 + Z_DOWN.index(i), width - 1)
                    value = jnp.where(lane == width - 1, edge, rolled(value, -1))
                back = OPPOSITE[i]
                tile = shifted.at[i, p]
                if step_y == 1:
                    tile[1:height, :] = value[: height - 1]
                    tile[0:1, :] = post_ref[back, p, 0:1, :]
                elif step_y == -1:
                    tile[0 : height - 1, :] = value[1:]
                    tile[height - 1 : height, :] = post_ref[back, p, height - 1 : height, :]
                else:
                    tile[...] = value
            copies.append(pltpu.make_async_copy(tile, read_ref.at[i, p], sems.at[len(copies)]))
            copies[-1].start()

    for p in range(2):
        sign = 2 * p - 1

        def rows(start, p=p, sign=sign):
            at = pl.ds(start, ROWS)
            upper = pl.ds(start + 9, ROWS)
            lower = pl.ds(start + 7, ROWS)
            cl_pack = conf_low[at, :]
            ch_pack = conf_high[at, :]
            l_pack = low_ref[at, :]
            h_pack = high_ref[at, :]
            lane = lanes_of(cl_pack)
            first = lane == 0
            final = lane == width - 1
            velocity = [velo_tall[a, p, pl.ds(start + 8, ROWS), :] for a in range(3)]
            grad = [[None] * 3 for _ in range(3)]
            for a in range(3):
                grad[0][a] = (-0.5 * sign) * velo_tall[a, 1 - p, pl.ds(start + 8, ROWS), :]
                grad[1][a] = 0.5 * (velo_tall[a, p, upper, :] - velo_tall[a, p, lower, :])
                above = jnp.where(
                    final, edge_value(h_pack, p, a, width - 1), rolled(velocity[a], -1)
                )
                below = jnp.where(first, edge_value(l_pack, p, a, 0), rolled(velocity[a], 1))
                grad[2][a] = 0.5 * (above - below)
            own = [conf_ref[f, p, at, :] for f in range(6)]
            peterlin = (1.0 / RELAX_TIME) * peterlin_of(own[0], own[1], own[2])
            for f in range(6):
                i, j = COMPONENT_PAIRS[f]
                x_in = conf_ref[f, 1 - p, at, :]
                x_out = halo[p, f, at, :]
                y_up = conf_tall[f, p, upper, :]
                y_low = conf_tall[f, p, lower, :]
                lane_number = 6 * p + f
                z_up = jnp.where(
                    final, rolled(ch_pack, width - 1 - lane_number), rolled(own[f], -1)
                )
                z_low = jnp.where(first, rolled(cl_pack, -lane_number), rolled(own[f], 1))
                around = (x_in + x_out) + (y_up + y_low) + (z_up + z_low)
                advect = (
                    (sign * velocity[0]) * (x_out - x_in)
                    + velocity[1] * (y_up - y_low)
                    + velocity[2] * (z_up - z_low)
                )
                stretch = None
                for k in range(3):
                    term = own[SYMMETRIC_INDEX[i][k]] * grad[k][j]
                    if i != j:
                        term = term + grad[k][i] * own[SYMMETRIC_INDEX[k][j]]
                    stretch = term if stretch is None else stretch + term
                if i == j:
                    stretch = 2.0 * stretch
                relax = peterlin * own[f]
                if f < 3:
                    relax = relax - 1.0 / RELAX_TIME
                part_ref[f, p, at, :] = (
                    own[f]
                    - 0.5 * advect
                    + stretch
                    - relax
                    + DIFFUSIVITY * (around - 6.0 * own[f])
                )

        for_rows(height, rows)
    for copy in copies:
        copy.wait()


def inner(planes, conform, halo_e, halo_o, conf_low, conf_high, low, high, post, velo_e, velo_o):
    height, width = conform.shape[2:]
    velo_spec = pl.BlockSpec((3, height, width), lambda g: (0, 0, 0))
    whole = lambda shape: pl.BlockSpec(shape, lambda g: (0,) * len(shape))
    return pl.pallas_call(
        inner_kernel,
        grid=(1,),
        out_shape=(
            jax.ShapeDtypeStruct(post.shape, F32),
            jax.ShapeDtypeStruct(conform.shape, F32),
        ),
        in_specs=[
            pl.BlockSpec(memory_space=pltpu.SMEM),
            whole(conform.shape),
            whole(halo_e.shape),
            whole(halo_o.shape),
            whole(conf_low.shape),
            whole(conf_low.shape),
            whole(conf_low.shape),
            whole(conf_low.shape),
            whole(post.shape),
            velo_spec,
            velo_spec,
        ],
        out_specs=(any_spec(), whole(conform.shape)),
        scratch_shapes=[
            VMEM((6, 2, height + 16, width), F32),
            VMEM((3, 2, height + 16, width), F32),
            VMEM((2, 6, height, width), F32),
            VMEM(post.shape, F32),
            pltpu.SemaphoreType.DMA((28,)),
        ],
        compiler_params=params(),
        name="inner",
    )(planes, conform, halo_e, halo_o, conf_low, conf_high, low, high, post, velo_e, velo_o)


def finish_kernel(
    second,
    plane_ref,
    part_ref,
    conf_ref,
    got_ref,
    bottom_ref,
    top_ref,
    corner_ref,
    *refs,
):
    if second:
        _, _, read_ref, new_ref, read_tile, new_tile, sems = refs
    else:
        _, read_ref, new_ref, read_tile, new_tile, sems = refs
    height, width = got_ref.shape[1:]
    plane = plane_ref[0]
    half_sign = jnp.where(plane == 1, 0.5, -0.5).astype(F32)
    copies = []

    def send(slot):
        target = jnp.where(plane == 1, MINUS[slot], PLUS[slot])
        copy = pltpu.make_async_copy(
            read_tile.at[slot], read_ref.at[target, plane], sems.at[slot]
        )
        copy.start()
        copies.append(copy)

    lane = lax.broadcasted_iota(jnp.int32, (height, width), 1)
    low = jnp.broadcast_to(corner_ref[pl.ds(6 + plane, 1), :], (width, height)).T
    high = jnp.broadcast_to(corner_ref[pl.ds(14 + plane, 1), :], (width, height)).T
    read_tile[0] = got_ref[3]
    send(0)
    read_tile[1, 1:height, :] = got_ref[4, 0 : height - 1, :]
    read_tile[1, 0:1, :] = bottom_ref[0, 0:1, :]
    send(1)
    read_tile[2, 0 : height - 1, :] = got_ref[5, 1:height, :]
    read_tile[2, height - 1 : height, :] = top_ref[0, 7:8, :]
    send(2)
    read_tile[3] = jnp.where(lane == 0, low, rolled(got_ref[6], 1))
    send(3)
    read_tile[4] = jnp.where(lane == width - 1, high, rolled(got_ref[7], -1))
    send(4)

    def rows(start):
        at = pl.ds(start, ROWS)
        slope = [half_sign * got_ref[a, at, :] for a in range(3)]
        row = [conf_ref[f, 0, at, :] for f in (0, 3, 4)]
        for f in range(6):
            i, j = COMPONENT_PAIRS[f]
            if i == j:
                term = 2.0 * (row[i] * slope[j])
            else:
                term = row[i] * slope[j] + slope[i] * row[j]
            new_tile[f, at, :] = part_ref[f, 0, at, :] + term

    for_rows(height, rows)
    for f in range(6):
        copy = pltpu.make_async_copy(new_tile.at[f], new_ref.at[f, plane], sems.at[5 + f])
        copy.start()
        copies.append(copy)
    for copy in copies:
        copy.wait()


def finish(plane, part, conform, got, sent, corner, read, new=None):
    height, width = conform.shape[2:]
    second = new is not None
    plane_spec = pl.BlockSpec((6, 1, height, width), lambda g, s: (0, s[0], 0, 0))
    in_specs = [
        plane_spec,
        plane_spec,
        pl.BlockSpec((8, height, width), lambda g, s: (0, 0, 0)),
        pl.BlockSpec((1, 8, width), lambda g, s: (5, 0, 0)),
        pl.BlockSpec((1, 8, width), lambda g, s: (4, height // 8 - 1, 0)),
        pl.BlockSpec((16, height), lambda g, s: (0, 0)),
        any_spec(),
    ]
    operands = [plane, part, conform, got, sent, sent, corner, read]
    aliases = {7: 0}
    if second:
        in_specs.append(any_spec())
        operands.append(new)
        aliases[8] = 1
    return pl.pallas_call(
        functools.partial(finish_kernel, second),
        grid_spec=pltpu.PrefetchScalarGridSpec(
            num_scalar_prefetch=1,
            grid=(1,),
            in_specs=in_specs,
            out_specs=(any_spec(), any_spec()),
            scratch_shapes=[
                VMEM((5, height, width), F32),
                VMEM((6, height, width), F32),
                pltpu.SemaphoreType.DMA((11,)),
            ],
        ),
        out_shape=(
            jax.ShapeDtypeStruct(read.shape, F32),
            jax.ShapeDtypeStruct(conform.shape, F32),
        ),
        input_output_aliases=aliases,
        compiler_params=params(),
        name="finish_odd" if second else "finish_even",
    )(*operands)


def body(popul, conform):
    wide = lax.axis_size("wide")
    narrow = lax.axis_size("narrow")
    odd = lax.rem(lax.axis_index("wide"), 2)
    plane_e = (1 - odd).astype(jnp.int32).reshape(1)
    plane_o = odd.astype(jnp.int32).reshape(1)
    even_pairs = [(i, i ^ 1) for i in range(wide)]
    odd_pairs = [(i, (i + 1) % wide if i % 2 else (i - 1) % wide) for i in range(wide)]
    up = [(i, (i + 1) % narrow) for i in range(narrow)]
    down = [(j, i) for i, j in up]

    conform, near = load(plane_e, conform)
    halo_e = lax.ppermute(near, "wide", even_pairs)
    conf_up, conf_down = edges(conform)
    conf_low = lax.ppermute(conf_up, "narrow", up)
    conf_high = lax.ppermute(conf_down, "narrow", down)
    popul, sums, far = moments(plane_o, popul, conform, conf_up)
    halo_o = lax.ppermute(far, "wide", odd_pairs)
    pre = prepare(conform, conf_low, conf_high)
    post, sent_e, z_up, z_down = collide(plane_e, popul, sums, pre, halo_e)
    got_e = lax.ppermute(sent_e, "wide", even_pairs)
    post, sent_o, z_up, z_down = collide(
        plane_o, popul, sums, pre, halo_o, (post, z_up, z_down)
    )
    got_o = lax.ppermute(sent_o, "wide", odd_pairs)
    low = lax.ppermute(z_up, "narrow", up)
    high = lax.ppermute(z_down, "narrow", down)
    corner_e, corner_o = corners(low, high)
    corner_e = lax.ppermute(corner_e, "wide", even_pairs)
    corner_o = lax.ppermute(corner_o, "wide", odd_pairs)
    read, part = inner(
        jnp.concatenate([plane_e, plane_o]),
        conform,
        halo_e,
        halo_o,
        conf_low,
        conf_high,
        low,
        high,
        post,
        sent_e,
        sent_o,
    )
    read, new = finish(plane_e, part, conform, got_e, sent_e, corner_e, read)
    return finish(plane_o, part, conform, got_o, sent_o, corner_o, read, new)


def solution(mesh):
    placed = P(None, "wide", None, "narrow")
    return jax.shard_map(
        body, mesh=mesh, in_specs=(placed, placed), out_specs=(placed, placed), check_vma=False
    )
```

```python
import functools

import jax
import jax.numpy as jnp
from jax import lax
from jax.experimental import pallas as pl
from jax.experimental.pallas import tpu as pltpu
from jax.sharding import PartitionSpec as P

VELOCITIES = (
    (0, 0, 0),
    (1, 0, 0),
    (-1, 0, 0),
    (0, 1, 0),
    (0, -1, 0),
    (0, 0, 1),
    (0, 0, -1),
    (1, 1, 0),
    (-1, -1, 0),
    (1, -1, 0),
    (-1, 1, 0),
    (1, 0, 1),
    (-1, 0, -1),
    (1, 0, -1),
    (-1, 0, 1),
    (0, 1, 1),
    (0, -1, -1),
    (0, 1, -1),
    (0, -1, 1),
)
LATTICE_WEIGHTS = (1.0 / 3.0,) + (1.0 / 18.0,) * 6 + (1.0 / 36.0,) * 12
OPPOSITE = (0, 2, 1, 4, 3, 6, 5, 8, 7, 10, 9, 12, 11, 14, 13, 16, 15, 18, 17)
SYMMETRIC_INDEX = ((0, 3, 4), (3, 1, 5), (4, 5, 2))
COMPONENT_PAIRS = ((0, 0), (1, 1), (2, 2), (0, 1), (0, 2), (1, 2))
SOLVENT_TIME = 0.8
RELAX_TIME = 20.0
POLYMER_VISC = 1.0
EXTENSION_SQ = 100.0
DIFFUSIVITY = 0.05
DRIVE_FORCE = 1e-05
STRESS_SCALE = POLYMER_VISC / RELAX_TIME

SLOT_SHIFTS = ((0, 0), (1, 0), (-1, 0), (0, 1), (0, -1))
PLUS = tuple(VELOCITIES.index((1, cy, cz)) for cy, cz in SLOT_SHIFTS)
MINUS = tuple(VELOCITIES.index((-1, cy, cz)) for cy, cz in SLOT_SHIFTS)
Z_UP = tuple(VELOCITIES.index(v) for v in ((0, 0, 1), (0, 1, 1), (0, -1, 1), (1, 0, 1), (-1, 0, 1)))
Z_DOWN = tuple(
    VELOCITIES.index(v) for v in ((0, 0, -1), (0, 1, -1), (0, -1, -1), (1, 0, -1), (-1, 0, -1))
)
COLUMNS = 16
ROWS = 32
F32 = jnp.float32
VMEM = pltpu.VMEM


def vmem_spec():
    return pl.BlockSpec(memory_space=pltpu.VMEM)


def any_spec():
    return pl.BlockSpec(memory_space=pl.ANY)


def params():
    return pltpu.CompilerParams(vmem_limit_bytes=12 << 20)


def lanes_of(like):
    return lax.broadcasted_iota(jnp.int32, like.shape, 1)


def rolled(value, shift, axis=1):
    shift = shift % value.shape[axis]
    return value if shift == 0 else pltpu.roll(value, shift, axis)


def pack_columns(values, source, packed=None, base=0):
    lane = lanes_of(values[0])
    if packed is None:
        packed = jnp.zeros_like(values[0])
    for number, value in enumerate(values, base):
        packed = jnp.where(lane == number, rolled(value, number - source), packed)
    return packed


def spread_columns(ref, width):
    return jnp.concatenate([ref[...]] * (width // COLUMNS), axis=0).T


def for_rows(total, body):
    def step(number, carry):
        body(pl.multiple_of(number * ROWS, ROWS))
        return carry

    lax.fori_loop(0, total // ROWS, step, 0)


def peterlin_of(c_xx, c_yy, c_zz):
    return (EXTENSION_SQ - 3.0) / (EXTENSION_SQ - (c_xx + c_yy + c_zz))


def divide(conf_ref, plane, early_ref, late_ref):
    for number, f in enumerate((0, 3, 4)):
        early_ref[number] = conf_ref[f, plane]
    early_ref[3] = conf_ref[1, plane] + conf_ref[2, plane]
    late_ref[0] = conf_ref[1, plane]
    late_ref[1] = conf_ref[5, plane]


def load_kernel(near_plane, conf_hbm, conf_ref, early_ref, late_ref, sems):
    near = near_plane[0]
    copy = pltpu.make_async_copy(conf_hbm, conf_ref, sems.at[0])
    copy.start()
    copy.wait()
    divide(conf_ref, near, early_ref, late_ref)


def load(near_plane, conform):
    shape = conform.shape
    return pl.pallas_call(
        load_kernel,
        out_shape=(
            jax.ShapeDtypeStruct(shape, F32),
            jax.ShapeDtypeStruct((4,) + shape[2:], F32),
            jax.ShapeDtypeStruct((2,) + shape[2:], F32),
        ),
        in_specs=[pl.BlockSpec(memory_space=pltpu.SMEM), any_spec()],
        out_specs=(vmem_spec(),) * 3,
        scratch_shapes=[pltpu.SemaphoreType.DMA((1,))],
        compiler_params=params(),
        name="load",
    )(near_plane, conform)


def edge_kernel(conf_ref, up_ref, down_ref, up_tile, down_tile):
    height, width = conf_ref.shape[2:]

    def rows(start):
        at = pl.ds(start, ROWS)
        values = [conf_ref[f, p, at, :] for p in range(2) for f in range(6)]
        up_tile[at, :] = pack_columns(values, width - 1)
        down_tile[at, :] = pack_columns(values, 0)

    for_rows(height, rows)
    up_ref[...] = up_tile[...].T[0:COLUMNS]
    down_ref[...] = down_tile[...].T[0:COLUMNS]


def edges(conform):
    height, width = conform.shape[2:]
    out = jax.ShapeDtypeStruct((COLUMNS, height), F32)
    return pl.pallas_call(
        edge_kernel,
        out_shape=(out, out),
        in_specs=[vmem_spec()],
        out_specs=(vmem_spec(), vmem_spec()),
        scratch_shapes=[VMEM((height, width), F32)] * 2,
        compiler_params=params(),
        name="edges",
    )(conform)


def pick_kernel(far_plane, conf_ref, _, early_ref, late_ref):
    divide(conf_ref, far_plane[0], early_ref, late_ref)


def pick(far_plane, conform, after):
    shape = conform.shape
    return pl.pallas_call(
        pick_kernel,
        out_shape=(
            jax.ShapeDtypeStruct((4,) + shape[2:], F32),
            jax.ShapeDtypeStruct((2,) + shape[2:], F32),
        ),
        in_specs=[pl.BlockSpec(memory_space=pltpu.SMEM), vmem_spec(), any_spec()],
        out_specs=(vmem_spec(),) * 2,
        compiler_params=params(),
        name="pick",
    )(far_plane, conform, after)


def moments_kernel(popul_hbm, _, popul_ref, sums_ref, sems):
    height = popul_ref.shape[2]
    copies = []
    for p in range(2):
        copies.append(pltpu.make_async_copy(popul_hbm.at[:, p], popul_ref.at[:, p], sems.at[p]))
        copies[-1].start()
    for p in range(2):
        copies[p].wait()

        def rows(start, p=p):
            at = pl.ds(start, ROWS)
            values = [popul_ref[i, p, at, :] for i in range(19)]
            density = values[0]
            for i in range(1, 19):
                density = density + values[i]
            sums_ref[0, p, at, :] = density
            for axis in range(3):
                moment = None
                for i in range(19):
                    if VELOCITIES[i][axis] == 1:
                        moment = values[i] if moment is None else moment + values[i]
                for i in range(19):
                    if VELOCITIES[i][axis] == -1:
                        moment = moment - values[i]
                sums_ref[1 + axis, p, at, :] = moment

        for_rows(height, rows)


def moments(popul, after):
    return pl.pallas_call(
        moments_kernel,
        out_shape=(
            jax.ShapeDtypeStruct(popul.shape, F32),
            jax.ShapeDtypeStruct((4,) + popul.shape[1:], F32),
        ),
        in_specs=[any_spec(), any_spec()],
        out_specs=(vmem_spec(),) * 2,
        scratch_shapes=[pltpu.SemaphoreType.DMA((2,))],
        compiler_params=params(),
        name="moments",
    )(popul, after)


def prepare_kernel(conf_ref, low_cols, high_cols, pre_ref, tall, low_ref, high_ref):
    height, width = conf_ref.shape[2:]
    low_ref[...] = spread_columns(low_cols, width)
    high_ref[...] = spread_columns(high_cols, width)

    def stress(fields, at_of):
        trace_parts = [at_of(f) for f in range(3)]
        peterlin = STRESS_SCALE * peterlin_of(*trace_parts)
        out = {}
        for f in fields:
            value = trace_parts[f] if f < 3 else at_of(f)
            out[f] = peterlin * value - (STRESS_SCALE if f < 3 else 0.0)
        return out

    for p in range(2):
        sign = 2 * p - 1

        def first(start, p=p, sign=sign):
            at = pl.ds(start, ROWS)
            own = stress(range(6), lambda f: conf_ref[f, p, at, :])
            other = stress((0, 3, 4), lambda f: conf_ref[f, 1 - p, at, :])
            low_pack = low_ref[at, :]
            high_pack = high_ref[at, :]
            low = stress((2, 4, 5), lambda f: rolled(low_pack, -(6 * p + f)))
            high = stress((2, 4, 5), lambda f: rolled(high_pack, width - 1 - (6 * p + f)))
            lane = lanes_of(low_pack)
            for number, f in enumerate((3, 1, 5)):
                tall[number, p, pl.ds(start + 8, ROWS), :] = own[f]
            for number in range(3):
                across = SYMMETRIC_INDEX[number][2]
                below = jnp.where(lane == 0, low[across], rolled(own[across], 1))
                above = jnp.where(lane == width - 1, high[across], rolled(own[across], -1))
                term = 0.5 * (above - below) - (0.5 * sign) * other[SYMMETRIC_INDEX[number][0]]
                if number == 0:
                    term = term + DRIVE_FORCE
                pre_ref[number, p, at, :] = term

        for_rows(height, first)
        for number in range(3):
            tall[number, p, 7:8, :] = tall[number, p, 8:9, :]
            tall[number, p, height + 8 : height + 9, :] = tall[number, p, height + 7 : height + 8, :]

        def second(start, p=p):
            at = pl.ds(start, ROWS)
            for number in range(3):
                above = tall[number, p, pl.ds(start + 9, ROWS), :]
                below = tall[number, p, pl.ds(start + 7, ROWS), :]
                pre_ref[number, p, at, :] = pre_ref[number, p, at, :] + 0.5 * (above - below)

        for_rows(height, second)


def prepare(conform, low, high):
    height, width = conform.shape[2:]
    return pl.pallas_call(
        prepare_kernel,
        out_shape=jax.ShapeDtypeStruct((3, 2, height, width), F32),
        in_specs=[vmem_spec()] * 3,
        out_specs=vmem_spec(),
        scratch_shapes=[VMEM((3, 2, height + 16, width), F32)]
        + [VMEM((height, width), F32)] * 2,
        compiler_params=params(),
        name="prepare",
    )(conform, low, high)


def collide_kernel(second, plane_ref, popul_ref, sums_ref, pre_ref, halo_ref, *refs):
    if second:
        _, up_in, down_in, _, post_ref, message_ref, up_out, down_out, up_ref, down_ref = refs
    else:
        post_ref, message_ref, up_ref, down_ref = refs
    height, width = halo_ref.shape[1:]
    plane = plane_ref[0]
    outward_plus = plane == 1
    half_sign = jnp.where(outward_plus, 0.5, -0.5).astype(F32)
    factor = 1.0 - 0.5 / SOLVENT_TIME
    keep = 1.0 - 1.0 / SOLVENT_TIME
    base = 8 if second else 0

    def rows(start):
        at = pl.ds(start, ROWS)
        halo = [halo_ref[f, at, :] for f in range(4)]
        trace = halo[0] + halo[3]
        peterlin = (STRESS_SCALE * (EXTENSION_SQ - 3.0)) / (EXTENSION_SQ - trace)
        stress = (peterlin * halo[0] - STRESS_SCALE, peterlin * halo[1], peterlin * halo[2])
        force = [pre_ref[a, plane, at, :] + half_sign * stress[a] for a in range(3)]
        density = sums_ref[0, plane, at, :]
        inverse = 1.0 / density
        velocity = [(sums_ref[1 + a, plane, at, :] + 0.5 * force[a]) * inverse for a in range(3)]
        speed_sq = (
            velocity[0] * velocity[0] + velocity[1] * velocity[1] + velocity[2] * velocity[2]
        )
        push = velocity[0] * force[0] + velocity[1] * force[1] + velocity[2] * force[2]
        rate = density * (1.0 / SOLVENT_TIME)
        common = rate * (1.0 - 1.5 * speed_sq) - (3.0 * factor) * push
        flow = [rate * velocity[a] for a in range(3)]
        drag = [factor * force[a] for a in range(3)]
        post = [None] * 19
        post[0] = keep * popul_ref[0, plane, at, :] + LATTICE_WEIGHTS[0] * common

        def along(vec, parts):
            total = None
            for axis in range(3):
                if vec[axis] == 1:
                    total = parts[axis] if total is None else total + parts[axis]
                elif vec[axis] == -1:
                    total = total - parts[axis]
            return total

        for i in range(1, 19, 2):
            vec = VELOCITIES[i]
            weight = LATTICE_WEIGHTS[i]
            c_u = along(vec, velocity)
            c_flow = along(vec, flow)
            c_drag = along(vec, drag)
            total = c_flow + c_drag
            even = weight * common + (4.5 * weight) * (c_u * (total + c_drag))
            odd = (3.0 * weight) * total
            post[i] = keep * popul_ref[i, plane, at, :] + (even + odd)
            post[i + 1] = keep * popul_ref[i + 1, plane, at, :] + (even - odd)
        for i in range(19):
            post_ref[i, plane, at, :] = post[i]
        for a in range(3):
            message_ref[a, at, :] = velocity[a]
        for slot in range(5):
            message_ref[3 + slot, at, :] = jnp.where(
                outward_plus, post[PLUS[slot]], post[MINUS[slot]]
            )
        up = up_in[at, :] if second else None
        down = down_in[at, :] if second else None
        up_ref[at, :] = pack_columns(
            velocity + [post[i] for i in Z_UP], width - 1, up, base
        )
        down_ref[at, :] = pack_columns(velocity + [post[i] for i in Z_DOWN], 0, down, base)

    for_rows(height, rows)
    if second:
        up_out[...] = up_ref[...].T[0:COLUMNS]
        down_out[...] = down_ref[...].T[0:COLUMNS]


def collide(plane, popul, sums, pre, halo, earlier=None):
    height, width = popul.shape[2:]
    second = earlier is not None
    tile = jax.ShapeDtypeStruct((COLUMNS, height) if second else (height, width), F32)
    operands = [plane, popul, sums, pre, halo] + (list(earlier) if second else [])
    return pl.pallas_call(
        functools.partial(collide_kernel, second),
        in_specs=[pl.BlockSpec(memory_space=pltpu.SMEM)]
        + [vmem_spec()] * 7
        + [any_spec()] * (len(operands) - 8)
        if second
        else [pl.BlockSpec(memory_space=pltpu.SMEM)] + [vmem_spec()] * 4,
        out_specs=(vmem_spec(),) * 4,
        out_shape=(
            jax.ShapeDtypeStruct(popul.shape, F32),
            jax.ShapeDtypeStruct((8, height, width), F32),
            tile,
            tile,
        ),
        scratch_shapes=[VMEM((height, width), F32)] * 2 if second else [],
        input_output_aliases={5: 0} if second else {},
        compiler_params=params(),
        name="collide_odd" if second else "collide_even",
    )(*operands)


def corner_kernel(low_ref, high_ref, first_ref, second_ref):
    for number, out in enumerate((first_ref, second_ref)):
        out[0:8, :] = low_ref[8 * number : 8 * number + 8, :]
        out[8:16, :] = high_ref[8 * number : 8 * number + 8, :]


def corners(low, high):
    out = jax.ShapeDtypeStruct(low.shape, F32)
    return pl.pallas_call(
        corner_kernel,
        out_shape=(out, out),
        in_specs=[vmem_spec()] * 2,
        out_specs=(vmem_spec(), vmem_spec()),
        compiler_params=params(),
        name="corners",
    )(low, high)


def inner_kernel(
    plane_e,
    plane_o,
    conf_ref,
    early_e,
    late_e,
    early_o,
    late_o,
    conf_low_cols,
    conf_high_cols,
    low_cols,
    high_cols,
    post_ref,
    velo_e,
    velo_o,
    read_ref,
    part_ref,
    conf_tall,
    velo_tall,
    halo,
    shifted,
    conf_low,
    conf_high,
    low_ref,
    high_ref,
    sems,
):
    height, width = conf_ref.shape[2:]
    conf_low[...] = spread_columns(conf_low_cols, width)
    conf_high[...] = spread_columns(conf_high_cols, width)
    low_ref[...] = spread_columns(low_cols, width)
    high_ref[...] = spread_columns(high_cols, width)
    planes = (plane_e[0], plane_o[0])
    for p, early, late in ((planes[0], early_e, late_e), (planes[1], early_o, late_o)):
        for number, f in enumerate((0, 3, 4)):
            halo[p, f] = early[number]
        halo[p, 1] = late[0]
        halo[p, 2] = early[3] - late[0]
        halo[p, 5] = late[1]
    for face, velo in enumerate((velo_e, velo_o)):
        p = planes[face]
        for a in range(3):
            velo_tall[a, p, 8 : 8 + height, :] = velo[a]
            velo_tall[a, p, 7:8, :] = -velo[a, 0:1, :]
            velo_tall[a, p, height + 8 : height + 9, :] = -velo[a, height - 1 : height, :]
    for p in range(2):
        for f in range(6):
            conf_tall[f, p, 8 : 8 + height, :] = conf_ref[f, p]
            conf_tall[f, p, 7:8, :] = conf_ref[f, p, 0:1, :]
            conf_tall[f, p, height + 8 : height + 9, :] = conf_ref[f, p, height - 1 : height, :]

    even_first = planes[0] == 0

    def lane_of(p, field):
        return (field, 8 + field) if p == 0 else (8 + field, field)

    def edge_value(pack, p, field, target):
        when_first, otherwise = lane_of(p, field)
        return jnp.where(
            even_first, rolled(pack, target - when_first), rolled(pack, target - otherwise)
        )

    copies = []
    full_low = low_ref[...]
    full_high = high_ref[...]
    lane = lanes_of(full_low)
    for i in range(19):
        step_x, step_y, step_z = VELOCITIES[i]
        for p in range(2):
            q = p - step_x
            if q not in (0, 1):
                continue
            tile = post_ref.at[i, q]
            if step_y or step_z:
                value = post_ref[i, q]
                if step_z == 1:
                    edge = edge_value(full_low, q, 3 + Z_UP.index(i), 0)
                    value = jnp.where(lane == 0, edge, rolled(value, 1))
                elif step_z == -1:
                    edge = edge_value(full_high, q, 3 + Z_DOWN.index(i), width - 1)
                    value = jnp.where(lane == width - 1, edge, rolled(value, -1))
                back = OPPOSITE[i]
                tile = shifted.at[i, p]
                if step_y == 1:
                    tile[1:height, :] = value[: height - 1]
                    tile[0:1, :] = post_ref[back, p, 0:1, :]
                elif step_y == -1:
                    tile[0 : height - 1, :] = value[1:]
                    tile[height - 1 : height, :] = post_ref[back, p, height - 1 : height, :]
                else:
                    tile[...] = value
            copies.append(pltpu.make_async_copy(tile, read_ref.at[i, p], sems.at[len(copies)]))
            copies[-1].start()

    for p in range(2):
        sign = 2 * p - 1

        def rows(start, p=p, sign=sign):
            at = pl.ds(start, ROWS)
            upper = pl.ds(start + 9, ROWS)
            lower = pl.ds(start + 7, ROWS)
            cl_pack = conf_low[at, :]
            ch_pack = conf_high[at, :]
            l_pack = low_ref[at, :]
            h_pack = high_ref[at, :]
            lane = lanes_of(cl_pack)
            first = lane == 0
            final = lane == width - 1
            velocity = [velo_tall[a, p, pl.ds(start + 8, ROWS), :] for a in range(3)]
            grad = [[None] * 3 for _ in range(3)]
            for a in range(3):
                grad[0][a] = (-0.5 * sign) * velo_tall[a, 1 - p, pl.ds(start + 8, ROWS), :]
                grad[1][a] = 0.5 * (velo_tall[a, p, upper, :] - velo_tall[a, p, lower, :])
                above = jnp.where(
                    final, edge_value(h_pack, p, a, width - 1), rolled(velocity[a], -1)
                )
                below = jnp.where(first, edge_value(l_pack, p, a, 0), rolled(velocity[a], 1))
                grad[2][a] = 0.5 * (above - below)
            own = [conf_ref[f, p, at, :] for f in range(6)]
            peterlin = (1.0 / RELAX_TIME) * peterlin_of(own[0], own[1], own[2])
            for f in range(6):
                i, j = COMPONENT_PAIRS[f]
                x_in = conf_ref[f, 1 - p, at, :]
                x_out = halo[p, f, at, :]
                y_up = conf_tall[f, p, upper, :]
                y_low = conf_tall[f, p, lower, :]
                lane_number = 6 * p + f
                z_up = jnp.where(
                    final, rolled(ch_pack, width - 1 - lane_number), rolled(own[f], -1)
                )
                z_low = jnp.where(first, rolled(cl_pack, -lane_number), rolled(own[f], 1))
                around = (x_in + x_out) + (y_up + y_low) + (z_up + z_low)
                advect = (
                    (sign * velocity[0]) * (x_out - x_in)
                    + velocity[1] * (y_up - y_low)
                    + velocity[2] * (z_up - z_low)
                )
                stretch = None
                for k in range(3):
                    term = own[SYMMETRIC_INDEX[i][k]] * grad[k][j]
                    if i != j:
                        term = term + grad[k][i] * own[SYMMETRIC_INDEX[k][j]]
                    stretch = term if stretch is None else stretch + term
                if i == j:
                    stretch = 2.0 * stretch
                relax = peterlin * own[f]
                if f < 3:
                    relax = relax - 1.0 / RELAX_TIME
                part_ref[f, p, at, :] = (
                    own[f]
                    - 0.5 * advect
                    + stretch
                    - relax
                    + DIFFUSIVITY * (around - 6.0 * own[f])
                )

        for_rows(height, rows)
    for copy in copies:
        copy.wait()


def inner(plane_e, plane_o, conform, halos, conf_low, conf_high, low, high, post, velo_e, velo_o):
    height, width = conform.shape[2:]
    velo_spec = pl.BlockSpec((3, height, width), lambda g: (0, 0, 0))
    whole = lambda shape: pl.BlockSpec(shape, lambda g: (0,) * len(shape))
    return pl.pallas_call(
        inner_kernel,
        grid=(1,),
        out_shape=(
            jax.ShapeDtypeStruct(post.shape, F32),
            jax.ShapeDtypeStruct(conform.shape, F32),
        ),
        in_specs=[
            pl.BlockSpec(memory_space=pltpu.SMEM),
            pl.BlockSpec(memory_space=pltpu.SMEM),
            whole(conform.shape),
            *[whole(halo.shape) for halo in halos],
            whole(conf_low.shape),
            whole(conf_low.shape),
            whole(conf_low.shape),
            whole(conf_low.shape),
            whole(post.shape),
            velo_spec,
            velo_spec,
        ],
        out_specs=(any_spec(), whole(conform.shape)),
        scratch_shapes=[
            VMEM((6, 2, height + 16, width), F32),
            VMEM((3, 2, height + 16, width), F32),
            VMEM((2, 6, height, width), F32),
            VMEM(post.shape, F32),
            VMEM((height, width), F32),
            VMEM((height, width), F32),
            VMEM((height, width), F32),
            VMEM((height, width), F32),
            pltpu.SemaphoreType.DMA((28,)),
        ],
        compiler_params=params(),
        name="inner",
    )(plane_e, plane_o, conform, *halos, conf_low, conf_high, low, high, post, velo_e, velo_o)


def finish_kernel(parted, chained, plane_ref, part_ref, conf_ref, corner, *refs):
    if parted:
        velo, cross, sent = refs[:3]
        refs = refs[3:]
    else:
        got, sent = refs[:2]
        velo, cross, sent = got.at[0:3], got.at[3:8], sent.at[3:8]
        refs = refs[2:]
    read_ref, new_ref, tile, new_tile, sems = refs[2:] if chained else refs[1:]
    height, width = conf_ref.shape[2:]
    plane = plane_ref[0]
    copies = []

    def send(source, target):
        copies.append(pltpu.make_async_copy(source, target, sems.at[len(copies)]))
        copies[-1].start()

    lane = lax.broadcasted_iota(jnp.int32, (height, width), 1)
    targets = [
        read_ref.at[jnp.where(plane == 1, MINUS[slot], PLUS[slot]), plane] for slot in range(5)
    ]
    send(cross.at[0], targets[0])
    tile[0, 1:height, :] = cross[1, 0 : height - 1, :]
    tile[0, 0:1, :] = sent[2, 0:1, :]
    send(tile.at[0], targets[1])
    tile[1, 0 : height - 1, :] = cross[2, 1:height, :]
    tile[1, height - 1 : height, :] = sent[1, height - 1 : height, :]
    send(tile.at[1], targets[2])
    low = jnp.broadcast_to(corner[pl.ds(6 + plane, 1), :], (width, height)).T
    tile[2] = jnp.where(lane == 0, low, rolled(cross[3], 1))
    send(tile.at[2], targets[3])
    high = jnp.broadcast_to(corner[pl.ds(14 + plane, 1), :], (width, height)).T
    tile[3] = jnp.where(lane == width - 1, high, rolled(cross[4], -1))
    send(tile.at[3], targets[4])
    half_sign = jnp.where(plane == 1, 0.5, -0.5).astype(F32)

    def rows(start):
        at = pl.ds(start, ROWS)
        slope = [half_sign * velo[a, at, :] for a in range(3)]
        row = [conf_ref[f, plane, at, :] for f in (0, 3, 4)]
        for f in range(6):
            i, j = COMPONENT_PAIRS[f]
            if i == j:
                term = 2.0 * (row[i] * slope[j])
            else:
                term = row[i] * slope[j] + slope[i] * row[j]
            new_tile[f, at, :] = part_ref[f, plane, at, :] + term

    for_rows(height, rows)
    for f in range(6):
        send(new_tile.at[f], new_ref.at[f, plane])
    for copy in copies:
        copy.wait()


def finish(plane, part, conform, corner, got, read, new=None):
    height, width = conform.shape[2:]
    chained = new is not None
    operands = [plane, part, conform, corner, *got, read] + ([new] if chained else [])
    first = 4 + len(got)
    return pl.pallas_call(
        functools.partial(finish_kernel, len(got) == 3, chained),
        out_shape=(
            jax.ShapeDtypeStruct(read.shape, F32),
            jax.ShapeDtypeStruct(conform.shape, F32),
        ),
        in_specs=[pl.BlockSpec(memory_space=pltpu.SMEM)]
        + [vmem_spec()] * (first - 1)
        + [any_spec()] * (2 if chained else 1),
        out_specs=(any_spec(), any_spec()),
        scratch_shapes=[
            VMEM((4, height, width), F32),
            VMEM((6, height, width), F32),
            pltpu.SemaphoreType.DMA((11,)),
        ],
        input_output_aliases={first: 0, first + 1: 1} if chained else {first: 0},
        compiler_params=params(),
        name="finish_last" if chained else "finish_first",
    )(*operands)


def body(popul, conform):
    wide = lax.axis_size("wide")
    narrow = lax.axis_size("narrow")
    odd = lax.rem(lax.axis_index("wide"), 2)
    plane_e = (1 - odd).astype(jnp.int32).reshape(1)
    plane_o = odd.astype(jnp.int32).reshape(1)
    even_pairs = [(i, i ^ 1) for i in range(wide)]
    odd_pairs = [(i, (i + 1) % wide if i % 2 else (i - 1) % wide) for i in range(wide)]
    up = [(i, (i + 1) % narrow) for i in range(narrow)]
    down = [(j, i) for i, j in up]

    conform, early, late = load(plane_e, conform)
    early_e = lax.ppermute(early, "wide", even_pairs)
    late_e = lax.ppermute(late, "wide", even_pairs)
    conf_up, conf_down = edges(conform)
    conf_low = lax.ppermute(conf_up, "narrow", up)
    conf_high = lax.ppermute(conf_down, "narrow", down)
    early, late = pick(plane_o, conform, conf_up)
    popul, sums = moments(popul, early)
    early_o = lax.ppermute(early, "wide", odd_pairs)
    late_o = lax.ppermute(late, "wide", odd_pairs)
    pre = prepare(conform, conf_low, conf_high)
    post, sent_e, z_up, z_down = collide(plane_e, popul, sums, pre, early_e)
    got_e = lax.ppermute(sent_e, "wide", even_pairs)
    post, sent_o, z_up, z_down = collide(
        plane_o, popul, sums, pre, early_o, (post, z_up, z_down, late_e)
    )
    got_o = lax.ppermute(sent_o, "wide", odd_pairs)
    low = lax.ppermute(z_up, "narrow", up)
    high = lax.ppermute(z_down, "narrow", down)
    corner_e, corner_o = corners(low, high)
    corner_e = lax.ppermute(corner_e, "wide", even_pairs)
    corner_o = lax.ppermute(corner_o, "wide", odd_pairs)
    read, part = inner(
        plane_e,
        plane_o,
        conform,
        (early_e, late_e, early_o, late_o),
        conf_low,
        conf_high,
        low,
        high,
        post,
        sent_e,
        sent_o,
    )
    read, new = finish(plane_e, part, conform, corner_e, (got_e, sent_e), read)
    return finish(plane_o, part, conform, corner_o, (got_o, sent_o), read, new)


def solution(mesh):
    placed = P(None, "wide", None, "narrow")
    return jax.shard_map(
        body, mesh=mesh, in_specs=(placed, placed), out_specs=(placed, placed), check_vma=False
    )
```

```python
import functools

import jax
import jax.numpy as jnp
from jax import lax
from jax.experimental import pallas as pl
from jax.experimental.pallas import tpu as pltpu
from jax.sharding import PartitionSpec as P

VELOCITIES = (
    (0, 0, 0),
    (1, 0, 0),
    (-1, 0, 0),
    (0, 1, 0),
    (0, -1, 0),
    (0, 0, 1),
    (0, 0, -1),
    (1, 1, 0),
    (-1, -1, 0),
    (1, -1, 0),
    (-1, 1, 0),
    (1, 0, 1),
    (-1, 0, -1),
    (1, 0, -1),
    (-1, 0, 1),
    (0, 1, 1),
    (0, -1, -1),
    (0, 1, -1),
    (0, -1, 1),
)
LATTICE_WEIGHTS = (1.0 / 3.0,) + (1.0 / 18.0,) * 6 + (1.0 / 36.0,) * 12
OPPOSITE = (0, 2, 1, 4, 3, 6, 5, 8, 7, 10, 9, 12, 11, 14, 13, 16, 15, 18, 17)
SYMMETRIC_INDEX = ((0, 3, 4), (3, 1, 5), (4, 5, 2))
COMPONENT_PAIRS = ((0, 0), (1, 1), (2, 2), (0, 1), (0, 2), (1, 2))
SOLVENT_TIME = 0.8
RELAX_TIME = 20.0
POLYMER_VISC = 1.0
EXTENSION_SQ = 100.0
DIFFUSIVITY = 0.05
DRIVE_FORCE = 1e-05
STRESS_SCALE = POLYMER_VISC / RELAX_TIME

SLOT_SHIFTS = ((0, 0), (1, 0), (-1, 0), (0, 1), (0, -1))
PLUS = tuple(VELOCITIES.index((1, cy, cz)) for cy, cz in SLOT_SHIFTS)
MINUS = tuple(VELOCITIES.index((-1, cy, cz)) for cy, cz in SLOT_SHIFTS)
Z_UP = tuple(VELOCITIES.index(v) for v in ((0, 0, 1), (0, 1, 1), (0, -1, 1), (1, 0, 1), (-1, 0, 1)))
Z_DOWN = tuple(
    VELOCITIES.index(v) for v in ((0, 0, -1), (0, 1, -1), (0, -1, -1), (1, 0, -1), (-1, 0, -1))
)
COLUMNS = 16
ROWS = 32
F32 = jnp.float32
VMEM = pltpu.VMEM


def vmem_spec():
    return pl.BlockSpec(memory_space=pltpu.VMEM)


def any_spec():
    return pl.BlockSpec(memory_space=pl.ANY)


def params():
    return pltpu.CompilerParams(vmem_limit_bytes=12 << 20)


def lanes_of(like):
    return lax.broadcasted_iota(jnp.int32, like.shape, 1)


def rolled(value, shift, axis=1):
    shift = shift % value.shape[axis]
    return value if shift == 0 else pltpu.roll(value, shift, axis)


def pack_columns(values, source, packed=None, base=0):
    lane = lanes_of(values[0])
    if packed is None:
        packed = jnp.zeros_like(values[0])
    for number, value in enumerate(values, base):
        packed = jnp.where(lane == number, rolled(value, number - source), packed)
    return packed


def spread_columns(ref, width):
    return jnp.concatenate([ref[...]] * (width // COLUMNS), axis=0).T


def for_rows(total, body):
    def step(number, carry):
        body(pl.multiple_of(number * ROWS, ROWS))
        return carry

    lax.fori_loop(0, total // ROWS, step, 0)


def peterlin_of(c_xx, c_yy, c_zz):
    return (EXTENSION_SQ - 3.0) / (EXTENSION_SQ - (c_xx + c_yy + c_zz))


def divide(conf_ref, plane, early_ref, late_ref):
    for number, f in enumerate((0, 3, 4)):
        early_ref[number] = conf_ref[f, plane]
    early_ref[3] = conf_ref[1, plane] + conf_ref[2, plane]
    late_ref[0] = conf_ref[1, plane]
    late_ref[1] = conf_ref[5, plane]


def load_kernel(near_plane, conf_hbm, conf_ref, early_ref, late_ref, sems):
    near = near_plane[0]
    copy = pltpu.make_async_copy(conf_hbm, conf_ref, sems.at[0])
    copy.start()
    copy.wait()
    divide(conf_ref, near, early_ref, late_ref)


def load(near_plane, conform):
    shape = conform.shape
    return pl.pallas_call(
        load_kernel,
        out_shape=(
            jax.ShapeDtypeStruct(shape, F32),
            jax.ShapeDtypeStruct((4,) + shape[2:], F32),
            jax.ShapeDtypeStruct((2,) + shape[2:], F32),
        ),
        in_specs=[pl.BlockSpec(memory_space=pltpu.SMEM), any_spec()],
        out_specs=(vmem_spec(),) * 3,
        scratch_shapes=[pltpu.SemaphoreType.DMA((1,))],
        compiler_params=params(),
        name="load",
    )(near_plane, conform)


def edge_kernel(conf_ref, up_ref, down_ref, up_tile, down_tile):
    height, width = conf_ref.shape[2:]

    def rows(start):
        at = pl.ds(start, ROWS)
        values = [conf_ref[f, p, at, :] for p in range(2) for f in range(6)]
        up_tile[at, :] = pack_columns(values, width - 1)
        down_tile[at, :] = pack_columns(values, 0)

    for_rows(height, rows)
    up_ref[...] = up_tile[...].T[0:COLUMNS]
    down_ref[...] = down_tile[...].T[0:COLUMNS]


def edges(conform):
    height, width = conform.shape[2:]
    out = jax.ShapeDtypeStruct((COLUMNS, height), F32)
    return pl.pallas_call(
        edge_kernel,
        out_shape=(out, out),
        in_specs=[vmem_spec()],
        out_specs=(vmem_spec(), vmem_spec()),
        scratch_shapes=[VMEM((height, width), F32)] * 2,
        compiler_params=params(),
        name="edges",
    )(conform)


def pick_kernel(far_plane, conf_ref, _, early_ref, late_ref):
    divide(conf_ref, far_plane[0], early_ref, late_ref)


def pick(far_plane, conform, after):
    shape = conform.shape
    return pl.pallas_call(
        pick_kernel,
        out_shape=(
            jax.ShapeDtypeStruct((4,) + shape[2:], F32),
            jax.ShapeDtypeStruct((2,) + shape[2:], F32),
        ),
        in_specs=[pl.BlockSpec(memory_space=pltpu.SMEM), vmem_spec(), any_spec()],
        out_specs=(vmem_spec(),) * 2,
        compiler_params=params(),
        name="pick",
    )(far_plane, conform, after)


def moments_kernel(popul_hbm, _, popul_ref, sums_ref, sems):
    height = popul_ref.shape[2]
    copies = []
    for p in range(2):
        copies.append(pltpu.make_async_copy(popul_hbm.at[:, p], popul_ref.at[:, p], sems.at[p]))
        copies[-1].start()
    for p in range(2):
        copies[p].wait()

        def rows(start, p=p):
            at = pl.ds(start, ROWS)
            values = [popul_ref[i, p, at, :] for i in range(19)]
            density = values[0]
            for i in range(1, 19):
                density = density + values[i]
            sums_ref[0, p, at, :] = density
            for axis in range(3):
                moment = None
                for i in range(19):
                    if VELOCITIES[i][axis] == 1:
                        moment = values[i] if moment is None else moment + values[i]
                for i in range(19):
                    if VELOCITIES[i][axis] == -1:
                        moment = moment - values[i]
                sums_ref[1 + axis, p, at, :] = moment

        for_rows(height, rows)


def moments(popul, after):
    return pl.pallas_call(
        moments_kernel,
        out_shape=(
            jax.ShapeDtypeStruct(popul.shape, F32),
            jax.ShapeDtypeStruct((4,) + popul.shape[1:], F32),
        ),
        in_specs=[any_spec(), any_spec()],
        out_specs=(vmem_spec(),) * 2,
        scratch_shapes=[pltpu.SemaphoreType.DMA((2,))],
        compiler_params=params(),
        name="moments",
    )(popul, after)


def prepare_kernel(conf_ref, low_cols, high_cols, pre_ref, tall, low_ref, high_ref):
    height, width = conf_ref.shape[2:]
    low_ref[...] = spread_columns(low_cols, width)
    high_ref[...] = spread_columns(high_cols, width)

    def stress(fields, at_of):
        trace_parts = [at_of(f) for f in range(3)]
        peterlin = STRESS_SCALE * peterlin_of(*trace_parts)
        out = {}
        for f in fields:
            value = trace_parts[f] if f < 3 else at_of(f)
            out[f] = peterlin * value - (STRESS_SCALE if f < 3 else 0.0)
        return out

    for p in range(2):
        sign = 2 * p - 1

        def first(start, p=p, sign=sign):
            at = pl.ds(start, ROWS)
            own = stress(range(6), lambda f: conf_ref[f, p, at, :])
            other = stress((0, 3, 4), lambda f: conf_ref[f, 1 - p, at, :])
            low_pack = low_ref[at, :]
            high_pack = high_ref[at, :]
            low = stress((2, 4, 5), lambda f: rolled(low_pack, -(6 * p + f)))
            high = stress((2, 4, 5), lambda f: rolled(high_pack, width - 1 - (6 * p + f)))
            lane = lanes_of(low_pack)
            for number, f in enumerate((3, 1, 5)):
                tall[number, p, pl.ds(start + 8, ROWS), :] = own[f]
            for number in range(3):
                across = SYMMETRIC_INDEX[number][2]
                below = jnp.where(lane == 0, low[across], rolled(own[across], 1))
                above = jnp.where(lane == width - 1, high[across], rolled(own[across], -1))
                term = 0.5 * (above - below) - (0.5 * sign) * other[SYMMETRIC_INDEX[number][0]]
                if number == 0:
                    term = term + DRIVE_FORCE
                pre_ref[number, p, at, :] = term

        for_rows(height, first)
        for number in range(3):
            tall[number, p, 7:8, :] = tall[number, p, 8:9, :]
            tall[number, p, height + 8 : height + 9, :] = tall[number, p, height + 7 : height + 8, :]

        def second(start, p=p):
            at = pl.ds(start, ROWS)
            for number in range(3):
                above = tall[number, p, pl.ds(start + 9, ROWS), :]
                below = tall[number, p, pl.ds(start + 7, ROWS), :]
                pre_ref[number, p, at, :] = pre_ref[number, p, at, :] + 0.5 * (above - below)

        for_rows(height, second)


def prepare(conform, low, high):
    height, width = conform.shape[2:]
    return pl.pallas_call(
        prepare_kernel,
        out_shape=jax.ShapeDtypeStruct((3, 2, height, width), F32),
        in_specs=[vmem_spec()] * 3,
        out_specs=vmem_spec(),
        scratch_shapes=[VMEM((3, 2, height + 16, width), F32)]
        + [VMEM((height, width), F32)] * 2,
        compiler_params=params(),
        name="prepare",
    )(conform, low, high)


def collide_kernel(second, plane_ref, popul_ref, sums_ref, pre_ref, halo_ref, *refs):
    if second:
        _, up_in, down_in, _, post_ref, message_ref, up_out, down_out, up_ref, down_ref = refs
    else:
        post_ref, message_ref, up_ref, down_ref = refs
    height, width = halo_ref.shape[1:]
    plane = plane_ref[0]
    outward_plus = plane == 1
    half_sign = jnp.where(outward_plus, 0.5, -0.5).astype(F32)
    factor = 1.0 - 0.5 / SOLVENT_TIME
    keep = 1.0 - 1.0 / SOLVENT_TIME
    base = 8 if second else 0

    def rows(start):
        at = pl.ds(start, ROWS)
        halo = [halo_ref[f, at, :] for f in range(4)]
        trace = halo[0] + halo[3]
        peterlin = (STRESS_SCALE * (EXTENSION_SQ - 3.0)) / (EXTENSION_SQ - trace)
        stress = (peterlin * halo[0] - STRESS_SCALE, peterlin * halo[1], peterlin * halo[2])
        force = [pre_ref[a, plane, at, :] + half_sign * stress[a] for a in range(3)]
        density = sums_ref[0, plane, at, :]
        inverse = 1.0 / density
        velocity = [(sums_ref[1 + a, plane, at, :] + 0.5 * force[a]) * inverse for a in range(3)]
        speed_sq = (
            velocity[0] * velocity[0] + velocity[1] * velocity[1] + velocity[2] * velocity[2]
        )
        push = velocity[0] * force[0] + velocity[1] * force[1] + velocity[2] * force[2]
        rate = density * (1.0 / SOLVENT_TIME)
        common = rate * (1.0 - 1.5 * speed_sq) - (3.0 * factor) * push
        flow = [rate * velocity[a] for a in range(3)]
        drag = [factor * force[a] for a in range(3)]
        post = [None] * 19
        post[0] = keep * popul_ref[0, plane, at, :] + LATTICE_WEIGHTS[0] * common

        def along(vec, parts):
            total = None
            for axis in range(3):
                if vec[axis] == 1:
                    total = parts[axis] if total is None else total + parts[axis]
                elif vec[axis] == -1:
                    total = total - parts[axis]
            return total

        for i in range(1, 19, 2):
            vec = VELOCITIES[i]
            weight = LATTICE_WEIGHTS[i]
            c_u = along(vec, velocity)
            c_flow = along(vec, flow)
            c_drag = along(vec, drag)
            total = c_flow + c_drag
            even = weight * common + (4.5 * weight) * (c_u * (total + c_drag))
            odd = (3.0 * weight) * total
            post[i] = keep * popul_ref[i, plane, at, :] + (even + odd)
            post[i + 1] = keep * popul_ref[i + 1, plane, at, :] + (even - odd)
        for i in range(19):
            post_ref[i, plane, at, :] = post[i]
        for a in range(3):
            message_ref[a, at, :] = velocity[a]
        for slot in range(5):
            message_ref[3 + slot, at, :] = jnp.where(
                outward_plus, post[PLUS[slot]], post[MINUS[slot]]
            )
        up = up_in[at, :] if second else None
        down = down_in[at, :] if second else None
        up_ref[at, :] = pack_columns(
            velocity + [post[i] for i in Z_UP], width - 1, up, base
        )
        down_ref[at, :] = pack_columns(velocity + [post[i] for i in Z_DOWN], 0, down, base)

    for_rows(height, rows)
    if second:
        up_out[...] = up_ref[...].T[0:COLUMNS]
        down_out[...] = down_ref[...].T[0:COLUMNS]


def collide(plane, popul, sums, pre, halo, earlier=None):
    height, width = popul.shape[2:]
    second = earlier is not None
    tile = jax.ShapeDtypeStruct((COLUMNS, height) if second else (height, width), F32)
    operands = [plane, popul, sums, pre, halo] + (list(earlier) if second else [])
    return pl.pallas_call(
        functools.partial(collide_kernel, second),
        in_specs=[pl.BlockSpec(memory_space=pltpu.SMEM)]
        + [vmem_spec()] * 7
        + [any_spec()] * (len(operands) - 8)
        if second
        else [pl.BlockSpec(memory_space=pltpu.SMEM)] + [vmem_spec()] * 4,
        out_specs=(vmem_spec(),) * 4,
        out_shape=(
            jax.ShapeDtypeStruct(popul.shape, F32),
            jax.ShapeDtypeStruct((8, height, width), F32),
            tile,
            tile,
        ),
        scratch_shapes=[VMEM((height, width), F32)] * 2 if second else [],
        input_output_aliases={5: 0} if second else {},
        compiler_params=params(),
        name="collide_odd" if second else "collide_even",
    )(*operands)


def corner_kernel(low_ref, high_ref, first_ref, second_ref):
    for number, out in enumerate((first_ref, second_ref)):
        out[0:8, :] = low_ref[8 * number : 8 * number + 8, :]
        out[8:16, :] = high_ref[8 * number : 8 * number + 8, :]


def corners(low, high):
    out = jax.ShapeDtypeStruct(low.shape, F32)
    return pl.pallas_call(
        corner_kernel,
        out_shape=(out, out),
        in_specs=[vmem_spec()] * 2,
        out_specs=(vmem_spec(), vmem_spec()),
        compiler_params=params(),
        name="corners",
    )(low, high)


def inner_kernel(
    plane_e,
    plane_o,
    conf_ref,
    early_e,
    late_e,
    early_o,
    late_o,
    conf_low_cols,
    conf_high_cols,
    low_cols,
    high_cols,
    post_ref,
    velo_e,
    velo_o,
    read_ref,
    part_ref,
    conf_tall,
    velo_tall,
    halo,
    shifted,
    conf_low,
    conf_high,
    low_ref,
    high_ref,
    sems,
):
    height, width = conf_ref.shape[2:]
    conf_low[...] = spread_columns(conf_low_cols, width)
    conf_high[...] = spread_columns(conf_high_cols, width)
    low_ref[...] = spread_columns(low_cols, width)
    high_ref[...] = spread_columns(high_cols, width)
    planes = (plane_e[0], plane_o[0])
    for p, early, late in ((planes[0], early_e, late_e), (planes[1], early_o, late_o)):
        for number, f in enumerate((0, 3, 4)):
            halo[p, f] = early[number]
        halo[p, 1] = late[0]
        halo[p, 2] = early[3] - late[0]
        halo[p, 5] = late[1]
    for face, velo in enumerate((velo_e, velo_o)):
        p = planes[face]
        for a in range(3):
            velo_tall[a, p, 8 : 8 + height, :] = velo[a]
            velo_tall[a, p, 7:8, :] = -velo[a, 0:1, :]
            velo_tall[a, p, height + 8 : height + 9, :] = -velo[a, height - 1 : height, :]
    for p in range(2):
        for f in range(6):
            conf_tall[f, p, 8 : 8 + height, :] = conf_ref[f, p]
            conf_tall[f, p, 7:8, :] = conf_ref[f, p, 0:1, :]
            conf_tall[f, p, height + 8 : height + 9, :] = conf_ref[f, p, height - 1 : height, :]

    even_first = planes[0] == 0

    def lane_of(p, field):
        return (field, 8 + field) if p == 0 else (8 + field, field)

    def edge_value(pack, p, field, target):
        when_first, otherwise = lane_of(p, field)
        return jnp.where(
            even_first, rolled(pack, target - when_first), rolled(pack, target - otherwise)
        )

    copies = []
    full_low = low_ref[...]
    full_high = high_ref[...]
    lane = lanes_of(full_low)
    for i in range(19):
        step_x, step_y, step_z = VELOCITIES[i]
        for p in range(2):
            q = p - step_x
            if q not in (0, 1):
                continue
            tile = post_ref.at[i, q]
            if step_y or step_z:
                value = post_ref[i, q]
                if step_z == 1:
                    edge = edge_value(full_low, q, 3 + Z_UP.index(i), 0)
                    value = jnp.where(lane == 0, edge, rolled(value, 1))
                elif step_z == -1:
                    edge = edge_value(full_high, q, 3 + Z_DOWN.index(i), width - 1)
                    value = jnp.where(lane == width - 1, edge, rolled(value, -1))
                back = OPPOSITE[i]
                tile = shifted.at[i, p]
                if step_y == 1:
                    tile[1:height, :] = value[: height - 1]
                    tile[0:1, :] = post_ref[back, p, 0:1, :]
                elif step_y == -1:
                    tile[0 : height - 1, :] = value[1:]
                    tile[height - 1 : height, :] = post_ref[back, p, height - 1 : height, :]
                else:
                    tile[...] = value
            copies.append(pltpu.make_async_copy(tile, read_ref.at[i, p], sems.at[len(copies)]))
            copies[-1].start()

    for p in range(2):
        sign = 2 * p - 1

        def rows(start, p=p, sign=sign):
            at = pl.ds(start, ROWS)
            upper = pl.ds(start + 9, ROWS)
            lower = pl.ds(start + 7, ROWS)
            cl_pack = conf_low[at, :]
            ch_pack = conf_high[at, :]
            l_pack = low_ref[at, :]
            h_pack = high_ref[at, :]
            lane = lanes_of(cl_pack)
            first = lane == 0
            final = lane == width - 1
            velocity = [velo_tall[a, p, pl.ds(start + 8, ROWS), :] for a in range(3)]
            grad = [[None] * 3 for _ in range(3)]
            for a in range(3):
                grad[0][a] = (-0.5 * sign) * velo_tall[a, 1 - p, pl.ds(start + 8, ROWS), :]
                grad[1][a] = 0.5 * (velo_tall[a, p, upper, :] - velo_tall[a, p, lower, :])
                above = jnp.where(
                    final, edge_value(h_pack, p, a, width - 1), rolled(velocity[a], -1)
                )
                below = jnp.where(first, edge_value(l_pack, p, a, 0), rolled(velocity[a], 1))
                grad[2][a] = 0.5 * (above - below)
            own = [conf_ref[f, p, at, :] for f in range(6)]
            peterlin = (1.0 / RELAX_TIME) * peterlin_of(own[0], own[1], own[2])
            for f in range(6):
                i, j = COMPONENT_PAIRS[f]
                x_in = conf_ref[f, 1 - p, at, :]
                x_out = halo[p, f, at, :]
                y_up = conf_tall[f, p, upper, :]
                y_low = conf_tall[f, p, lower, :]
                lane_number = 6 * p + f
                z_up = jnp.where(
                    final, rolled(ch_pack, width - 1 - lane_number), rolled(own[f], -1)
                )
                z_low = jnp.where(first, rolled(cl_pack, -lane_number), rolled(own[f], 1))
                around = (x_in + x_out) + (y_up + y_low) + (z_up + z_low)
                advect = (
                    (sign * velocity[0]) * (x_out - x_in)
                    + velocity[1] * (y_up - y_low)
                    + velocity[2] * (z_up - z_low)
                )
                stretch = None
                for k in range(3):
                    term = own[SYMMETRIC_INDEX[i][k]] * grad[k][j]
                    if i != j:
                        term = term + grad[k][i] * own[SYMMETRIC_INDEX[k][j]]
                    stretch = term if stretch is None else stretch + term
                if i == j:
                    stretch = 2.0 * stretch
                relax = peterlin * own[f]
                if f < 3:
                    relax = relax - 1.0 / RELAX_TIME
                part_ref[f, p, at, :] = (
                    own[f]
                    - 0.5 * advect
                    + stretch
                    - relax
                    + DIFFUSIVITY * (around - 6.0 * own[f])
                )

        for_rows(height, rows)
    for copy in copies:
        copy.wait()


def inner(plane_e, plane_o, conform, halos, conf_low, conf_high, low, high, post, velo_e, velo_o):
    height, width = conform.shape[2:]
    velo_spec = pl.BlockSpec((3, height, width), lambda g: (0, 0, 0))
    whole = lambda shape: pl.BlockSpec(shape, lambda g: (0,) * len(shape))
    return pl.pallas_call(
        inner_kernel,
        grid=(1,),
        out_shape=(
            jax.ShapeDtypeStruct(post.shape, F32),
            jax.ShapeDtypeStruct(conform.shape, F32),
        ),
        in_specs=[
            pl.BlockSpec(memory_space=pltpu.SMEM),
            pl.BlockSpec(memory_space=pltpu.SMEM),
            whole(conform.shape),
            *[whole(halo.shape) for halo in halos],
            whole(conf_low.shape),
            whole(conf_low.shape),
            whole(conf_low.shape),
            whole(conf_low.shape),
            whole(post.shape),
            velo_spec,
            velo_spec,
        ],
        out_specs=(any_spec(), whole(conform.shape)),
        scratch_shapes=[
            VMEM((6, 2, height + 16, width), F32),
            VMEM((3, 2, height + 16, width), F32),
            VMEM((2, 6, height, width), F32),
            VMEM(post.shape, F32),
            VMEM((height, width), F32),
            VMEM((height, width), F32),
            VMEM((height, width), F32),
            VMEM((height, width), F32),
            pltpu.SemaphoreType.DMA((28,)),
        ],
        compiler_params=params(),
        name="inner",
    )(plane_e, plane_o, conform, *halos, conf_low, conf_high, low, high, post, velo_e, velo_o)


def touch_kernel(_, out_ref):
    out_ref[...] = jnp.zeros_like(out_ref)


def touch(value):
    return pl.pallas_call(
        touch_kernel,
        out_shape=jax.ShapeDtypeStruct((8, 128), F32),
        in_specs=[any_spec()],
        out_specs=vmem_spec(),
        compiler_params=params(),
        name="touch",
    )(value)


def finish_kernel(
    plane_e,
    plane_o,
    part_ref,
    conf_ref,
    got_e,
    sent_e,
    corner_e,
    got_o,
    sent_o,
    corner_o,
    _,
    __,
    read_ref,
    new_ref,
    read_tile,
    new_tile,
    sems,
):
    height, width = conf_ref.shape[2:]
    faces = ((plane_o[0], got_o, sent_o, corner_o), (plane_e[0], got_e, sent_e, corner_e))
    lane = lax.broadcasted_iota(jnp.int32, (height, width), 1)
    copies = []

    def send(source, target):
        copies.append(pltpu.make_async_copy(source, target, sems.at[len(copies)]))
        copies[-1].start()

    for face, (plane, got, sent, corner) in enumerate(faces):
        half_sign = jnp.where(plane == 1, 0.5, -0.5).astype(F32)
        tile = read_tile.at[face]
        targets = [
            read_ref.at[jnp.where(plane == 1, MINUS[slot], PLUS[slot]), plane] for slot in range(5)
        ]
        send(got.at[3], targets[0])

        def rows(start, face=face, plane=plane, half_sign=half_sign, got=got):
            at = pl.ds(start, ROWS)
            slope = [half_sign * got[a, at, :] for a in range(3)]
            row = [conf_ref[f, plane, at, :] for f in (0, 3, 4)]
            for f in range(6):
                i, j = COMPONENT_PAIRS[f]
                if i == j:
                    term = 2.0 * (row[i] * slope[j])
                else:
                    term = row[i] * slope[j] + slope[i] * row[j]
                new_tile[face, f, at, :] = part_ref[f, plane, at, :] + term

        for_rows(height, rows)
        send(new_tile.at[face], new_ref.at[:, plane])
        tile[0, 1:height, :] = got[4, 0 : height - 1, :]
        tile[0, 0:1, :] = sent[5, 0:1, :]
        send(tile.at[0], targets[1])
        tile[1, 0 : height - 1, :] = got[5, 1:height, :]
        tile[1, height - 1 : height, :] = sent[4, height - 1 : height, :]
        send(tile.at[1], targets[2])
        low = jnp.broadcast_to(corner[pl.ds(6 + plane, 1), :], (width, height)).T
        tile[2] = jnp.where(lane == 0, low, rolled(got[6], 1))
        send(tile.at[2], targets[3])
        high = jnp.broadcast_to(corner[pl.ds(14 + plane, 1), :], (width, height)).T
        tile[3] = jnp.where(lane == width - 1, high, rolled(got[7], -1))
        send(tile.at[3], targets[4])
    for copy in copies:
        copy.wait()


def finish(plane_e, plane_o, part, conform, even, odd, read):
    height, width = conform.shape[2:]
    smem = pl.BlockSpec(memory_space=pltpu.SMEM)
    return pl.pallas_call(
        finish_kernel,
        out_shape=(
            jax.ShapeDtypeStruct(read.shape, F32),
            jax.ShapeDtypeStruct(conform.shape, F32),
        ),
        in_specs=[smem] * 2 + [vmem_spec()] * 8 + [any_spec()] * 2,
        out_specs=(any_spec(), any_spec()),
        scratch_shapes=[
            VMEM((2, 4, height, width), F32),
            VMEM((2, 6, height, width), F32),
            pltpu.SemaphoreType.DMA((12,)),
        ],
        input_output_aliases={10: 0},
        compiler_params=params(),
        name="finish",
    )(plane_e, plane_o, part, conform, *even, *odd, read, touch(even[0]))


def body(popul, conform):
    wide = lax.axis_size("wide")
    narrow = lax.axis_size("narrow")
    odd = lax.rem(lax.axis_index("wide"), 2)
    plane_e = (1 - odd).astype(jnp.int32).reshape(1)
    plane_o = odd.astype(jnp.int32).reshape(1)
    even_pairs = [(i, i ^ 1) for i in range(wide)]
    odd_pairs = [(i, (i + 1) % wide if i % 2 else (i - 1) % wide) for i in range(wide)]
    up = [(i, (i + 1) % narrow) for i in range(narrow)]
    down = [(j, i) for i, j in up]

    conform, early, late = load(plane_e, conform)
    early_e = lax.ppermute(early, "wide", even_pairs)
    late_e = lax.ppermute(late, "wide", even_pairs)
    conf_up, conf_down = edges(conform)
    conf_low = lax.ppermute(conf_up, "narrow", up)
    conf_high = lax.ppermute(conf_down, "narrow", down)
    early, late = pick(plane_o, conform, conf_up)
    popul, sums = moments(popul, early)
    early_o = lax.ppermute(early, "wide", odd_pairs)
    late_o = lax.ppermute(late, "wide", odd_pairs)
    pre = prepare(conform, conf_low, conf_high)
    post, sent_e, z_up, z_down = collide(plane_e, popul, sums, pre, early_e)
    got_e = lax.ppermute(sent_e, "wide", even_pairs)
    post, sent_o, z_up, z_down = collide(
        plane_o, popul, sums, pre, early_o, (post, z_up, z_down, late_e)
    )
    got_o = lax.ppermute(sent_o, "wide", odd_pairs)
    low = lax.ppermute(z_up, "narrow", up)
    high = lax.ppermute(z_down, "narrow", down)
    corner_e, corner_o = corners(low, high)
    corner_e = lax.ppermute(corner_e, "wide", even_pairs)
    corner_o = lax.ppermute(corner_o, "wide", odd_pairs)
    read, part = inner(
        plane_e,
        plane_o,
        conform,
        (early_e, late_e, early_o, late_o),
        conf_low,
        conf_high,
        low,
        high,
        post,
        sent_e,
        sent_o,
    )
    even = (got_e, sent_e, corner_e)
    odd = (got_o, sent_o, corner_o)
    return finish(plane_e, plane_o, part, conform, even, odd, read)


def solution(mesh):
    placed = P(None, "wide", None, "narrow")
    return jax.shard_map(
        body, mesh=mesh, in_specs=(placed, placed), out_specs=(placed, placed), check_vma=False
    )
```

```python
import functools

import jax
import jax.numpy as jnp
from jax import lax
from jax.experimental import pallas as pl
from jax.experimental.pallas import tpu as pltpu
from jax.sharding import PartitionSpec as P

VELOCITIES = (
    (0, 0, 0),
    (1, 0, 0),
    (-1, 0, 0),
    (0, 1, 0),
    (0, -1, 0),
    (0, 0, 1),
    (0, 0, -1),
    (1, 1, 0),
    (-1, -1, 0),
    (1, -1, 0),
    (-1, 1, 0),
    (1, 0, 1),
    (-1, 0, -1),
    (1, 0, -1),
    (-1, 0, 1),
    (0, 1, 1),
    (0, -1, -1),
    (0, 1, -1),
    (0, -1, 1),
)
LATTICE_WEIGHTS = (1.0 / 3.0,) + (1.0 / 18.0,) * 6 + (1.0 / 36.0,) * 12
OPPOSITE = (0, 2, 1, 4, 3, 6, 5, 8, 7, 10, 9, 12, 11, 14, 13, 16, 15, 18, 17)
SYMMETRIC_INDEX = ((0, 3, 4), (3, 1, 5), (4, 5, 2))
COMPONENT_PAIRS = ((0, 0), (1, 1), (2, 2), (0, 1), (0, 2), (1, 2))
SOLVENT_TIME = 0.8
RELAX_TIME = 20.0
POLYMER_VISC = 1.0
EXTENSION_SQ = 100.0
DIFFUSIVITY = 0.05
DRIVE_FORCE = 1e-05
STRESS_SCALE = POLYMER_VISC / RELAX_TIME

SLOT_SHIFTS = ((0, 0), (1, 0), (-1, 0), (0, 1), (0, -1))
PLUS = tuple(VELOCITIES.index((1, cy, cz)) for cy, cz in SLOT_SHIFTS)
MINUS = tuple(VELOCITIES.index((-1, cy, cz)) for cy, cz in SLOT_SHIFTS)
Z_UP = tuple(VELOCITIES.index(v) for v in ((0, 0, 1), (0, 1, 1), (0, -1, 1), (1, 0, 1), (-1, 0, 1)))
Z_DOWN = tuple(
    VELOCITIES.index(v) for v in ((0, 0, -1), (0, 1, -1), (0, -1, -1), (1, 0, -1), (-1, 0, -1))
)
COLUMNS = 16
ROWS = 32
F32 = jnp.float32
VMEM = pltpu.VMEM


def vmem_spec():
    return pl.BlockSpec(memory_space=pltpu.VMEM)


def any_spec():
    return pl.BlockSpec(memory_space=pl.ANY)


def params():
    return pltpu.CompilerParams(vmem_limit_bytes=12 << 20)


def lanes_of(like):
    return lax.broadcasted_iota(jnp.int32, like.shape, 1)


def rolled(value, shift, axis=1):
    shift = shift % value.shape[axis]
    return value if shift == 0 else pltpu.roll(value, shift, axis)


def pack_columns(values, source, packed=None, base=0):
    lane = lanes_of(values[0])
    if packed is None:
        packed = jnp.zeros_like(values[0])
    for number, value in enumerate(values, base):
        packed = jnp.where(lane == number, rolled(value, number - source), packed)
    return packed


def spread_columns(ref, width):
    return jnp.concatenate([ref[...]] * (width // COLUMNS), axis=0).T


def for_rows(total, body):
    def step(number, carry):
        body(pl.multiple_of(number * ROWS, ROWS))
        return carry

    lax.fori_loop(0, total // ROWS, step, 0)


def peterlin_of(c_xx, c_yy, c_zz):
    return (EXTENSION_SQ - 3.0) / (EXTENSION_SQ - (c_xx + c_yy + c_zz))


def divide(conf_ref, plane, early_ref, late_ref):
    for number, f in enumerate((0, 3, 4)):
        early_ref[number] = conf_ref[f, plane]
    early_ref[3] = conf_ref[1, plane] + conf_ref[2, plane]
    late_ref[0] = conf_ref[1, plane]
    late_ref[1] = conf_ref[5, plane]


def load_kernel(near_plane, conf_hbm, conf_ref, early_ref, late_ref, sems):
    near = near_plane[0]
    copy = pltpu.make_async_copy(conf_hbm, conf_ref, sems.at[0])
    copy.start()
    copy.wait()
    divide(conf_ref, near, early_ref, late_ref)


def load(near_plane, conform):
    shape = conform.shape
    return pl.pallas_call(
        load_kernel,
        out_shape=(
            jax.ShapeDtypeStruct(shape, F32),
            jax.ShapeDtypeStruct((4,) + shape[2:], F32),
            jax.ShapeDtypeStruct((2,) + shape[2:], F32),
        ),
        in_specs=[pl.BlockSpec(memory_space=pltpu.SMEM), any_spec()],
        out_specs=(vmem_spec(),) * 3,
        scratch_shapes=[pltpu.SemaphoreType.DMA((1,))],
        compiler_params=params(),
        name="load",
    )(near_plane, conform)


def edge_kernel(conf_ref, up_ref, down_ref, up_tile, down_tile):
    height, width = conf_ref.shape[2:]

    def rows(start):
        at = pl.ds(start, ROWS)
        values = [conf_ref[f, p, at, :] for p in range(2) for f in range(6)]
        up_tile[at, :] = pack_columns(values, width - 1)
        down_tile[at, :] = pack_columns(values, 0)

    for_rows(height, rows)
    up_ref[...] = up_tile[...].T[0:COLUMNS]
    down_ref[...] = down_tile[...].T[0:COLUMNS]


def edges(conform):
    height, width = conform.shape[2:]
    out = jax.ShapeDtypeStruct((COLUMNS, height), F32)
    return pl.pallas_call(
        edge_kernel,
        out_shape=(out, out),
        in_specs=[vmem_spec()],
        out_specs=(vmem_spec(), vmem_spec()),
        scratch_shapes=[VMEM((height, width), F32)] * 2,
        compiler_params=params(),
        name="edges",
    )(conform)


def pick_kernel(far_plane, conf_ref, _, early_ref, late_ref):
    divide(conf_ref, far_plane[0], early_ref, late_ref)


def pick(far_plane, conform, after):
    shape = conform.shape
    return pl.pallas_call(
        pick_kernel,
        out_shape=(
            jax.ShapeDtypeStruct((4,) + shape[2:], F32),
            jax.ShapeDtypeStruct((2,) + shape[2:], F32),
        ),
        in_specs=[pl.BlockSpec(memory_space=pltpu.SMEM), vmem_spec(), any_spec()],
        out_specs=(vmem_spec(),) * 2,
        compiler_params=params(),
        name="pick",
    )(far_plane, conform, after)


def moments_kernel(popul_hbm, _, popul_ref, sums_ref, sems):
    height = popul_ref.shape[2]
    copies = []
    for p in range(2):
        copies.append(pltpu.make_async_copy(popul_hbm.at[:, p], popul_ref.at[:, p], sems.at[p]))
        copies[-1].start()
    for p in range(2):
        copies[p].wait()

        def rows(start, p=p):
            at = pl.ds(start, ROWS)
            values = [popul_ref[i, p, at, :] for i in range(19)]
            density = values[0]
            for i in range(1, 19):
                density = density + values[i]
            sums_ref[0, p, at, :] = density
            for axis in range(3):
                moment = None
                for i in range(19):
                    if VELOCITIES[i][axis] == 1:
                        moment = values[i] if moment is None else moment + values[i]
                for i in range(19):
                    if VELOCITIES[i][axis] == -1:
                        moment = moment - values[i]
                sums_ref[1 + axis, p, at, :] = moment

        for_rows(height, rows)


def moments(popul, after):
    return pl.pallas_call(
        moments_kernel,
        out_shape=(
            jax.ShapeDtypeStruct(popul.shape, F32),
            jax.ShapeDtypeStruct((4,) + popul.shape[1:], F32),
        ),
        in_specs=[any_spec(), any_spec()],
        out_specs=(vmem_spec(),) * 2,
        scratch_shapes=[pltpu.SemaphoreType.DMA((2,))],
        compiler_params=params(),
        name="moments",
    )(popul, after)


def prepare_kernel(conf_ref, low_cols, high_cols, pre_ref, tall, low_ref, high_ref):
    height, width = conf_ref.shape[2:]
    low_ref[...] = spread_columns(low_cols, width)
    high_ref[...] = spread_columns(high_cols, width)

    def stress(fields, at_of):
        trace_parts = [at_of(f) for f in range(3)]
        peterlin = STRESS_SCALE * peterlin_of(*trace_parts)
        out = {}
        for f in fields:
            value = trace_parts[f] if f < 3 else at_of(f)
            out[f] = peterlin * value - (STRESS_SCALE if f < 3 else 0.0)
        return out

    for p in range(2):
        sign = 2 * p - 1

        def first(start, p=p, sign=sign):
            at = pl.ds(start, ROWS)
            own = stress(range(6), lambda f: conf_ref[f, p, at, :])
            other = stress((0, 3, 4), lambda f: conf_ref[f, 1 - p, at, :])
            low_pack = low_ref[at, :]
            high_pack = high_ref[at, :]
            low = stress((2, 4, 5), lambda f: rolled(low_pack, -(6 * p + f)))
            high = stress((2, 4, 5), lambda f: rolled(high_pack, width - 1 - (6 * p + f)))
            lane = lanes_of(low_pack)
            for number, f in enumerate((3, 1, 5)):
                tall[number, p, pl.ds(start + 8, ROWS), :] = own[f]
            for number in range(3):
                across = SYMMETRIC_INDEX[number][2]
                below = jnp.where(lane == 0, low[across], rolled(own[across], 1))
                above = jnp.where(lane == width - 1, high[across], rolled(own[across], -1))
                term = 0.5 * (above - below) - (0.5 * sign) * other[SYMMETRIC_INDEX[number][0]]
                if number == 0:
                    term = term + DRIVE_FORCE
                pre_ref[number, p, at, :] = term

        for_rows(height, first)
        for number in range(3):
            tall[number, p, 7:8, :] = tall[number, p, 8:9, :]
            tall[number, p, height + 8 : height + 9, :] = tall[number, p, height + 7 : height + 8, :]

        def second(start, p=p):
            at = pl.ds(start, ROWS)
            for number in range(3):
                above = tall[number, p, pl.ds(start + 9, ROWS), :]
                below = tall[number, p, pl.ds(start + 7, ROWS), :]
                pre_ref[number, p, at, :] = pre_ref[number, p, at, :] + 0.5 * (above - below)

        for_rows(height, second)


def prepare(conform, low, high):
    height, width = conform.shape[2:]
    return pl.pallas_call(
        prepare_kernel,
        out_shape=jax.ShapeDtypeStruct((3, 2, height, width), F32),
        in_specs=[vmem_spec()] * 3,
        out_specs=vmem_spec(),
        scratch_shapes=[VMEM((3, 2, height + 16, width), F32)]
        + [VMEM((height, width), F32)] * 2,
        compiler_params=params(),
        name="prepare",
    )(conform, low, high)


def collide_kernel(second, plane_ref, popul_ref, sums_ref, pre_ref, halo_ref, *refs):
    if second:
        _, up_in, down_in, _, post_ref, message_ref, up_out, down_out, up_ref, down_ref = refs
    else:
        post_ref, message_ref, up_ref, down_ref = refs
    height, width = halo_ref.shape[1:]
    plane = plane_ref[0]
    outward_plus = plane == 1
    half_sign = jnp.where(outward_plus, 0.5, -0.5).astype(F32)
    factor = 1.0 - 0.5 / SOLVENT_TIME
    keep = 1.0 - 1.0 / SOLVENT_TIME
    base = 8 if second else 0

    def rows(start):
        at = pl.ds(start, ROWS)
        halo = [halo_ref[f, at, :] for f in range(4)]
        trace = halo[0] + halo[3]
        peterlin = (STRESS_SCALE * (EXTENSION_SQ - 3.0)) / (EXTENSION_SQ - trace)
        stress = (peterlin * halo[0] - STRESS_SCALE, peterlin * halo[1], peterlin * halo[2])
        force = [pre_ref[a, plane, at, :] + half_sign * stress[a] for a in range(3)]
        density = sums_ref[0, plane, at, :]
        inverse = 1.0 / density
        velocity = [(sums_ref[1 + a, plane, at, :] + 0.5 * force[a]) * inverse for a in range(3)]
        speed_sq = (
            velocity[0] * velocity[0] + velocity[1] * velocity[1] + velocity[2] * velocity[2]
        )
        push = velocity[0] * force[0] + velocity[1] * force[1] + velocity[2] * force[2]
        rate = density * (1.0 / SOLVENT_TIME)
        common = rate * (1.0 - 1.5 * speed_sq) - (3.0 * factor) * push
        flow = [rate * velocity[a] for a in range(3)]
        drag = [factor * force[a] for a in range(3)]
        post = [None] * 19
        post[0] = keep * popul_ref[0, plane, at, :] + LATTICE_WEIGHTS[0] * common

        def along(vec, parts):
            total = None
            for axis in range(3):
                if vec[axis] == 1:
                    total = parts[axis] if total is None else total + parts[axis]
                elif vec[axis] == -1:
                    total = total - parts[axis]
            return total

        for i in range(1, 19, 2):
            vec = VELOCITIES[i]
            weight = LATTICE_WEIGHTS[i]
            c_u = along(vec, velocity)
            c_flow = along(vec, flow)
            c_drag = along(vec, drag)
            total = c_flow + c_drag
            even = weight * common + (4.5 * weight) * (c_u * (total + c_drag))
            odd = (3.0 * weight) * total
            post[i] = keep * popul_ref[i, plane, at, :] + (even + odd)
            post[i + 1] = keep * popul_ref[i + 1, plane, at, :] + (even - odd)
        for i in range(19):
            post_ref[i, plane, at, :] = post[i]
        for a in range(3):
            message_ref[a, at, :] = velocity[a]
        for slot in range(5):
            message_ref[3 + slot, at, :] = jnp.where(
                outward_plus, post[PLUS[slot]], post[MINUS[slot]]
            )
        up = up_in[at, :] if second else None
        down = down_in[at, :] if second else None
        up_ref[at, :] = pack_columns(
            velocity + [post[i] for i in Z_UP], width - 1, up, base
        )
        down_ref[at, :] = pack_columns(velocity + [post[i] for i in Z_DOWN], 0, down, base)

    for_rows(height, rows)
    if second:
        up_out[...] = up_ref[...].T[0:COLUMNS]
        down_out[...] = down_ref[...].T[0:COLUMNS]


def collide(plane, popul, sums, pre, halo, earlier=None):
    height, width = popul.shape[2:]
    second = earlier is not None
    tile = jax.ShapeDtypeStruct((COLUMNS, height) if second else (height, width), F32)
    operands = [plane, popul, sums, pre, halo] + (list(earlier) if second else [])
    return pl.pallas_call(
        functools.partial(collide_kernel, second),
        in_specs=[pl.BlockSpec(memory_space=pltpu.SMEM)]
        + [vmem_spec()] * 7
        + [any_spec()] * (len(operands) - 8)
        if second
        else [pl.BlockSpec(memory_space=pltpu.SMEM)] + [vmem_spec()] * 4,
        out_specs=(vmem_spec(),) * 4,
        out_shape=(
            jax.ShapeDtypeStruct(popul.shape, F32),
            jax.ShapeDtypeStruct((8, height, width), F32),
            tile,
            tile,
        ),
        scratch_shapes=[VMEM((height, width), F32)] * 2 if second else [],
        input_output_aliases={5: 0} if second else {},
        compiler_params=params(),
        name="collide_odd" if second else "collide_even",
    )(*operands)


def corner_kernel(plane_1, plane_2, low_ref, high_ref, first_ref, second_ref):
    for base, plane, out in ((0, plane_1[0], first_ref), (8, plane_2[0], second_ref)):
        row = base + 7 - plane
        out[0:1, :] = low_ref[pl.ds(row, 1), :]
        out[1:2, :] = high_ref[pl.ds(row, 1), :]


def corners(plane_1, plane_2, low, high):
    out = jax.ShapeDtypeStruct((2, low.shape[1]), F32)
    smem = pl.BlockSpec(memory_space=pltpu.SMEM)
    return pl.pallas_call(
        corner_kernel,
        out_shape=(out, out),
        in_specs=[smem, smem, vmem_spec(), vmem_spec()],
        out_specs=(vmem_spec(), vmem_spec()),
        compiler_params=params(),
        name="corners",
    )(plane_1, plane_2, low, high)


def inner_kernel(
    plane_e,
    plane_o,
    conf_ref,
    early_e,
    late_e,
    early_o,
    late_o,
    conf_low_cols,
    conf_high_cols,
    low_cols,
    high_cols,
    post_ref,
    velo_e,
    velo_o,
    read_ref,
    part_ref,
    conf_tall,
    velo_tall,
    halo,
    shifted,
    conf_low,
    conf_high,
    low_ref,
    high_ref,
    sems,
):
    height, width = conf_ref.shape[2:]
    conf_low[...] = spread_columns(conf_low_cols, width)
    conf_high[...] = spread_columns(conf_high_cols, width)
    low_ref[...] = spread_columns(low_cols, width)
    high_ref[...] = spread_columns(high_cols, width)
    planes = (plane_e[0], plane_o[0])
    for p, early, late in ((planes[0], early_e, late_e), (planes[1], early_o, late_o)):
        for number, f in enumerate((0, 3, 4)):
            halo[p, f] = early[number]
        halo[p, 1] = late[0]
        halo[p, 2] = early[3] - late[0]
        halo[p, 5] = late[1]
    for face, velo in enumerate((velo_e, velo_o)):
        p = planes[face]
        for a in range(3):
            velo_tall[a, p, 8 : 8 + height, :] = velo[a]
            velo_tall[a, p, 7:8, :] = -velo[a, 0:1, :]
            velo_tall[a, p, height + 8 : height + 9, :] = -velo[a, height - 1 : height, :]
    for p in range(2):
        for f in range(6):
            conf_tall[f, p, 8 : 8 + height, :] = conf_ref[f, p]
            conf_tall[f, p, 7:8, :] = conf_ref[f, p, 0:1, :]
            conf_tall[f, p, height + 8 : height + 9, :] = conf_ref[f, p, height - 1 : height, :]

    even_first = planes[0] == 0

    def lane_of(p, field):
        return (field, 8 + field) if p == 0 else (8 + field, field)

    def edge_value(pack, p, field, target):
        when_first, otherwise = lane_of(p, field)
        return jnp.where(
            even_first, rolled(pack, target - when_first), rolled(pack, target - otherwise)
        )

    copies = []
    full_low = low_ref[...]
    full_high = high_ref[...]
    lane = lanes_of(full_low)
    for i in range(19):
        step_x, step_y, step_z = VELOCITIES[i]
        for p in range(2):
            q = p - step_x
            if q not in (0, 1):
                continue
            tile = post_ref.at[i, q]
            if step_y or step_z:
                value = post_ref[i, q]
                if step_z == 1:
                    edge = edge_value(full_low, q, 3 + Z_UP.index(i), 0)
                    value = jnp.where(lane == 0, edge, rolled(value, 1))
                elif step_z == -1:
                    edge = edge_value(full_high, q, 3 + Z_DOWN.index(i), width - 1)
                    value = jnp.where(lane == width - 1, edge, rolled(value, -1))
                back = OPPOSITE[i]
                tile = shifted.at[i, p]
                if step_y == 1:
                    tile[1:height, :] = value[: height - 1]
                    tile[0:1, :] = post_ref[back, p, 0:1, :]
                elif step_y == -1:
                    tile[0 : height - 1, :] = value[1:]
                    tile[height - 1 : height, :] = post_ref[back, p, height - 1 : height, :]
                else:
                    tile[...] = value
            copies.append(pltpu.make_async_copy(tile, read_ref.at[i, p], sems.at[len(copies)]))
            copies[-1].start()

    for p in range(2):
        sign = 2 * p - 1

        def rows(start, p=p, sign=sign):
            at = pl.ds(start, ROWS)
            upper = pl.ds(start + 9, ROWS)
            lower = pl.ds(start + 7, ROWS)
            cl_pack = conf_low[at, :]
            ch_pack = conf_high[at, :]
            l_pack = low_ref[at, :]
            h_pack = high_ref[at, :]
            lane = lanes_of(cl_pack)
            first = lane == 0
            final = lane == width - 1
            velocity = [velo_tall[a, p, pl.ds(start + 8, ROWS), :] for a in range(3)]
            grad = [[None] * 3 for _ in range(3)]
            for a in range(3):
                grad[0][a] = (-0.5 * sign) * velo_tall[a, 1 - p, pl.ds(start + 8, ROWS), :]
                grad[1][a] = 0.5 * (velo_tall[a, p, upper, :] - velo_tall[a, p, lower, :])
                above = jnp.where(
                    final, edge_value(h_pack, p, a, width - 1), rolled(velocity[a], -1)
                )
                below = jnp.where(first, edge_value(l_pack, p, a, 0), rolled(velocity[a], 1))
                grad[2][a] = 0.5 * (above - below)
            own = [conf_ref[f, p, at, :] for f in range(6)]
            peterlin = (1.0 / RELAX_TIME) * peterlin_of(own[0], own[1], own[2])
            for f in range(6):
                i, j = COMPONENT_PAIRS[f]
                x_in = conf_ref[f, 1 - p, at, :]
                x_out = halo[p, f, at, :]
                y_up = conf_tall[f, p, upper, :]
                y_low = conf_tall[f, p, lower, :]
                lane_number = 6 * p + f
                z_up = jnp.where(
                    final, rolled(ch_pack, width - 1 - lane_number), rolled(own[f], -1)
                )
                z_low = jnp.where(first, rolled(cl_pack, -lane_number), rolled(own[f], 1))
                around = (x_in + x_out) + (y_up + y_low) + (z_up + z_low)
                advect = (
                    (sign * velocity[0]) * (x_out - x_in)
                    + velocity[1] * (y_up - y_low)
                    + velocity[2] * (z_up - z_low)
                )
                stretch = None
                for k in range(3):
                    term = own[SYMMETRIC_INDEX[i][k]] * grad[k][j]
                    if i != j:
                        term = term + grad[k][i] * own[SYMMETRIC_INDEX[k][j]]
                    stretch = term if stretch is None else stretch + term
                if i == j:
                    stretch = 2.0 * stretch
                relax = peterlin * own[f]
                if f < 3:
                    relax = relax - 1.0 / RELAX_TIME
                part_ref[f, p, at, :] = (
                    own[f]
                    - 0.5 * advect
                    + stretch
                    - relax
                    + DIFFUSIVITY * (around - 6.0 * own[f])
                )

        for_rows(height, rows)
    for copy in copies:
        copy.wait()


def inner(plane_e, plane_o, conform, halos, conf_low, conf_high, low, high, post, velo_e, velo_o):
    height, width = conform.shape[2:]
    velo_spec = pl.BlockSpec((3, height, width), lambda g: (0, 0, 0))
    whole = lambda shape: pl.BlockSpec(shape, lambda g: (0,) * len(shape))
    return pl.pallas_call(
        inner_kernel,
        grid=(1,),
        out_shape=(
            jax.ShapeDtypeStruct(post.shape, F32),
            jax.ShapeDtypeStruct(conform.shape, F32),
        ),
        in_specs=[
            pl.BlockSpec(memory_space=pltpu.SMEM),
            pl.BlockSpec(memory_space=pltpu.SMEM),
            whole(conform.shape),
            *[whole(halo.shape) for halo in halos],
            whole(conf_low.shape),
            whole(conf_low.shape),
            whole(conf_low.shape),
            whole(conf_low.shape),
            whole(post.shape),
            velo_spec,
            velo_spec,
        ],
        out_specs=(any_spec(), whole(conform.shape)),
        scratch_shapes=[
            VMEM((6, 2, height + 16, width), F32),
            VMEM((3, 2, height + 16, width), F32),
            VMEM((2, 6, height, width), F32),
            VMEM(post.shape, F32),
            VMEM((height, width), F32),
            VMEM((height, width), F32),
            VMEM((height, width), F32),
            VMEM((height, width), F32),
            pltpu.SemaphoreType.DMA((28,)),
        ],
        compiler_params=params(),
        name="inner",
    )(plane_e, plane_o, conform, *halos, conf_low, conf_high, low, high, post, velo_e, velo_o)


def touch_kernel(_, out_ref):
    out_ref[...] = jnp.zeros_like(out_ref)


def touch(value):
    return pl.pallas_call(
        touch_kernel,
        out_shape=jax.ShapeDtypeStruct((8, 128), F32),
        in_specs=[any_spec()],
        out_specs=vmem_spec(),
        compiler_params=params(),
        name="touch",
    )(value)


def finish_kernel(
    plane_e,
    plane_o,
    part_ref,
    conf_ref,
    got_e,
    sent_e,
    corner_e,
    got_o,
    sent_o,
    corner_o,
    _,
    __,
    read_ref,
    new_ref,
    read_tile,
    new_tile,
    sems,
):
    height, width = conf_ref.shape[2:]
    faces = ((plane_o[0], got_o, sent_o, corner_o), (plane_e[0], got_e, sent_e, corner_e))
    lane = lax.broadcasted_iota(jnp.int32, (height, width), 1)
    copies = []

    def send(source, target):
        copies.append(pltpu.make_async_copy(source, target, sems.at[len(copies)]))
        copies[-1].start()

    for face, (plane, got, sent, corner) in enumerate(faces):
        half_sign = jnp.where(plane == 1, 0.5, -0.5).astype(F32)
        tile = read_tile.at[face]
        targets = [
            read_ref.at[jnp.where(plane == 1, MINUS[slot], PLUS[slot]), plane] for slot in range(5)
        ]
        send(got.at[3], targets[0])

        def rows(start, face=face, plane=plane, half_sign=half_sign, got=got):
            at = pl.ds(start, ROWS)
            slope = [half_sign * got[a, at, :] for a in range(3)]
            row = [conf_ref[f, plane, at, :] for f in (0, 3, 4)]
            for f in range(6):
                i, j = COMPONENT_PAIRS[f]
                if i == j:
                    term = 2.0 * (row[i] * slope[j])
                else:
                    term = row[i] * slope[j] + slope[i] * row[j]
                new_tile[face, f, at, :] = part_ref[f, plane, at, :] + term

        for_rows(height, rows)
        send(new_tile.at[face], new_ref.at[:, plane])
        tile[0, 1:height, :] = got[4, 0 : height - 1, :]
        tile[0, 0:1, :] = sent[5, 0:1, :]
        send(tile.at[0], targets[1])
        tile[1, 0 : height - 1, :] = got[5, 1:height, :]
        tile[1, height - 1 : height, :] = sent[4, height - 1 : height, :]
        send(tile.at[1], targets[2])
        low = jnp.broadcast_to(corner[0:1, :], (width, height)).T
        tile[2] = jnp.where(lane == 0, low, rolled(got[6], 1))
        send(tile.at[2], targets[3])
        high = jnp.broadcast_to(corner[1:2, :], (width, height)).T
        tile[3] = jnp.where(lane == width - 1, high, rolled(got[7], -1))
        send(tile.at[3], targets[4])
    for copy in copies:
        copy.wait()


def finish(plane_e, plane_o, part, conform, even, odd, read):
    height, width = conform.shape[2:]
    smem = pl.BlockSpec(memory_space=pltpu.SMEM)
    return pl.pallas_call(
        finish_kernel,
        out_shape=(
            jax.ShapeDtypeStruct(read.shape, F32),
            jax.ShapeDtypeStruct(conform.shape, F32),
        ),
        in_specs=[smem] * 2 + [vmem_spec()] * 8 + [any_spec()] * 2,
        out_specs=(any_spec(), any_spec()),
        scratch_shapes=[
            VMEM((2, 4, height, width), F32),
            VMEM((2, 6, height, width), F32),
            pltpu.SemaphoreType.DMA((12,)),
        ],
        input_output_aliases={10: 0},
        compiler_params=params(),
        name="finish",
    )(plane_e, plane_o, part, conform, *even, *odd, read, touch(even[0]))


def body(popul, conform):
    wide = lax.axis_size("wide")
    narrow = lax.axis_size("narrow")
    odd = lax.rem(lax.axis_index("wide"), 2)
    plane_e = (1 - odd).astype(jnp.int32).reshape(1)
    plane_o = odd.astype(jnp.int32).reshape(1)
    even_pairs = [(i, i ^ 1) for i in range(wide)]
    odd_pairs = [(i, (i + 1) % wide if i % 2 else (i - 1) % wide) for i in range(wide)]
    up = [(i, (i + 1) % narrow) for i in range(narrow)]
    down = [(j, i) for i, j in up]

    conform, early, late = load(plane_e, conform)
    early_e = lax.ppermute(early, "wide", even_pairs)
    late_e = lax.ppermute(late, "wide", even_pairs)
    conf_up, conf_down = edges(conform)
    conf_low = lax.ppermute(conf_up, "narrow", up)
    conf_high = lax.ppermute(conf_down, "narrow", down)
    early, late = pick(plane_o, conform, conf_up)
    popul, sums = moments(popul, early)
    early_o = lax.ppermute(early, "wide", odd_pairs)
    late_o = lax.ppermute(late, "wide", odd_pairs)
    pre = prepare(conform, conf_low, conf_high)
    post, sent_e, z_up, z_down = collide(plane_e, popul, sums, pre, early_e)
    got_e = lax.ppermute(sent_e, "wide", even_pairs)
    post, sent_o, z_up, z_down = collide(
        plane_o, popul, sums, pre, early_o, (post, z_up, z_down, late_e)
    )
    got_o = lax.ppermute(sent_o, "wide", odd_pairs)
    low = lax.ppermute(z_up, "narrow", up)
    high = lax.ppermute(z_down, "narrow", down)
    corner_e, corner_o = corners(plane_e, plane_o, low, high)
    corner_e = lax.ppermute(corner_e, "wide", even_pairs)
    corner_o = lax.ppermute(corner_o, "wide", odd_pairs)
    read, part = inner(
        plane_e,
        plane_o,
        conform,
        (early_e, late_e, early_o, late_o),
        conf_low,
        conf_high,
        low,
        high,
        post,
        sent_e,
        sent_o,
    )
    even = (got_e, sent_e, corner_e)
    odd = (got_o, sent_o, corner_o)
    return finish(plane_e, plane_o, part, conform, even, odd, read)


def solution(mesh):
    placed = P(None, "wide", None, "narrow")
    return jax.shard_map(
        body, mesh=mesh, in_specs=(placed, placed), out_specs=(placed, placed), check_vma=False
    )
```

```python
import functools

import jax
import jax.numpy as jnp
from jax import lax
from jax.experimental import pallas as pl
from jax.experimental.pallas import tpu as pltpu
from jax.sharding import PartitionSpec as P

VELOCITIES = (
    (0, 0, 0),
    (1, 0, 0),
    (-1, 0, 0),
    (0, 1, 0),
    (0, -1, 0),
    (0, 0, 1),
    (0, 0, -1),
    (1, 1, 0),
    (-1, -1, 0),
    (1, -1, 0),
    (-1, 1, 0),
    (1, 0, 1),
    (-1, 0, -1),
    (1, 0, -1),
    (-1, 0, 1),
    (0, 1, 1),
    (0, -1, -1),
    (0, 1, -1),
    (0, -1, 1),
)
LATTICE_WEIGHTS = (1.0 / 3.0,) + (1.0 / 18.0,) * 6 + (1.0 / 36.0,) * 12
OPPOSITE = (0, 2, 1, 4, 3, 6, 5, 8, 7, 10, 9, 12, 11, 14, 13, 16, 15, 18, 17)
SYMMETRIC_INDEX = ((0, 3, 4), (3, 1, 5), (4, 5, 2))
COMPONENT_PAIRS = ((0, 0), (1, 1), (2, 2), (0, 1), (0, 2), (1, 2))
SOLVENT_TIME = 0.8
RELAX_TIME = 20.0
POLYMER_VISC = 1.0
EXTENSION_SQ = 100.0
DIFFUSIVITY = 0.05
DRIVE_FORCE = 1e-05
STRESS_SCALE = POLYMER_VISC / RELAX_TIME

SLOT_SHIFTS = ((0, 0), (1, 0), (-1, 0), (0, 1), (0, -1))
PLUS = tuple(VELOCITIES.index((1, cy, cz)) for cy, cz in SLOT_SHIFTS)
MINUS = tuple(VELOCITIES.index((-1, cy, cz)) for cy, cz in SLOT_SHIFTS)
Z_UP = tuple(VELOCITIES.index(v) for v in ((0, 0, 1), (0, 1, 1), (0, -1, 1), (1, 0, 1), (-1, 0, 1)))
Z_DOWN = tuple(
    VELOCITIES.index(v) for v in ((0, 0, -1), (0, 1, -1), (0, -1, -1), (1, 0, -1), (-1, 0, -1))
)
COLUMNS = 16
ROWS = 32
F32 = jnp.float32
VMEM = pltpu.VMEM


def vmem_spec():
    return pl.BlockSpec(memory_space=pltpu.VMEM)


def any_spec():
    return pl.BlockSpec(memory_space=pl.ANY)


def params():
    return pltpu.CompilerParams(vmem_limit_bytes=12 << 20)


def lanes_of(like):
    return lax.broadcasted_iota(jnp.int32, like.shape, 1)


def rolled(value, shift, axis=1):
    shift = shift % value.shape[axis]
    return value if shift == 0 else pltpu.roll(value, shift, axis)


def pack_columns(values, source, packed=None, base=0):
    lane = lanes_of(values[0])
    if packed is None:
        packed = jnp.zeros_like(values[0])
    for number, value in enumerate(values, base):
        packed = jnp.where(lane == number, rolled(value, number - source), packed)
    return packed


def spread_columns(ref, width):
    return jnp.concatenate([ref[...]] * (width // COLUMNS), axis=0).T


def for_rows(total, body):
    def step(number, carry):
        body(pl.multiple_of(number * ROWS, ROWS))
        return carry

    lax.fori_loop(0, total // ROWS, step, 0)


def peterlin_of(c_xx, c_yy, c_zz):
    return (EXTENSION_SQ - 3.0) / (EXTENSION_SQ - (c_xx + c_yy + c_zz))


def divide(conf_ref, plane, early_ref, late_ref):
    for number, f in enumerate((0, 3, 4)):
        early_ref[number] = conf_ref[f, plane]
    early_ref[3] = conf_ref[1, plane] + conf_ref[2, plane]
    late_ref[0] = conf_ref[1, plane]
    late_ref[1] = conf_ref[5, plane]


def load_kernel(near_plane, conf_hbm, conf_ref, early_ref, late_ref, sems):
    near = near_plane[0]
    copy = pltpu.make_async_copy(conf_hbm, conf_ref, sems.at[0])
    copy.start()
    copy.wait()
    divide(conf_ref, near, early_ref, late_ref)


def load(near_plane, conform):
    shape = conform.shape
    return pl.pallas_call(
        load_kernel,
        out_shape=(
            jax.ShapeDtypeStruct(shape, F32),
            jax.ShapeDtypeStruct((4,) + shape[2:], F32),
            jax.ShapeDtypeStruct((2,) + shape[2:], F32),
        ),
        in_specs=[pl.BlockSpec(memory_space=pltpu.SMEM), any_spec()],
        out_specs=(vmem_spec(),) * 3,
        scratch_shapes=[pltpu.SemaphoreType.DMA((1,))],
        compiler_params=params(),
        name="load",
    )(near_plane, conform)


def edge_kernel(conf_ref, up_ref, down_ref, up_tile, down_tile):
    height, width = conf_ref.shape[2:]

    def rows(start):
        at = pl.ds(start, ROWS)
        values = [conf_ref[f, p, at, :] for p in range(2) for f in range(6)]
        up_tile[at, :] = pack_columns(values, width - 1)
        down_tile[at, :] = pack_columns(values, 0)

    for_rows(height, rows)
    up_ref[...] = up_tile[...].T[0:COLUMNS]
    down_ref[...] = down_tile[...].T[0:COLUMNS]


def edges(conform):
    height, width = conform.shape[2:]
    out = jax.ShapeDtypeStruct((COLUMNS, height), F32)
    return pl.pallas_call(
        edge_kernel,
        out_shape=(out, out),
        in_specs=[vmem_spec()],
        out_specs=(vmem_spec(), vmem_spec()),
        scratch_shapes=[VMEM((height, width), F32)] * 2,
        compiler_params=params(),
        name="edges",
    )(conform)


def pick_kernel(far_plane, conf_ref, _, early_ref, late_ref):
    divide(conf_ref, far_plane[0], early_ref, late_ref)


def pick(far_plane, conform, after):
    shape = conform.shape
    return pl.pallas_call(
        pick_kernel,
        out_shape=(
            jax.ShapeDtypeStruct((4,) + shape[2:], F32),
            jax.ShapeDtypeStruct((2,) + shape[2:], F32),
        ),
        in_specs=[pl.BlockSpec(memory_space=pltpu.SMEM), vmem_spec(), any_spec()],
        out_specs=(vmem_spec(),) * 2,
        compiler_params=params(),
        name="pick",
    )(far_plane, conform, after)


def moments_kernel(popul_hbm, _, popul_ref, sums_ref, sems):
    height = popul_ref.shape[2]
    copies = []
    for p in range(2):
        copies.append(pltpu.make_async_copy(popul_hbm.at[:, p], popul_ref.at[:, p], sems.at[p]))
        copies[-1].start()
    for p in range(2):
        copies[p].wait()

        def rows(start, p=p):
            at = pl.ds(start, ROWS)
            values = [popul_ref[i, p, at, :] for i in range(19)]
            density = values[0]
            for i in range(1, 19):
                density = density + values[i]
            sums_ref[0, p, at, :] = density
            for axis in range(3):
                moment = None
                for i in range(19):
                    if VELOCITIES[i][axis] == 1:
                        moment = values[i] if moment is None else moment + values[i]
                for i in range(19):
                    if VELOCITIES[i][axis] == -1:
                        moment = moment - values[i]
                sums_ref[1 + axis, p, at, :] = moment

        for_rows(height, rows)


def moments(popul, after):
    return pl.pallas_call(
        moments_kernel,
        out_shape=(
            jax.ShapeDtypeStruct(popul.shape, F32),
            jax.ShapeDtypeStruct((4,) + popul.shape[1:], F32),
        ),
        in_specs=[any_spec(), any_spec()],
        out_specs=(vmem_spec(),) * 2,
        scratch_shapes=[pltpu.SemaphoreType.DMA((2,))],
        compiler_params=params(),
        name="moments",
    )(popul, after)


def prepare_kernel(conf_ref, low_cols, high_cols, pre_ref, tall, low_ref, high_ref):
    height, width = conf_ref.shape[2:]
    low_ref[...] = spread_columns(low_cols, width)
    high_ref[...] = spread_columns(high_cols, width)

    def stress(fields, at_of):
        trace_parts = [at_of(f) for f in range(3)]
        peterlin = STRESS_SCALE * peterlin_of(*trace_parts)
        out = {}
        for f in fields:
            value = trace_parts[f] if f < 3 else at_of(f)
            out[f] = peterlin * value - (STRESS_SCALE if f < 3 else 0.0)
        return out

    for p in range(2):
        sign = 2 * p - 1

        def first(start, p=p, sign=sign):
            at = pl.ds(start, ROWS)
            own = stress(range(6), lambda f: conf_ref[f, p, at, :])
            other = stress((0, 3, 4), lambda f: conf_ref[f, 1 - p, at, :])
            low_pack = low_ref[at, :]
            high_pack = high_ref[at, :]
            low = stress((2, 4, 5), lambda f: rolled(low_pack, -(6 * p + f)))
            high = stress((2, 4, 5), lambda f: rolled(high_pack, width - 1 - (6 * p + f)))
            lane = lanes_of(low_pack)
            for number, f in enumerate((3, 1, 5)):
                tall[number, p, pl.ds(start + 8, ROWS), :] = own[f]
            for number in range(3):
                across = SYMMETRIC_INDEX[number][2]
                below = jnp.where(lane == 0, low[across], rolled(own[across], 1))
                above = jnp.where(lane == width - 1, high[across], rolled(own[across], -1))
                term = 0.5 * (above - below) - (0.5 * sign) * other[SYMMETRIC_INDEX[number][0]]
                if number == 0:
                    term = term + DRIVE_FORCE
                pre_ref[number, p, at, :] = term

        for_rows(height, first)
        for number in range(3):
            tall[number, p, 7:8, :] = tall[number, p, 8:9, :]
            tall[number, p, height + 8 : height + 9, :] = tall[number, p, height + 7 : height + 8, :]

        def second(start, p=p):
            at = pl.ds(start, ROWS)
            for number in range(3):
                above = tall[number, p, pl.ds(start + 9, ROWS), :]
                below = tall[number, p, pl.ds(start + 7, ROWS), :]
                pre_ref[number, p, at, :] = pre_ref[number, p, at, :] + 0.5 * (above - below)

        for_rows(height, second)


def prepare(conform, low, high):
    height, width = conform.shape[2:]
    return pl.pallas_call(
        prepare_kernel,
        out_shape=jax.ShapeDtypeStruct((3, 2, height, width), F32),
        in_specs=[vmem_spec()] * 3,
        out_specs=vmem_spec(),
        scratch_shapes=[VMEM((3, 2, height + 16, width), F32)]
        + [VMEM((height, width), F32)] * 2,
        compiler_params=params(),
        name="prepare",
    )(conform, low, high)


def collide_kernel(second, plane_ref, popul_ref, sums_ref, pre_ref, halo_ref, *refs):
    if second:
        _, up_in, down_in, _, post_ref, message_ref, slant_ref, up_out, down_out, up_ref, down_ref = refs
    else:
        post_ref, message_ref, slant_ref, up_ref, down_ref = refs
    height, width = halo_ref.shape[1:]
    plane = plane_ref[0]
    outward_plus = plane == 1
    half_sign = jnp.where(outward_plus, 0.5, -0.5).astype(F32)
    factor = 1.0 - 0.5 / SOLVENT_TIME
    keep = 1.0 - 1.0 / SOLVENT_TIME
    base = 8 if second else 0

    def rows(start):
        at = pl.ds(start, ROWS)
        halo = [halo_ref[f, at, :] for f in range(4)]
        trace = halo[0] + halo[3]
        peterlin = (STRESS_SCALE * (EXTENSION_SQ - 3.0)) / (EXTENSION_SQ - trace)
        stress = (peterlin * halo[0] - STRESS_SCALE, peterlin * halo[1], peterlin * halo[2])
        force = [pre_ref[a, plane, at, :] + half_sign * stress[a] for a in range(3)]
        density = sums_ref[0, plane, at, :]
        inverse = 1.0 / density
        velocity = [(sums_ref[1 + a, plane, at, :] + 0.5 * force[a]) * inverse for a in range(3)]
        speed_sq = (
            velocity[0] * velocity[0] + velocity[1] * velocity[1] + velocity[2] * velocity[2]
        )
        push = velocity[0] * force[0] + velocity[1] * force[1] + velocity[2] * force[2]
        rate = density * (1.0 / SOLVENT_TIME)
        common = rate * (1.0 - 1.5 * speed_sq) - (3.0 * factor) * push
        flow = [rate * velocity[a] for a in range(3)]
        drag = [factor * force[a] for a in range(3)]
        post = [None] * 19
        post[0] = keep * popul_ref[0, plane, at, :] + LATTICE_WEIGHTS[0] * common

        def along(vec, parts):
            total = None
            for axis in range(3):
                if vec[axis] == 1:
                    total = parts[axis] if total is None else total + parts[axis]
                elif vec[axis] == -1:
                    total = total - parts[axis]
            return total

        for i in range(1, 19, 2):
            vec = VELOCITIES[i]
            weight = LATTICE_WEIGHTS[i]
            c_u = along(vec, velocity)
            c_flow = along(vec, flow)
            c_drag = along(vec, drag)
            total = c_flow + c_drag
            even = weight * common + (4.5 * weight) * (c_u * (total + c_drag))
            odd = (3.0 * weight) * total
            post[i] = keep * popul_ref[i, plane, at, :] + (even + odd)
            post[i + 1] = keep * popul_ref[i + 1, plane, at, :] + (even - odd)
        for i in range(19):
            post_ref[i, plane, at, :] = post[i]
        for a in range(3):
            message_ref[a, at, :] = velocity[a]
        for slot in range(5):
            out = message_ref.at[3 + slot] if slot < 3 else slant_ref.at[slot - 3]
            out[at, :] = jnp.where(outward_plus, post[PLUS[slot]], post[MINUS[slot]])
        up = up_in[at, :] if second else None
        down = down_in[at, :] if second else None
        up_ref[at, :] = pack_columns(
            velocity + [post[i] for i in Z_UP], width - 1, up, base
        )
        down_ref[at, :] = pack_columns(velocity + [post[i] for i in Z_DOWN], 0, down, base)

    for_rows(height, rows)
    if second:
        up_out[...] = up_ref[...].T[0:COLUMNS]
        down_out[...] = down_ref[...].T[0:COLUMNS]


def collide(plane, popul, sums, pre, halo, earlier=None):
    height, width = popul.shape[2:]
    second = earlier is not None
    tile = jax.ShapeDtypeStruct((COLUMNS, height) if second else (height, width), F32)
    operands = [plane, popul, sums, pre, halo] + (list(earlier) if second else [])
    return pl.pallas_call(
        functools.partial(collide_kernel, second),
        in_specs=[pl.BlockSpec(memory_space=pltpu.SMEM)]
        + [vmem_spec()] * 7
        + [any_spec()] * (len(operands) - 8)
        if second
        else [pl.BlockSpec(memory_space=pltpu.SMEM)] + [vmem_spec()] * 4,
        out_specs=(vmem_spec(),) * 5,
        out_shape=(
            jax.ShapeDtypeStruct(popul.shape, F32),
            jax.ShapeDtypeStruct((6, height, width), F32),
            jax.ShapeDtypeStruct((2, height, width), F32),
            tile,
            tile,
        ),
        scratch_shapes=[VMEM((height, width), F32)] * 2 if second else [],
        input_output_aliases={5: 0} if second else {},
        compiler_params=params(),
        name="collide_odd" if second else "collide_even",
    )(*operands)


def slant_kernel(plane_e, plane_o, low_ref, high_ref, slant_e, slant_o, even_ref, odd_ref):
    height, width = slant_e.shape[1:]
    lane = lax.broadcasted_iota(jnp.int32, (height, width), 1)
    faces = ((0, plane_e[0], slant_e, even_ref), (8, plane_o[0], slant_o, odd_ref))
    for base, plane, slant, out in faces:
        row = pl.ds(base + 7 - plane, 1)
        low = jnp.broadcast_to(low_ref[row, :], (width, height)).T
        high = jnp.broadcast_to(high_ref[row, :], (width, height)).T
        out[0] = jnp.where(lane == 0, low, rolled(slant[0], 1))
        out[1] = jnp.where(lane == width - 1, high, rolled(slant[1], -1))


def slants(plane_e, plane_o, low, high, slant_e, slant_o):
    out = jax.ShapeDtypeStruct(slant_e.shape, F32)
    smem = pl.BlockSpec(memory_space=pltpu.SMEM)
    return pl.pallas_call(
        slant_kernel,
        out_shape=(out, out),
        in_specs=[smem] * 2 + [vmem_spec()] * 4,
        out_specs=(vmem_spec(), vmem_spec()),
        compiler_params=params(),
        name="slants",
    )(plane_e, plane_o, low, high, slant_e, slant_o)


def inner_kernel(
    plane_e,
    plane_o,
    conf_ref,
    early_e,
    late_e,
    early_o,
    late_o,
    conf_low_cols,
    conf_high_cols,
    low_cols,
    high_cols,
    post_ref,
    velo_e,
    velo_o,
    read_ref,
    part_ref,
    conf_tall,
    velo_tall,
    halo,
    shifted,
    conf_low,
    conf_high,
    low_ref,
    high_ref,
    sems,
):
    height, width = conf_ref.shape[2:]
    conf_low[...] = spread_columns(conf_low_cols, width)
    conf_high[...] = spread_columns(conf_high_cols, width)
    low_ref[...] = spread_columns(low_cols, width)
    high_ref[...] = spread_columns(high_cols, width)
    planes = (plane_e[0], plane_o[0])
    for p, early, late in ((planes[0], early_e, late_e), (planes[1], early_o, late_o)):
        for number, f in enumerate((0, 3, 4)):
            halo[p, f] = early[number]
        halo[p, 1] = late[0]
        halo[p, 2] = early[3] - late[0]
        halo[p, 5] = late[1]
    for face, velo in enumerate((velo_e, velo_o)):
        p = planes[face]
        for a in range(3):
            velo_tall[a, p, 8 : 8 + height, :] = velo[a]
            velo_tall[a, p, 7:8, :] = -velo[a, 0:1, :]
            velo_tall[a, p, height + 8 : height + 9, :] = -velo[a, height - 1 : height, :]
    for p in range(2):
        for f in range(6):
            conf_tall[f, p, 8 : 8 + height, :] = conf_ref[f, p]
            conf_tall[f, p, 7:8, :] = conf_ref[f, p, 0:1, :]
            conf_tall[f, p, height + 8 : height + 9, :] = conf_ref[f, p, height - 1 : height, :]

    even_first = planes[0] == 0

    def lane_of(p, field):
        return (field, 8 + field) if p == 0 else (8 + field, field)

    def edge_value(pack, p, field, target):
        when_first, otherwise = lane_of(p, field)
        return jnp.where(
            even_first, rolled(pack, target - when_first), rolled(pack, target - otherwise)
        )

    copies = []
    full_low = low_ref[...]
    full_high = high_ref[...]
    lane = lanes_of(full_low)
    for i in range(19):
        step_x, step_y, step_z = VELOCITIES[i]
        for p in range(2):
            q = p - step_x
            if q not in (0, 1):
                continue
            tile = post_ref.at[i, q]
            if step_y or step_z:
                value = post_ref[i, q]
                if step_z == 1:
                    edge = edge_value(full_low, q, 3 + Z_UP.index(i), 0)
                    value = jnp.where(lane == 0, edge, rolled(value, 1))
                elif step_z == -1:
                    edge = edge_value(full_high, q, 3 + Z_DOWN.index(i), width - 1)
                    value = jnp.where(lane == width - 1, edge, rolled(value, -1))
                back = OPPOSITE[i]
                tile = shifted.at[i, p]
                if step_y == 1:
                    tile[1:height, :] = value[: height - 1]
                    tile[0:1, :] = post_ref[back, p, 0:1, :]
                elif step_y == -1:
                    tile[0 : height - 1, :] = value[1:]
                    tile[height - 1 : height, :] = post_ref[back, p, height - 1 : height, :]
                else:
                    tile[...] = value
            copies.append(pltpu.make_async_copy(tile, read_ref.at[i, p], sems.at[len(copies)]))
            copies[-1].start()

    for p in range(2):
        sign = 2 * p - 1

        def rows(start, p=p, sign=sign):
            at = pl.ds(start, ROWS)
            upper = pl.ds(start + 9, ROWS)
            lower = pl.ds(start + 7, ROWS)
            cl_pack = conf_low[at, :]
            ch_pack = conf_high[at, :]
            l_pack = low_ref[at, :]
            h_pack = high_ref[at, :]
            lane = lanes_of(cl_pack)
            first = lane == 0
            final = lane == width - 1
            velocity = [velo_tall[a, p, pl.ds(start + 8, ROWS), :] for a in range(3)]
            grad = [[None] * 3 for _ in range(3)]
            for a in range(3):
                grad[0][a] = (-0.5 * sign) * velo_tall[a, 1 - p, pl.ds(start + 8, ROWS), :]
                grad[1][a] = 0.5 * (velo_tall[a, p, upper, :] - velo_tall[a, p, lower, :])
                above = jnp.where(
                    final, edge_value(h_pack, p, a, width - 1), rolled(velocity[a], -1)
                )
                below = jnp.where(first, edge_value(l_pack, p, a, 0), rolled(velocity[a], 1))
                grad[2][a] = 0.5 * (above - below)
            own = [conf_ref[f, p, at, :] for f in range(6)]
            peterlin = (1.0 / RELAX_TIME) * peterlin_of(own[0], own[1], own[2])
            for f in range(6):
                i, j = COMPONENT_PAIRS[f]
                x_in = conf_ref[f, 1 - p, at, :]
                x_out = halo[p, f, at, :]
                y_up = conf_tall[f, p, upper, :]
                y_low = conf_tall[f, p, lower, :]
                lane_number = 6 * p + f
                z_up = jnp.where(
                    final, rolled(ch_pack, width - 1 - lane_number), rolled(own[f], -1)
                )
                z_low = jnp.where(first, rolled(cl_pack, -lane_number), rolled(own[f], 1))
                around = (x_in + x_out) + (y_up + y_low) + (z_up + z_low)
                advect = (
                    (sign * velocity[0]) * (x_out - x_in)
                    + velocity[1] * (y_up - y_low)
                    + velocity[2] * (z_up - z_low)
                )
                stretch = None
                for k in range(3):
                    term = own[SYMMETRIC_INDEX[i][k]] * grad[k][j]
                    if i != j:
                        term = term + grad[k][i] * own[SYMMETRIC_INDEX[k][j]]
                    stretch = term if stretch is None else stretch + term
                if i == j:
                    stretch = 2.0 * stretch
                relax = peterlin * own[f]
                if f < 3:
                    relax = relax - 1.0 / RELAX_TIME
                part_ref[f, p, at, :] = (
                    own[f]
                    - 0.5 * advect
                    + stretch
                    - relax
                    + DIFFUSIVITY * (around - 6.0 * own[f])
                )

        for_rows(height, rows)
    for copy in copies:
        copy.wait()


def inner(plane_e, plane_o, conform, halos, conf_low, conf_high, low, high, post, velo_e, velo_o):
    height, width = conform.shape[2:]
    velo_spec = pl.BlockSpec((3, height, width), lambda g: (0, 0, 0))
    whole = lambda shape: pl.BlockSpec(shape, lambda g: (0,) * len(shape))
    return pl.pallas_call(
        inner_kernel,
        grid=(1,),
        out_shape=(
            jax.ShapeDtypeStruct(post.shape, F32),
            jax.ShapeDtypeStruct(conform.shape, F32),
        ),
        in_specs=[
            pl.BlockSpec(memory_space=pltpu.SMEM),
            pl.BlockSpec(memory_space=pltpu.SMEM),
            whole(conform.shape),
            *[whole(halo.shape) for halo in halos],
            whole(conf_low.shape),
            whole(conf_low.shape),
            whole(conf_low.shape),
            whole(conf_low.shape),
            whole(post.shape),
            velo_spec,
            velo_spec,
        ],
        out_specs=(any_spec(), whole(conform.shape)),
        scratch_shapes=[
            VMEM((6, 2, height + 16, width), F32),
            VMEM((3, 2, height + 16, width), F32),
            VMEM((2, 6, height, width), F32),
            VMEM(post.shape, F32),
            VMEM((height, width), F32),
            VMEM((height, width), F32),
            VMEM((height, width), F32),
            VMEM((height, width), F32),
            pltpu.SemaphoreType.DMA((28,)),
        ],
        compiler_params=params(),
        name="inner",
    )(plane_e, plane_o, conform, *halos, conf_low, conf_high, low, high, post, velo_e, velo_o)


def touch_kernel(_, out_ref):
    out_ref[...] = jnp.zeros_like(out_ref)


def touch(value):
    return pl.pallas_call(
        touch_kernel,
        out_shape=jax.ShapeDtypeStruct((8, 128), F32),
        in_specs=[any_spec()],
        out_specs=vmem_spec(),
        compiler_params=params(),
        name="touch",
    )(value)


def targets_of(read_ref, plane):
    return [
        read_ref.at[jnp.where(plane == 1, MINUS[slot], PLUS[slot]), plane] for slot in range(5)
    ]


def finish_kernel(
    plane_e,
    plane_o,
    part_ref,
    conf_ref,
    got_e,
    sent_e,
    got_o,
    sent_o,
    _,
    __,
    read_ref,
    new_ref,
    read_tile,
    new_tile,
    sems,
):
    height = conf_ref.shape[2]
    faces = ((plane_o[0], got_o, sent_o), (plane_e[0], got_e, sent_e))
    copies = []

    def send(source, target):
        copies.append(pltpu.make_async_copy(source, target, sems.at[len(copies)]))
        copies[-1].start()

    for face, (plane, got, sent) in enumerate(faces):
        half_sign = jnp.where(plane == 1, 0.5, -0.5).astype(F32)
        tile = read_tile.at[face]
        targets = targets_of(read_ref, plane)
        send(got.at[3], targets[0])

        def rows(start, face=face, plane=plane, half_sign=half_sign, got=got):
            at = pl.ds(start, ROWS)
            slope = [half_sign * got[a, at, :] for a in range(3)]
            row = [conf_ref[f, plane, at, :] for f in (0, 3, 4)]
            for f in range(6):
                i, j = COMPONENT_PAIRS[f]
                if i == j:
                    term = 2.0 * (row[i] * slope[j])
                else:
                    term = row[i] * slope[j] + slope[i] * row[j]
                new_tile[face, f, at, :] = part_ref[f, plane, at, :] + term

        for_rows(height, rows)
        send(new_tile.at[face], new_ref.at[:, plane])
        tile[0, 1:height, :] = got[4, 0 : height - 1, :]
        tile[0, 0:1, :] = sent[5, 0:1, :]
        send(tile.at[0], targets[1])
        tile[1, 0 : height - 1, :] = got[5, 1:height, :]
        tile[1, height - 1 : height, :] = sent[4, height - 1 : height, :]
        send(tile.at[1], targets[2])
    for copy in copies:
        copy.wait()


def last_kernel(plane_e, plane_o, slant_e, slant_o, _, read_ref, sems):
    copies = []
    for plane, slant in ((plane_o[0], slant_o), (plane_e[0], slant_e)):
        targets = targets_of(read_ref, plane)
        for slot in (3, 4):
            copies.append(
                pltpu.make_async_copy(slant.at[slot - 3], targets[slot], sems.at[len(copies)])
            )
            copies[-1].start()
    for copy in copies:
        copy.wait()


def finish(plane_e, plane_o, part, conform, even, odd, slant_e, slant_o, read):
    height, width = conform.shape[2:]
    smem = pl.BlockSpec(memory_space=pltpu.SMEM)
    read_shape = jax.ShapeDtypeStruct(read.shape, F32)
    read, new = pl.pallas_call(
        finish_kernel,
        out_shape=(read_shape, jax.ShapeDtypeStruct(conform.shape, F32)),
        in_specs=[smem] * 2 + [vmem_spec()] * 6 + [any_spec()] * 2,
        out_specs=(any_spec(), any_spec()),
        scratch_shapes=[
            VMEM((2, 2, height, width), F32),
            VMEM((2, 6, height, width), F32),
            pltpu.SemaphoreType.DMA((8,)),
        ],
        input_output_aliases={8: 0},
        compiler_params=params(),
        name="finish",
    )(plane_e, plane_o, part, conform, *even, *odd, read, touch(even[0]))
    read = pl.pallas_call(
        last_kernel,
        out_shape=read_shape,
        in_specs=[smem] * 2 + [vmem_spec()] * 2 + [any_spec()],
        out_specs=any_spec(),
        scratch_shapes=[pltpu.SemaphoreType.DMA((4,))],
        input_output_aliases={4: 0},
        compiler_params=params(),
        name="last",
    )(plane_e, plane_o, slant_e, slant_o, read)
    return read, new


def body(popul, conform):
    wide = lax.axis_size("wide")
    narrow = lax.axis_size("narrow")
    odd = lax.rem(lax.axis_index("wide"), 2)
    plane_e = (1 - odd).astype(jnp.int32).reshape(1)
    plane_o = odd.astype(jnp.int32).reshape(1)
    even_pairs = [(i, i ^ 1) for i in range(wide)]
    odd_pairs = [(i, (i + 1) % wide if i % 2 else (i - 1) % wide) for i in range(wide)]
    up = [(i, (i + 1) % narrow) for i in range(narrow)]
    down = [(j, i) for i, j in up]

    conform, early, late = load(plane_e, conform)
    early_e = lax.ppermute(early, "wide", even_pairs)
    late_e = lax.ppermute(late, "wide", even_pairs)
    conf_up, conf_down = edges(conform)
    conf_low = lax.ppermute(conf_up, "narrow", up)
    conf_high = lax.ppermute(conf_down, "narrow", down)
    early, late = pick(plane_o, conform, conf_up)
    popul, sums = moments(popul, early)
    early_o = lax.ppermute(early, "wide", odd_pairs)
    late_o = lax.ppermute(late, "wide", odd_pairs)
    pre = prepare(conform, conf_low, conf_high)
    post, sent_e, slant_e, z_up, z_down = collide(plane_e, popul, sums, pre, early_e)
    got_e = lax.ppermute(sent_e, "wide", even_pairs)
    post, sent_o, slant_o, z_up, z_down = collide(
        plane_o, popul, sums, pre, early_o, (post, z_up, z_down, late_e)
    )
    got_o = lax.ppermute(sent_o, "wide", odd_pairs)
    low = lax.ppermute(z_up, "narrow", up)
    high = lax.ppermute(z_down, "narrow", down)
    slant_e, slant_o = slants(plane_e, plane_o, low, high, slant_e, slant_o)
    slant_e = lax.ppermute(slant_e, "wide", even_pairs)
    slant_o = lax.ppermute(slant_o, "wide", odd_pairs)
    read, part = inner(
        plane_e,
        plane_o,
        conform,
        (early_e, late_e, early_o, late_o),
        conf_low,
        conf_high,
        low,
        high,
        post,
        sent_e,
        sent_o,
    )
    even = (got_e, sent_e)
    odd = (got_o, sent_o)
    return finish(plane_e, plane_o, part, conform, even, odd, slant_e, slant_o, read)


def solution(mesh):
    placed = P(None, "wide", None, "narrow")
    return jax.shard_map(
        body, mesh=mesh, in_specs=(placed, placed), out_specs=(placed, placed), check_vma=False
    )
```

```python
import functools

import jax
import jax.numpy as jnp
from jax import lax
from jax.experimental import pallas as pl
from jax.experimental.pallas import tpu as pltpu
from jax.sharding import PartitionSpec as P

VELOCITIES = (
    (0, 0, 0),
    (1, 0, 0),
    (-1, 0, 0),
    (0, 1, 0),
    (0, -1, 0),
    (0, 0, 1),
    (0, 0, -1),
    (1, 1, 0),
    (-1, -1, 0),
    (1, -1, 0),
    (-1, 1, 0),
    (1, 0, 1),
    (-1, 0, -1),
    (1, 0, -1),
    (-1, 0, 1),
    (0, 1, 1),
    (0, -1, -1),
    (0, 1, -1),
    (0, -1, 1),
)
LATTICE_WEIGHTS = (1.0 / 3.0,) + (1.0 / 18.0,) * 6 + (1.0 / 36.0,) * 12
OPPOSITE = (0, 2, 1, 4, 3, 6, 5, 8, 7, 10, 9, 12, 11, 14, 13, 16, 15, 18, 17)
SYMMETRIC_INDEX = ((0, 3, 4), (3, 1, 5), (4, 5, 2))
COMPONENT_PAIRS = ((0, 0), (1, 1), (2, 2), (0, 1), (0, 2), (1, 2))
SOLVENT_TIME = 0.8
RELAX_TIME = 20.0
POLYMER_VISC = 1.0
EXTENSION_SQ = 100.0
DIFFUSIVITY = 0.05
DRIVE_FORCE = 1e-05
STRESS_SCALE = POLYMER_VISC / RELAX_TIME

SLOT_SHIFTS = ((0, 0), (1, 0), (-1, 0), (0, 1), (0, -1))
PLUS = tuple(VELOCITIES.index((1, cy, cz)) for cy, cz in SLOT_SHIFTS)
MINUS = tuple(VELOCITIES.index((-1, cy, cz)) for cy, cz in SLOT_SHIFTS)
Z_UP = tuple(VELOCITIES.index(v) for v in ((0, 0, 1), (0, 1, 1), (0, -1, 1), (1, 0, 1), (-1, 0, 1)))
Z_DOWN = tuple(
    VELOCITIES.index(v) for v in ((0, 0, -1), (0, 1, -1), (0, -1, -1), (1, 0, -1), (-1, 0, -1))
)
COLUMNS = 16
ROWS = 64
F32 = jnp.float32
VMEM = pltpu.VMEM


def vmem_spec():
    return pl.BlockSpec(memory_space=pltpu.VMEM)


def any_spec():
    return pl.BlockSpec(memory_space=pl.ANY)


def params():
    return pltpu.CompilerParams(vmem_limit_bytes=12 << 20)


def lanes_of(like):
    return lax.broadcasted_iota(jnp.int32, like.shape, 1)


def rolled(value, shift, axis=1):
    shift = shift % value.shape[axis]
    return value if shift == 0 else pltpu.roll(value, shift, axis)


def pack_columns(values, source, packed=None, base=0):
    lane = lanes_of(values[0])
    if packed is None:
        packed = jnp.zeros_like(values[0])
    for number, value in enumerate(values, base):
        packed = jnp.where(lane == number, rolled(value, number - source), packed)
    return packed


def spread_columns(ref, width):
    return jnp.concatenate([ref[...]] * (width // COLUMNS), axis=0).T


def for_rows(total, body):
    def step(number, carry):
        body(pl.multiple_of(number * ROWS, ROWS))
        return carry

    lax.fori_loop(0, total // ROWS, step, 0)


def peterlin_of(c_xx, c_yy, c_zz):
    return (EXTENSION_SQ - 3.0) / (EXTENSION_SQ - (c_xx + c_yy + c_zz))


def divide(conf_ref, plane, early_ref, late_ref):
    for number, f in enumerate((0, 3, 4)):
        early_ref[number] = conf_ref[f, plane]
    early_ref[3] = conf_ref[1, plane] + conf_ref[2, plane]
    late_ref[0] = conf_ref[1, plane]
    late_ref[1] = conf_ref[5, plane]


def load_kernel(near_plane, conf_hbm, conf_ref, early_ref, late_ref, sems):
    near = near_plane[0]
    copy = pltpu.make_async_copy(conf_hbm, conf_ref, sems.at[0])
    copy.start()
    copy.wait()
    divide(conf_ref, near, early_ref, late_ref)


def load(near_plane, conform):
    shape = conform.shape
    return pl.pallas_call(
        load_kernel,
        out_shape=(
            jax.ShapeDtypeStruct(shape, F32),
            jax.ShapeDtypeStruct((4,) + shape[2:], F32),
            jax.ShapeDtypeStruct((2,) + shape[2:], F32),
        ),
        in_specs=[pl.BlockSpec(memory_space=pltpu.SMEM), any_spec()],
        out_specs=(vmem_spec(),) * 3,
        scratch_shapes=[pltpu.SemaphoreType.DMA((1,))],
        compiler_params=params(),
        name="load",
    )(near_plane, conform)


def edge_kernel(conf_ref, up_ref, down_ref, up_tile, down_tile):
    height, width = conf_ref.shape[2:]

    def rows(start):
        at = pl.ds(start, ROWS)
        values = [conf_ref[f, p, at, :] for p in range(2) for f in range(6)]
        up_tile[at, :] = pack_columns(values, width - 1)
        down_tile[at, :] = pack_columns(values, 0)

    for_rows(height, rows)
    up_ref[...] = up_tile[...].T[0:COLUMNS]
    down_ref[...] = down_tile[...].T[0:COLUMNS]


def edges(conform):
    height, width = conform.shape[2:]
    out = jax.ShapeDtypeStruct((COLUMNS, height), F32)
    return pl.pallas_call(
        edge_kernel,
        out_shape=(out, out),
        in_specs=[vmem_spec()],
        out_specs=(vmem_spec(), vmem_spec()),
        scratch_shapes=[VMEM((height, width), F32)] * 2,
        compiler_params=params(),
        name="edges",
    )(conform)


def pick_kernel(far_plane, conf_ref, _, early_ref, late_ref):
    divide(conf_ref, far_plane[0], early_ref, late_ref)


def pick(far_plane, conform, after):
    shape = conform.shape
    return pl.pallas_call(
        pick_kernel,
        out_shape=(
            jax.ShapeDtypeStruct((4,) + shape[2:], F32),
            jax.ShapeDtypeStruct((2,) + shape[2:], F32),
        ),
        in_specs=[pl.BlockSpec(memory_space=pltpu.SMEM), vmem_spec(), any_spec()],
        out_specs=(vmem_spec(),) * 2,
        compiler_params=params(),
        name="pick",
    )(far_plane, conform, after)


def moments_kernel(popul_hbm, _, popul_ref, sums_ref, sems):
    height = popul_ref.shape[2]
    copies = []
    for p in range(2):
        copies.append(pltpu.make_async_copy(popul_hbm.at[:, p], popul_ref.at[:, p], sems.at[p]))
        copies[-1].start()
    for p in range(2):
        copies[p].wait()

        def rows(start, p=p):
            at = pl.ds(start, ROWS)
            values = [popul_ref[i, p, at, :] for i in range(19)]
            density = values[0]
            for i in range(1, 19):
                density = density + values[i]
            sums_ref[0, p, at, :] = density
            for axis in range(3):
                moment = None
                for i in range(19):
                    if VELOCITIES[i][axis] == 1:
                        moment = values[i] if moment is None else moment + values[i]
                for i in range(19):
                    if VELOCITIES[i][axis] == -1:
                        moment = moment - values[i]
                sums_ref[1 + axis, p, at, :] = moment

        for_rows(height, rows)


def moments(popul, after):
    return pl.pallas_call(
        moments_kernel,
        out_shape=(
            jax.ShapeDtypeStruct(popul.shape, F32),
            jax.ShapeDtypeStruct((4,) + popul.shape[1:], F32),
        ),
        in_specs=[any_spec(), any_spec()],
        out_specs=(vmem_spec(),) * 2,
        scratch_shapes=[pltpu.SemaphoreType.DMA((2,))],
        compiler_params=params(),
        name="moments",
    )(popul, after)


def prepare_kernel(conf_ref, low_cols, high_cols, pre_ref, tall, low_ref, high_ref):
    height, width = conf_ref.shape[2:]
    low_ref[...] = spread_columns(low_cols, width)
    high_ref[...] = spread_columns(high_cols, width)

    def stress(fields, at_of):
        trace_parts = [at_of(f) for f in range(3)]
        peterlin = STRESS_SCALE * peterlin_of(*trace_parts)
        out = {}
        for f in fields:
            value = trace_parts[f] if f < 3 else at_of(f)
            out[f] = peterlin * value - (STRESS_SCALE if f < 3 else 0.0)
        return out

    for p in range(2):
        sign = 2 * p - 1

        def first(start, p=p, sign=sign):
            at = pl.ds(start, ROWS)
            own = stress(range(6), lambda f: conf_ref[f, p, at, :])
            other = stress((0, 3, 4), lambda f: conf_ref[f, 1 - p, at, :])
            low_pack = low_ref[at, :]
            high_pack = high_ref[at, :]
            low = stress((2, 4, 5), lambda f: rolled(low_pack, -(6 * p + f)))
            high = stress((2, 4, 5), lambda f: rolled(high_pack, width - 1 - (6 * p + f)))
            lane = lanes_of(low_pack)
            for number, f in enumerate((3, 1, 5)):
                tall[number, p, pl.ds(start + 8, ROWS), :] = own[f]
            for number in range(3):
                across = SYMMETRIC_INDEX[number][2]
                below = jnp.where(lane == 0, low[across], rolled(own[across], 1))
                above = jnp.where(lane == width - 1, high[across], rolled(own[across], -1))
                term = 0.5 * (above - below) - (0.5 * sign) * other[SYMMETRIC_INDEX[number][0]]
                if number == 0:
                    term = term + DRIVE_FORCE
                pre_ref[number, p, at, :] = term

        for_rows(height, first)
        for number in range(3):
            tall[number, p, 7:8, :] = tall[number, p, 8:9, :]
            tall[number, p, height + 8 : height + 9, :] = tall[number, p, height + 7 : height + 8, :]

        def second(start, p=p):
            at = pl.ds(start, ROWS)
            for number in range(3):
                above = tall[number, p, pl.ds(start + 9, ROWS), :]
                below = tall[number, p, pl.ds(start + 7, ROWS), :]
                pre_ref[number, p, at, :] = pre_ref[number, p, at, :] + 0.5 * (above - below)

        for_rows(height, second)


def prepare(conform, low, high):
    height, width = conform.shape[2:]
    return pl.pallas_call(
        prepare_kernel,
        out_shape=jax.ShapeDtypeStruct((3, 2, height, width), F32),
        in_specs=[vmem_spec()] * 3,
        out_specs=vmem_spec(),
        scratch_shapes=[VMEM((3, 2, height + 16, width), F32)]
        + [VMEM((height, width), F32)] * 2,
        compiler_params=params(),
        name="prepare",
    )(conform, low, high)


def collide_kernel(second, plane_ref, popul_ref, sums_ref, pre_ref, halo_ref, *refs):
    if second:
        _, up_in, down_in, _, post_ref, message_ref, slant_ref, up_out, down_out, up_ref, down_ref = refs
    else:
        post_ref, message_ref, slant_ref, up_ref, down_ref = refs
    height, width = halo_ref.shape[1:]
    plane = plane_ref[0]
    outward_plus = plane == 1
    half_sign = jnp.where(outward_plus, 0.5, -0.5).astype(F32)
    factor = 1.0 - 0.5 / SOLVENT_TIME
    keep = 1.0 - 1.0 / SOLVENT_TIME
    base = 8 if second else 0

    def rows(start):
        at = pl.ds(start, ROWS)
        halo = [halo_ref[f, at, :] for f in range(4)]
        trace = halo[0] + halo[3]
        peterlin = (STRESS_SCALE * (EXTENSION_SQ - 3.0)) / (EXTENSION_SQ - trace)
        stress = (peterlin * halo[0] - STRESS_SCALE, peterlin * halo[1], peterlin * halo[2])
        force = [pre_ref[a, plane, at, :] + half_sign * stress[a] for a in range(3)]
        density = sums_ref[0, plane, at, :]
        inverse = 1.0 / density
        velocity = [(sums_ref[1 + a, plane, at, :] + 0.5 * force[a]) * inverse for a in range(3)]
        speed_sq = (
            velocity[0] * velocity[0] + velocity[1] * velocity[1] + velocity[2] * velocity[2]
        )
        push = velocity[0] * force[0] + velocity[1] * force[1] + velocity[2] * force[2]
        rate = density * (1.0 / SOLVENT_TIME)
        common = rate * (1.0 - 1.5 * speed_sq) - (3.0 * factor) * push
        flow = [rate * velocity[a] for a in range(3)]
        drag = [factor * force[a] for a in range(3)]
        post = [None] * 19
        post[0] = keep * popul_ref[0, plane, at, :] + LATTICE_WEIGHTS[0] * common

        def along(vec, parts):
            total = None
            for axis in range(3):
                if vec[axis] == 1:
                    total = parts[axis] if total is None else total + parts[axis]
                elif vec[axis] == -1:
                    total = total - parts[axis]
            return total

        for i in range(1, 19, 2):
            vec = VELOCITIES[i]
            weight = LATTICE_WEIGHTS[i]
            c_u = along(vec, velocity)
            c_flow = along(vec, flow)
            c_drag = along(vec, drag)
            total = c_flow + c_drag
            even = weight * common + (4.5 * weight) * (c_u * (total + c_drag))
            odd = (3.0 * weight) * total
            post[i] = keep * popul_ref[i, plane, at, :] + (even + odd)
            post[i + 1] = keep * popul_ref[i + 1, plane, at, :] + (even - odd)
        for i in range(19):
            post_ref[i, plane, at, :] = post[i]
        for a in range(3):
            message_ref[a, at, :] = velocity[a]
        for slot in range(5):
            out = message_ref.at[3 + slot] if slot < 3 else slant_ref.at[slot - 3]
            out[at, :] = jnp.where(outward_plus, post[PLUS[slot]], post[MINUS[slot]])
        up = up_in[at, :] if second else None
        down = down_in[at, :] if second else None
        up_ref[at, :] = pack_columns(
            velocity + [post[i] for i in Z_UP], width - 1, up, base
        )
        down_ref[at, :] = pack_columns(velocity + [post[i] for i in Z_DOWN], 0, down, base)

    for_rows(height, rows)
    if second:
        up_out[...] = up_ref[...].T[0:COLUMNS]
        down_out[...] = down_ref[...].T[0:COLUMNS]


def collide(plane, popul, sums, pre, halo, earlier=None):
    height, width = popul.shape[2:]
    second = earlier is not None
    tile = jax.ShapeDtypeStruct((COLUMNS, height) if second else (height, width), F32)
    operands = [plane, popul, sums, pre, halo] + (list(earlier) if second else [])
    return pl.pallas_call(
        functools.partial(collide_kernel, second),
        in_specs=[pl.BlockSpec(memory_space=pltpu.SMEM)]
        + [vmem_spec()] * 7
        + [any_spec()] * (len(operands) - 8)
        if second
        else [pl.BlockSpec(memory_space=pltpu.SMEM)] + [vmem_spec()] * 4,
        out_specs=(vmem_spec(),) * 5,
        out_shape=(
            jax.ShapeDtypeStruct(popul.shape, F32),
            jax.ShapeDtypeStruct((6, height, width), F32),
            jax.ShapeDtypeStruct((2, height, width), F32),
            tile,
            tile,
        ),
        scratch_shapes=[VMEM((height, width), F32)] * 2 if second else [],
        input_output_aliases={5: 0} if second else {},
        compiler_params=params(),
        name="collide_odd" if second else "collide_even",
    )(*operands)


def slant_kernel(plane_e, plane_o, low_ref, high_ref, slant_e, slant_o, even_ref, odd_ref):
    height, width = slant_e.shape[1:]
    lane = lax.broadcasted_iota(jnp.int32, (height, width), 1)
    faces = ((0, plane_e[0], slant_e, even_ref), (8, plane_o[0], slant_o, odd_ref))
    for base, plane, slant, out in faces:
        row = pl.ds(base + 7 - plane, 1)
        low = jnp.broadcast_to(low_ref[row, :], (width, height)).T
        high = jnp.broadcast_to(high_ref[row, :], (width, height)).T
        out[0] = jnp.where(lane == 0, low, rolled(slant[0], 1))
        out[1] = jnp.where(lane == width - 1, high, rolled(slant[1], -1))


def slants(plane_e, plane_o, low, high, slant_e, slant_o):
    out = jax.ShapeDtypeStruct(slant_e.shape, F32)
    smem = pl.BlockSpec(memory_space=pltpu.SMEM)
    return pl.pallas_call(
        slant_kernel,
        out_shape=(out, out),
        in_specs=[smem] * 2 + [vmem_spec()] * 4,
        out_specs=(vmem_spec(), vmem_spec()),
        compiler_params=params(),
        name="slants",
    )(plane_e, plane_o, low, high, slant_e, slant_o)


def inner_kernel(
    plane_e,
    plane_o,
    conf_ref,
    early_e,
    late_e,
    early_o,
    late_o,
    conf_low_cols,
    conf_high_cols,
    low_cols,
    high_cols,
    post_ref,
    velo_e,
    velo_o,
    read_ref,
    part_ref,
    conf_tall,
    velo_tall,
    halo,
    shifted,
    conf_low,
    conf_high,
    low_ref,
    high_ref,
    sems,
):
    height, width = conf_ref.shape[2:]
    conf_low[...] = spread_columns(conf_low_cols, width)
    conf_high[...] = spread_columns(conf_high_cols, width)
    low_ref[...] = spread_columns(low_cols, width)
    high_ref[...] = spread_columns(high_cols, width)
    planes = (plane_e[0], plane_o[0])
    for p, early, late in ((planes[0], early_e, late_e), (planes[1], early_o, late_o)):
        for number, f in enumerate((0, 3, 4)):
            halo[p, f] = early[number]
        halo[p, 1] = late[0]
        halo[p, 2] = early[3] - late[0]
        halo[p, 5] = late[1]
    for face, velo in enumerate((velo_e, velo_o)):
        p = planes[face]
        for a in range(3):
            velo_tall[a, p, 8 : 8 + height, :] = velo[a]
            velo_tall[a, p, 7:8, :] = -velo[a, 0:1, :]
            velo_tall[a, p, height + 8 : height + 9, :] = -velo[a, height - 1 : height, :]
    for p in range(2):
        for f in range(6):
            conf_tall[f, p, 8 : 8 + height, :] = conf_ref[f, p]
            conf_tall[f, p, 7:8, :] = conf_ref[f, p, 0:1, :]
            conf_tall[f, p, height + 8 : height + 9, :] = conf_ref[f, p, height - 1 : height, :]

    even_first = planes[0] == 0

    def lane_of(p, field):
        return (field, 8 + field) if p == 0 else (8 + field, field)

    def edge_value(pack, p, field, target):
        when_first, otherwise = lane_of(p, field)
        return jnp.where(
            even_first, rolled(pack, target - when_first), rolled(pack, target - otherwise)
        )

    copies = []
    full_low = low_ref[...]
    full_high = high_ref[...]
    lane = lanes_of(full_low)
    for i in range(19):
        step_x, step_y, step_z = VELOCITIES[i]
        for p in range(2):
            q = p - step_x
            if q not in (0, 1):
                continue
            tile = post_ref.at[i, q]
            if step_y or step_z:
                value = post_ref[i, q]
                if step_z == 1:
                    edge = edge_value(full_low, q, 3 + Z_UP.index(i), 0)
                    value = jnp.where(lane == 0, edge, rolled(value, 1))
                elif step_z == -1:
                    edge = edge_value(full_high, q, 3 + Z_DOWN.index(i), width - 1)
                    value = jnp.where(lane == width - 1, edge, rolled(value, -1))
                back = OPPOSITE[i]
                tile = shifted.at[i, p]
                if step_y == 1:
                    tile[1:height, :] = value[: height - 1]
                    tile[0:1, :] = post_ref[back, p, 0:1, :]
                elif step_y == -1:
                    tile[0 : height - 1, :] = value[1:]
                    tile[height - 1 : height, :] = post_ref[back, p, height - 1 : height, :]
                else:
                    tile[...] = value
            copies.append(pltpu.make_async_copy(tile, read_ref.at[i, p], sems.at[len(copies)]))
            copies[-1].start()

    for p in range(2):
        sign = 2 * p - 1

        def rows(start, p=p, sign=sign):
            at = pl.ds(start, ROWS)
            upper = pl.ds(start + 9, ROWS)
            lower = pl.ds(start + 7, ROWS)
            cl_pack = conf_low[at, :]
            ch_pack = conf_high[at, :]
            l_pack = low_ref[at, :]
            h_pack = high_ref[at, :]
            lane = lanes_of(cl_pack)
            first = lane == 0
            final = lane == width - 1
            velocity = [velo_tall[a, p, pl.ds(start + 8, ROWS), :] for a in range(3)]
            grad = [[None] * 3 for _ in range(3)]
            for a in range(3):
                grad[0][a] = (-0.5 * sign) * velo_tall[a, 1 - p, pl.ds(start + 8, ROWS), :]
                grad[1][a] = 0.5 * (velo_tall[a, p, upper, :] - velo_tall[a, p, lower, :])
                above = jnp.where(
                    final, edge_value(h_pack, p, a, width - 1), rolled(velocity[a], -1)
                )
                below = jnp.where(first, edge_value(l_pack, p, a, 0), rolled(velocity[a], 1))
                grad[2][a] = 0.5 * (above - below)
            own = [conf_ref[f, p, at, :] for f in range(6)]
            peterlin = (1.0 / RELAX_TIME) * peterlin_of(own[0], own[1], own[2])
            for f in range(6):
                i, j = COMPONENT_PAIRS[f]
                x_in = conf_ref[f, 1 - p, at, :]
                x_out = halo[p, f, at, :]
                y_up = conf_tall[f, p, upper, :]
                y_low = conf_tall[f, p, lower, :]
                lane_number = 6 * p + f
                z_up = jnp.where(
                    final, rolled(ch_pack, width - 1 - lane_number), rolled(own[f], -1)
                )
                z_low = jnp.where(first, rolled(cl_pack, -lane_number), rolled(own[f], 1))
                around = (x_in + x_out) + (y_up + y_low) + (z_up + z_low)
                advect = (
                    (sign * velocity[0]) * (x_out - x_in)
                    + velocity[1] * (y_up - y_low)
                    + velocity[2] * (z_up - z_low)
                )
                stretch = None
                for k in range(3):
                    term = own[SYMMETRIC_INDEX[i][k]] * grad[k][j]
                    if i != j:
                        term = term + grad[k][i] * own[SYMMETRIC_INDEX[k][j]]
                    stretch = term if stretch is None else stretch + term
                if i == j:
                    stretch = 2.0 * stretch
                relax = peterlin * own[f]
                if f < 3:
                    relax = relax - 1.0 / RELAX_TIME
                part_ref[f, p, at, :] = (
                    own[f]
                    - 0.5 * advect
                    + stretch
                    - relax
                    + DIFFUSIVITY * (around - 6.0 * own[f])
                )

        for_rows(height, rows)
    for copy in copies:
        copy.wait()


def inner(plane_e, plane_o, conform, halos, conf_low, conf_high, low, high, post, velo_e, velo_o):
    height, width = conform.shape[2:]
    velo_spec = pl.BlockSpec((3, height, width), lambda g: (0, 0, 0))
    whole = lambda shape: pl.BlockSpec(shape, lambda g: (0,) * len(shape))
    return pl.pallas_call(
        inner_kernel,
        grid=(1,),
        out_shape=(
            jax.ShapeDtypeStruct(post.shape, F32),
            jax.ShapeDtypeStruct(conform.shape, F32),
        ),
        in_specs=[
            pl.BlockSpec(memory_space=pltpu.SMEM),
            pl.BlockSpec(memory_space=pltpu.SMEM),
            whole(conform.shape),
            *[whole(halo.shape) for halo in halos],
            whole(conf_low.shape),
            whole(conf_low.shape),
            whole(conf_low.shape),
            whole(conf_low.shape),
            whole(post.shape),
            velo_spec,
            velo_spec,
        ],
        out_specs=(any_spec(), whole(conform.shape)),
        scratch_shapes=[
            VMEM((6, 2, height + 16, width), F32),
            VMEM((3, 2, height + 16, width), F32),
            VMEM((2, 6, height, width), F32),
            VMEM(post.shape, F32),
            VMEM((height, width), F32),
            VMEM((height, width), F32),
            VMEM((height, width), F32),
            VMEM((height, width), F32),
            pltpu.SemaphoreType.DMA((28,)),
        ],
        compiler_params=params(),
        name="inner",
    )(plane_e, plane_o, conform, *halos, conf_low, conf_high, low, high, post, velo_e, velo_o)


def touch_kernel(_, out_ref):
    out_ref[...] = jnp.zeros_like(out_ref)


def touch(value):
    return pl.pallas_call(
        touch_kernel,
        out_shape=jax.ShapeDtypeStruct((8, 128), F32),
        in_specs=[any_spec()],
        out_specs=vmem_spec(),
        compiler_params=params(),
        name="touch",
    )(value)


def targets_of(read_ref, plane):
    return [
        read_ref.at[jnp.where(plane == 1, MINUS[slot], PLUS[slot]), plane] for slot in range(5)
    ]


def finish_kernel(
    plane_e,
    plane_o,
    part_ref,
    conf_ref,
    got_e,
    sent_e,
    got_o,
    sent_o,
    _,
    __,
    read_ref,
    new_ref,
    read_tile,
    new_tile,
    sems,
):
    height = conf_ref.shape[2]
    faces = ((plane_o[0], got_o, sent_o), (plane_e[0], got_e, sent_e))
    copies = []

    def send(source, target):
        copies.append(pltpu.make_async_copy(source, target, sems.at[len(copies)]))
        copies[-1].start()

    for face, (plane, got, sent) in enumerate(faces):
        half_sign = jnp.where(plane == 1, 0.5, -0.5).astype(F32)
        tile = read_tile.at[face]
        targets = targets_of(read_ref, plane)
        send(got.at[3], targets[0])

        def rows(start, face=face, plane=plane, half_sign=half_sign, got=got):
            at = pl.ds(start, ROWS)
            slope = [half_sign * got[a, at, :] for a in range(3)]
            row = [conf_ref[f, plane, at, :] for f in (0, 3, 4)]
            for f in range(6):
                i, j = COMPONENT_PAIRS[f]
                if i == j:
                    term = 2.0 * (row[i] * slope[j])
                else:
                    term = row[i] * slope[j] + slope[i] * row[j]
                new_tile[face, f, at, :] = part_ref[f, plane, at, :] + term

        for_rows(height, rows)
        send(new_tile.at[face], new_ref.at[:, plane])
        tile[0, 1:height, :] = got[4, 0 : height - 1, :]
        tile[0, 0:1, :] = sent[5, 0:1, :]
        send(tile.at[0], targets[1])
        tile[1, 0 : height - 1, :] = got[5, 1:height, :]
        tile[1, height - 1 : height, :] = sent[4, height - 1 : height, :]
        send(tile.at[1], targets[2])
    for copy in copies:
        copy.wait()


def last_kernel(plane_e, plane_o, slant_e, slant_o, _, read_ref, sems):
    copies = []
    for plane, slant in ((plane_o[0], slant_o), (plane_e[0], slant_e)):
        targets = targets_of(read_ref, plane)
        for slot in (3, 4):
            copies.append(
                pltpu.make_async_copy(slant.at[slot - 3], targets[slot], sems.at[len(copies)])
            )
            copies[-1].start()
    for copy in copies:
        copy.wait()


def finish(plane_e, plane_o, part, conform, even, odd, slant_e, slant_o, read):
    height, width = conform.shape[2:]
    smem = pl.BlockSpec(memory_space=pltpu.SMEM)
    read_shape = jax.ShapeDtypeStruct(read.shape, F32)
    read, new = pl.pallas_call(
        finish_kernel,
        out_shape=(read_shape, jax.ShapeDtypeStruct(conform.shape, F32)),
        in_specs=[smem] * 2 + [vmem_spec()] * 6 + [any_spec()] * 2,
        out_specs=(any_spec(), any_spec()),
        scratch_shapes=[
            VMEM((2, 2, height, width), F32),
            VMEM((2, 6, height, width), F32),
            pltpu.SemaphoreType.DMA((8,)),
        ],
        input_output_aliases={8: 0},
        compiler_params=params(),
        name="finish",
    )(plane_e, plane_o, part, conform, *even, *odd, read, touch(even[0]))
    read = pl.pallas_call(
        last_kernel,
        out_shape=read_shape,
        in_specs=[smem] * 2 + [vmem_spec()] * 2 + [any_spec()],
        out_specs=any_spec(),
        scratch_shapes=[pltpu.SemaphoreType.DMA((4,))],
        input_output_aliases={4: 0},
        compiler_params=params(),
        name="last",
    )(plane_e, plane_o, slant_e, slant_o, read)
    return read, new


def body(popul, conform):
    wide = lax.axis_size("wide")
    narrow = lax.axis_size("narrow")
    odd = lax.rem(lax.axis_index("wide"), 2)
    plane_e = (1 - odd).astype(jnp.int32).reshape(1)
    plane_o = odd.astype(jnp.int32).reshape(1)
    even_pairs = [(i, i ^ 1) for i in range(wide)]
    odd_pairs = [(i, (i + 1) % wide if i % 2 else (i - 1) % wide) for i in range(wide)]
    up = [(i, (i + 1) % narrow) for i in range(narrow)]
    down = [(j, i) for i, j in up]

    conform, early, late = load(plane_e, conform)
    early_e = lax.ppermute(early, "wide", even_pairs)
    late_e = lax.ppermute(late, "wide", even_pairs)
    conf_up, conf_down = edges(conform)
    conf_low = lax.ppermute(conf_up, "narrow", up)
    conf_high = lax.ppermute(conf_down, "narrow", down)
    early, late = pick(plane_o, conform, conf_up)
    popul, sums = moments(popul, early)
    early_o = lax.ppermute(early, "wide", odd_pairs)
    late_o = lax.ppermute(late, "wide", odd_pairs)
    pre = prepare(conform, conf_low, conf_high)
    post, sent_e, slant_e, z_up, z_down = collide(plane_e, popul, sums, pre, early_e)
    got_e = lax.ppermute(sent_e, "wide", even_pairs)
    post, sent_o, slant_o, z_up, z_down = collide(
        plane_o, popul, sums, pre, early_o, (post, z_up, z_down, late_e)
    )
    got_o = lax.ppermute(sent_o, "wide", odd_pairs)
    low = lax.ppermute(z_up, "narrow", up)
    high = lax.ppermute(z_down, "narrow", down)
    slant_e, slant_o = slants(plane_e, plane_o, low, high, slant_e, slant_o)
    slant_e = lax.ppermute(slant_e, "wide", even_pairs)
    slant_o = lax.ppermute(slant_o, "wide", odd_pairs)
    read, part = inner(
        plane_e,
        plane_o,
        conform,
        (early_e, late_e, early_o, late_o),
        conf_low,
        conf_high,
        low,
        high,
        post,
        sent_e,
        sent_o,
    )
    even = (got_e, sent_e)
    odd = (got_o, sent_o)
    return finish(plane_e, plane_o, part, conform, even, odd, slant_e, slant_o, read)


def solution(mesh):
    placed = P(None, "wide", None, "narrow")
    return jax.shard_map(
        body, mesh=mesh, in_specs=(placed, placed), out_specs=(placed, placed), check_vma=False
    )
```

```python
import functools

import jax
import jax.numpy as jnp
from jax import lax
from jax.experimental import pallas as pl
from jax.experimental.pallas import tpu as pltpu
from jax.sharding import PartitionSpec as P

VELOCITIES = (
    (0, 0, 0),
    (1, 0, 0),
    (-1, 0, 0),
    (0, 1, 0),
    (0, -1, 0),
    (0, 0, 1),
    (0, 0, -1),
    (1, 1, 0),
    (-1, -1, 0),
    (1, -1, 0),
    (-1, 1, 0),
    (1, 0, 1),
    (-1, 0, -1),
    (1, 0, -1),
    (-1, 0, 1),
    (0, 1, 1),
    (0, -1, -1),
    (0, 1, -1),
    (0, -1, 1),
)
LATTICE_WEIGHTS = (1.0 / 3.0,) + (1.0 / 18.0,) * 6 + (1.0 / 36.0,) * 12
OPPOSITE = (0, 2, 1, 4, 3, 6, 5, 8, 7, 10, 9, 12, 11, 14, 13, 16, 15, 18, 17)
SYMMETRIC_INDEX = ((0, 3, 4), (3, 1, 5), (4, 5, 2))
COMPONENT_PAIRS = ((0, 0), (1, 1), (2, 2), (0, 1), (0, 2), (1, 2))
SOLVENT_TIME = 0.8
RELAX_TIME = 20.0
POLYMER_VISC = 1.0
EXTENSION_SQ = 100.0
DIFFUSIVITY = 0.05
DRIVE_FORCE = 1e-05
STRESS_SCALE = POLYMER_VISC / RELAX_TIME

SLOT_SHIFTS = ((0, 0), (1, 0), (-1, 0), (0, 1), (0, -1))
PLUS = tuple(VELOCITIES.index((1, cy, cz)) for cy, cz in SLOT_SHIFTS)
MINUS = tuple(VELOCITIES.index((-1, cy, cz)) for cy, cz in SLOT_SHIFTS)
Z_UP = tuple(VELOCITIES.index(v) for v in ((0, 0, 1), (0, 1, 1), (0, -1, 1), (1, 0, 1), (-1, 0, 1)))
Z_DOWN = tuple(
    VELOCITIES.index(v) for v in ((0, 0, -1), (0, 1, -1), (0, -1, -1), (1, 0, -1), (-1, 0, -1))
)
COLUMNS = 16
ROWS = 128
F32 = jnp.float32
VMEM = pltpu.VMEM


def vmem_spec():
    return pl.BlockSpec(memory_space=pltpu.VMEM)


def any_spec():
    return pl.BlockSpec(memory_space=pl.ANY)


def params():
    return pltpu.CompilerParams(vmem_limit_bytes=12 << 20)


def lanes_of(like):
    return lax.broadcasted_iota(jnp.int32, like.shape, 1)


def rolled(value, shift, axis=1):
    shift = shift % value.shape[axis]
    return value if shift == 0 else pltpu.roll(value, shift, axis)


def pack_columns(values, source, packed=None, base=0):
    lane = lanes_of(values[0])
    if packed is None:
        packed = jnp.zeros_like(values[0])
    for number, value in enumerate(values, base):
        packed = jnp.where(lane == number, rolled(value, number - source), packed)
    return packed


def spread_columns(ref, width):
    return jnp.concatenate([ref[...]] * (width // COLUMNS), axis=0).T


def for_rows(total, body):
    def step(number, carry):
        body(pl.multiple_of(number * ROWS, ROWS))
        return carry

    lax.fori_loop(0, total // ROWS, step, 0)


def peterlin_of(c_xx, c_yy, c_zz):
    return (EXTENSION_SQ - 3.0) / (EXTENSION_SQ - (c_xx + c_yy + c_zz))


def divide(conf_ref, plane, early_ref, late_ref):
    for number, f in enumerate((0, 3, 4)):
        early_ref[number] = conf_ref[f, plane]
    early_ref[3] = conf_ref[1, plane] + conf_ref[2, plane]
    late_ref[0] = conf_ref[1, plane]
    late_ref[1] = conf_ref[5, plane]


def load_kernel(near_plane, conf_hbm, conf_ref, early_ref, late_ref, sems):
    near = near_plane[0]
    copy = pltpu.make_async_copy(conf_hbm, conf_ref, sems.at[0])
    copy.start()
    copy.wait()
    divide(conf_ref, near, early_ref, late_ref)


def load(near_plane, conform):
    shape = conform.shape
    return pl.pallas_call(
        load_kernel,
        out_shape=(
            jax.ShapeDtypeStruct(shape, F32),
            jax.ShapeDtypeStruct((4,) + shape[2:], F32),
            jax.ShapeDtypeStruct((2,) + shape[2:], F32),
        ),
        in_specs=[pl.BlockSpec(memory_space=pltpu.SMEM), any_spec()],
        out_specs=(vmem_spec(),) * 3,
        scratch_shapes=[pltpu.SemaphoreType.DMA((1,))],
        compiler_params=params(),
        name="load",
    )(near_plane, conform)


def edge_kernel(conf_ref, up_ref, down_ref, up_tile, down_tile):
    height, width = conf_ref.shape[2:]

    def rows(start):
        at = pl.ds(start, ROWS)
        values = [conf_ref[f, p, at, :] for p in range(2) for f in range(6)]
        up_tile[at, :] = pack_columns(values, width - 1)
        down_tile[at, :] = pack_columns(values, 0)

    for_rows(height, rows)
    up_ref[...] = up_tile[...].T[0:COLUMNS]
    down_ref[...] = down_tile[...].T[0:COLUMNS]


def edges(conform):
    height, width = conform.shape[2:]
    out = jax.ShapeDtypeStruct((COLUMNS, height), F32)
    return pl.pallas_call(
        edge_kernel,
        out_shape=(out, out),
        in_specs=[vmem_spec()],
        out_specs=(vmem_spec(), vmem_spec()),
        scratch_shapes=[VMEM((height, width), F32)] * 2,
        compiler_params=params(),
        name="edges",
    )(conform)


def pick_kernel(far_plane, conf_ref, _, early_ref, late_ref):
    divide(conf_ref, far_plane[0], early_ref, late_ref)


def pick(far_plane, conform, after):
    shape = conform.shape
    return pl.pallas_call(
        pick_kernel,
        out_shape=(
            jax.ShapeDtypeStruct((4,) + shape[2:], F32),
            jax.ShapeDtypeStruct((2,) + shape[2:], F32),
        ),
        in_specs=[pl.BlockSpec(memory_space=pltpu.SMEM), vmem_spec(), any_spec()],
        out_specs=(vmem_spec(),) * 2,
        compiler_params=params(),
        name="pick",
    )(far_plane, conform, after)


def moments_kernel(popul_hbm, _, popul_ref, sums_ref, sems):
    height = popul_ref.shape[2]
    copies = []
    for p in range(2):
        copies.append(pltpu.make_async_copy(popul_hbm.at[:, p], popul_ref.at[:, p], sems.at[p]))
        copies[-1].start()
    for p in range(2):
        copies[p].wait()

        def rows(start, p=p):
            at = pl.ds(start, ROWS)
            values = [popul_ref[i, p, at, :] for i in range(19)]
            density = values[0]
            for i in range(1, 19):
                density = density + values[i]
            sums_ref[0, p, at, :] = density
            for axis in range(3):
                moment = None
                for i in range(19):
                    if VELOCITIES[i][axis] == 1:
                        moment = values[i] if moment is None else moment + values[i]
                for i in range(19):
                    if VELOCITIES[i][axis] == -1:
                        moment = moment - values[i]
                sums_ref[1 + axis, p, at, :] = moment

        for_rows(height, rows)


def moments(popul, after):
    return pl.pallas_call(
        moments_kernel,
        out_shape=(
            jax.ShapeDtypeStruct(popul.shape, F32),
            jax.ShapeDtypeStruct((4,) + popul.shape[1:], F32),
        ),
        in_specs=[any_spec(), any_spec()],
        out_specs=(vmem_spec(),) * 2,
        scratch_shapes=[pltpu.SemaphoreType.DMA((2,))],
        compiler_params=params(),
        name="moments",
    )(popul, after)


def prepare_kernel(conf_ref, low_cols, high_cols, pre_ref, tall, low_ref, high_ref):
    height, width = conf_ref.shape[2:]
    low_ref[...] = spread_columns(low_cols, width)
    high_ref[...] = spread_columns(high_cols, width)

    def stress(fields, at_of):
        trace_parts = [at_of(f) for f in range(3)]
        peterlin = STRESS_SCALE * peterlin_of(*trace_parts)
        out = {}
        for f in fields:
            value = trace_parts[f] if f < 3 else at_of(f)
            out[f] = peterlin * value - (STRESS_SCALE if f < 3 else 0.0)
        return out

    for p in range(2):
        sign = 2 * p - 1

        def first(start, p=p, sign=sign):
            at = pl.ds(start, ROWS)
            own = stress(range(6), lambda f: conf_ref[f, p, at, :])
            other = stress((0, 3, 4), lambda f: conf_ref[f, 1 - p, at, :])
            low_pack = low_ref[at, :]
            high_pack = high_ref[at, :]
            low = stress((2, 4, 5), lambda f: rolled(low_pack, -(6 * p + f)))
            high = stress((2, 4, 5), lambda f: rolled(high_pack, width - 1 - (6 * p + f)))
            lane = lanes_of(low_pack)
            for number, f in enumerate((3, 1, 5)):
                tall[number, p, pl.ds(start + 8, ROWS), :] = own[f]
            for number in range(3):
                across = SYMMETRIC_INDEX[number][2]
                below = jnp.where(lane == 0, low[across], rolled(own[across], 1))
                above = jnp.where(lane == width - 1, high[across], rolled(own[across], -1))
                term = 0.5 * (above - below) - (0.5 * sign) * other[SYMMETRIC_INDEX[number][0]]
                if number == 0:
                    term = term + DRIVE_FORCE
                pre_ref[number, p, at, :] = term

        for_rows(height, first)
        for number in range(3):
            tall[number, p, 7:8, :] = tall[number, p, 8:9, :]
            tall[number, p, height + 8 : height + 9, :] = tall[number, p, height + 7 : height + 8, :]

        def second(start, p=p):
            at = pl.ds(start, ROWS)
            for number in range(3):
                above = tall[number, p, pl.ds(start + 9, ROWS), :]
                below = tall[number, p, pl.ds(start + 7, ROWS), :]
                pre_ref[number, p, at, :] = pre_ref[number, p, at, :] + 0.5 * (above - below)

        for_rows(height, second)


def prepare(conform, low, high):
    height, width = conform.shape[2:]
    return pl.pallas_call(
        prepare_kernel,
        out_shape=jax.ShapeDtypeStruct((3, 2, height, width), F32),
        in_specs=[vmem_spec()] * 3,
        out_specs=vmem_spec(),
        scratch_shapes=[VMEM((3, 2, height + 16, width), F32)]
        + [VMEM((height, width), F32)] * 2,
        compiler_params=params(),
        name="prepare",
    )(conform, low, high)


def collide_kernel(second, plane_ref, popul_ref, sums_ref, pre_ref, halo_ref, *refs):
    if second:
        _, up_in, down_in, _, post_ref, message_ref, slant_ref, up_out, down_out, up_ref, down_ref = refs
    else:
        post_ref, message_ref, slant_ref, up_ref, down_ref = refs
    height, width = halo_ref.shape[1:]
    plane = plane_ref[0]
    outward_plus = plane == 1
    half_sign = jnp.where(outward_plus, 0.5, -0.5).astype(F32)
    factor = 1.0 - 0.5 / SOLVENT_TIME
    keep = 1.0 - 1.0 / SOLVENT_TIME
    base = 8 if second else 0

    def rows(start):
        at = pl.ds(start, ROWS)
        halo = [halo_ref[f, at, :] for f in range(4)]
        trace = halo[0] + halo[3]
        peterlin = (STRESS_SCALE * (EXTENSION_SQ - 3.0)) / (EXTENSION_SQ - trace)
        stress = (peterlin * halo[0] - STRESS_SCALE, peterlin * halo[1], peterlin * halo[2])
        force = [pre_ref[a, plane, at, :] + half_sign * stress[a] for a in range(3)]
        density = sums_ref[0, plane, at, :]
        inverse = 1.0 / density
        velocity = [(sums_ref[1 + a, plane, at, :] + 0.5 * force[a]) * inverse for a in range(3)]
        speed_sq = (
            velocity[0] * velocity[0] + velocity[1] * velocity[1] + velocity[2] * velocity[2]
        )
        push = velocity[0] * force[0] + velocity[1] * force[1] + velocity[2] * force[2]
        rate = density * (1.0 / SOLVENT_TIME)
        common = rate * (1.0 - 1.5 * speed_sq) - (3.0 * factor) * push
        flow = [rate * velocity[a] for a in range(3)]
        drag = [factor * force[a] for a in range(3)]
        post = [None] * 19
        post[0] = keep * popul_ref[0, plane, at, :] + LATTICE_WEIGHTS[0] * common

        def along(vec, parts):
            total = None
            for axis in range(3):
                if vec[axis] == 1:
                    total = parts[axis] if total is None else total + parts[axis]
                elif vec[axis] == -1:
                    total = total - parts[axis]
            return total

        for i in range(1, 19, 2):
            vec = VELOCITIES[i]
            weight = LATTICE_WEIGHTS[i]
            c_u = along(vec, velocity)
            c_flow = along(vec, flow)
            c_drag = along(vec, drag)
            total = c_flow + c_drag
            even = weight * common + (4.5 * weight) * (c_u * (total + c_drag))
            odd = (3.0 * weight) * total
            post[i] = keep * popul_ref[i, plane, at, :] + (even + odd)
            post[i + 1] = keep * popul_ref[i + 1, plane, at, :] + (even - odd)
        for i in range(19):
            post_ref[i, plane, at, :] = post[i]
        for a in range(3):
            message_ref[a, at, :] = velocity[a]
        for slot in range(5):
            out = message_ref.at[3 + slot] if slot < 3 else slant_ref.at[slot - 3]
            out[at, :] = jnp.where(outward_plus, post[PLUS[slot]], post[MINUS[slot]])
        up = up_in[at, :] if second else None
        down = down_in[at, :] if second else None
        up_ref[at, :] = pack_columns(
            velocity + [post[i] for i in Z_UP], width - 1, up, base
        )
        down_ref[at, :] = pack_columns(velocity + [post[i] for i in Z_DOWN], 0, down, base)

    for_rows(height, rows)
    if second:
        up_out[...] = up_ref[...].T[0:COLUMNS]
        down_out[...] = down_ref[...].T[0:COLUMNS]


def collide(plane, popul, sums, pre, halo, earlier=None):
    height, width = popul.shape[2:]
    second = earlier is not None
    tile = jax.ShapeDtypeStruct((COLUMNS, height) if second else (height, width), F32)
    operands = [plane, popul, sums, pre, halo] + (list(earlier) if second else [])
    return pl.pallas_call(
        functools.partial(collide_kernel, second),
        in_specs=[pl.BlockSpec(memory_space=pltpu.SMEM)]
        + [vmem_spec()] * 7
        + [any_spec()] * (len(operands) - 8)
        if second
        else [pl.BlockSpec(memory_space=pltpu.SMEM)] + [vmem_spec()] * 4,
        out_specs=(vmem_spec(),) * 5,
        out_shape=(
            jax.ShapeDtypeStruct(popul.shape, F32),
            jax.ShapeDtypeStruct((6, height, width), F32),
            jax.ShapeDtypeStruct((2, height, width), F32),
            tile,
            tile,
        ),
        scratch_shapes=[VMEM((height, width), F32)] * 2 if second else [],
        input_output_aliases={5: 0} if second else {},
        compiler_params=params(),
        name="collide_odd" if second else "collide_even",
    )(*operands)


def slant_kernel(plane_e, plane_o, low_ref, high_ref, slant_e, slant_o, even_ref, odd_ref):
    height, width = slant_e.shape[1:]
    lane = lax.broadcasted_iota(jnp.int32, (height, width), 1)
    faces = ((0, plane_e[0], slant_e, even_ref), (8, plane_o[0], slant_o, odd_ref))
    for base, plane, slant, out in faces:
        row = pl.ds(base + 7 - plane, 1)
        low = jnp.broadcast_to(low_ref[row, :], (width, height)).T
        high = jnp.broadcast_to(high_ref[row, :], (width, height)).T
        out[0] = jnp.where(lane == 0, low, rolled(slant[0], 1))
        out[1] = jnp.where(lane == width - 1, high, rolled(slant[1], -1))


def slants(plane_e, plane_o, low, high, slant_e, slant_o):
    out = jax.ShapeDtypeStruct(slant_e.shape, F32)
    smem = pl.BlockSpec(memory_space=pltpu.SMEM)
    return pl.pallas_call(
        slant_kernel,
        out_shape=(out, out),
        in_specs=[smem] * 2 + [vmem_spec()] * 4,
        out_specs=(vmem_spec(), vmem_spec()),
        compiler_params=params(),
        name="slants",
    )(plane_e, plane_o, low, high, slant_e, slant_o)


def inner_kernel(
    plane_e,
    plane_o,
    conf_ref,
    early_e,
    late_e,
    early_o,
    late_o,
    conf_low_cols,
    conf_high_cols,
    low_cols,
    high_cols,
    post_ref,
    velo_e,
    velo_o,
    read_ref,
    part_ref,
    conf_tall,
    velo_tall,
    halo,
    shifted,
    conf_low,
    conf_high,
    low_ref,
    high_ref,
    sems,
):
    height, width = conf_ref.shape[2:]
    conf_low[...] = spread_columns(conf_low_cols, width)
    conf_high[...] = spread_columns(conf_high_cols, width)
    low_ref[...] = spread_columns(low_cols, width)
    high_ref[...] = spread_columns(high_cols, width)
    planes = (plane_e[0], plane_o[0])
    for p, early, late in ((planes[0], early_e, late_e), (planes[1], early_o, late_o)):
        for number, f in enumerate((0, 3, 4)):
            halo[p, f] = early[number]
        halo[p, 1] = late[0]
        halo[p, 2] = early[3] - late[0]
        halo[p, 5] = late[1]
    for face, velo in enumerate((velo_e, velo_o)):
        p = planes[face]
        for a in range(3):
            velo_tall[a, p, 8 : 8 + height, :] = velo[a]
            velo_tall[a, p, 7:8, :] = -velo[a, 0:1, :]
            velo_tall[a, p, height + 8 : height + 9, :] = -velo[a, height - 1 : height, :]
    for p in range(2):
        for f in range(6):
            conf_tall[f, p, 8 : 8 + height, :] = conf_ref[f, p]
            conf_tall[f, p, 7:8, :] = conf_ref[f, p, 0:1, :]
            conf_tall[f, p, height + 8 : height + 9, :] = conf_ref[f, p, height - 1 : height, :]

    even_first = planes[0] == 0

    def lane_of(p, field):
        return (field, 8 + field) if p == 0 else (8 + field, field)

    def edge_value(pack, p, field, target):
        when_first, otherwise = lane_of(p, field)
        return jnp.where(
            even_first, rolled(pack, target - when_first), rolled(pack, target - otherwise)
        )

    copies = []
    full_low = low_ref[...]
    full_high = high_ref[...]
    lane = lanes_of(full_low)
    for i in range(19):
        step_x, step_y, step_z = VELOCITIES[i]
        for p in range(2):
            q = p - step_x
            if q not in (0, 1):
                continue
            tile = post_ref.at[i, q]
            if step_y or step_z:
                value = post_ref[i, q]
                if step_z == 1:
                    edge = edge_value(full_low, q, 3 + Z_UP.index(i), 0)
                    value = jnp.where(lane == 0, edge, rolled(value, 1))
                elif step_z == -1:
                    edge = edge_value(full_high, q, 3 + Z_DOWN.index(i), width - 1)
                    value = jnp.where(lane == width - 1, edge, rolled(value, -1))
                back = OPPOSITE[i]
                tile = shifted.at[i, p]
                if step_y == 1:
                    tile[1:height, :] = value[: height - 1]
                    tile[0:1, :] = post_ref[back, p, 0:1, :]
                elif step_y == -1:
                    tile[0 : height - 1, :] = value[1:]
                    tile[height - 1 : height, :] = post_ref[back, p, height - 1 : height, :]
                else:
                    tile[...] = value
            copies.append(pltpu.make_async_copy(tile, read_ref.at[i, p], sems.at[len(copies)]))
            copies[-1].start()

    for p in range(2):
        sign = 2 * p - 1

        def rows(start, p=p, sign=sign):
            at = pl.ds(start, ROWS)
            upper = pl.ds(start + 9, ROWS)
            lower = pl.ds(start + 7, ROWS)
            cl_pack = conf_low[at, :]
            ch_pack = conf_high[at, :]
            l_pack = low_ref[at, :]
            h_pack = high_ref[at, :]
            lane = lanes_of(cl_pack)
            first = lane == 0
            final = lane == width - 1
            velocity = [velo_tall[a, p, pl.ds(start + 8, ROWS), :] for a in range(3)]
            grad = [[None] * 3 for _ in range(3)]
            for a in range(3):
                grad[0][a] = (-0.5 * sign) * velo_tall[a, 1 - p, pl.ds(start + 8, ROWS), :]
                grad[1][a] = 0.5 * (velo_tall[a, p, upper, :] - velo_tall[a, p, lower, :])
                above = jnp.where(
                    final, edge_value(h_pack, p, a, width - 1), rolled(velocity[a], -1)
                )
                below = jnp.where(first, edge_value(l_pack, p, a, 0), rolled(velocity[a], 1))
                grad[2][a] = 0.5 * (above - below)
            own = [conf_ref[f, p, at, :] for f in range(6)]
            peterlin = (1.0 / RELAX_TIME) * peterlin_of(own[0], own[1], own[2])
            for f in range(6):
                i, j = COMPONENT_PAIRS[f]
                x_in = conf_ref[f, 1 - p, at, :]
                x_out = halo[p, f, at, :]
                y_up = conf_tall[f, p, upper, :]
                y_low = conf_tall[f, p, lower, :]
                lane_number = 6 * p + f
                z_up = jnp.where(
                    final, rolled(ch_pack, width - 1 - lane_number), rolled(own[f], -1)
                )
                z_low = jnp.where(first, rolled(cl_pack, -lane_number), rolled(own[f], 1))
                around = (x_in + x_out) + (y_up + y_low) + (z_up + z_low)
                advect = (
                    (sign * velocity[0]) * (x_out - x_in)
                    + velocity[1] * (y_up - y_low)
                    + velocity[2] * (z_up - z_low)
                )
                stretch = None
                for k in range(3):
                    term = own[SYMMETRIC_INDEX[i][k]] * grad[k][j]
                    if i != j:
                        term = term + grad[k][i] * own[SYMMETRIC_INDEX[k][j]]
                    stretch = term if stretch is None else stretch + term
                if i == j:
                    stretch = 2.0 * stretch
                relax = peterlin * own[f]
                if f < 3:
                    relax = relax - 1.0 / RELAX_TIME
                part_ref[f, p, at, :] = (
                    own[f]
                    - 0.5 * advect
                    + stretch
                    - relax
                    + DIFFUSIVITY * (around - 6.0 * own[f])
                )

        for_rows(height, rows)
    for copy in copies:
        copy.wait()


def inner(plane_e, plane_o, conform, halos, conf_low, conf_high, low, high, post, velo_e, velo_o):
    height, width = conform.shape[2:]
    velo_spec = pl.BlockSpec((3, height, width), lambda g: (0, 0, 0))
    whole = lambda shape: pl.BlockSpec(shape, lambda g: (0,) * len(shape))
    return pl.pallas_call(
        inner_kernel,
        grid=(1,),
        out_shape=(
            jax.ShapeDtypeStruct(post.shape, F32),
            jax.ShapeDtypeStruct(conform.shape, F32),
        ),
        in_specs=[
            pl.BlockSpec(memory_space=pltpu.SMEM),
            pl.BlockSpec(memory_space=pltpu.SMEM),
            whole(conform.shape),
            *[whole(halo.shape) for halo in halos],
            whole(conf_low.shape),
            whole(conf_low.shape),
            whole(conf_low.shape),
            whole(conf_low.shape),
            whole(post.shape),
            velo_spec,
            velo_spec,
        ],
        out_specs=(any_spec(), whole(conform.shape)),
        scratch_shapes=[
            VMEM((6, 2, height + 16, width), F32),
            VMEM((3, 2, height + 16, width), F32),
            VMEM((2, 6, height, width), F32),
            VMEM(post.shape, F32),
            VMEM((height, width), F32),
            VMEM((height, width), F32),
            VMEM((height, width), F32),
            VMEM((height, width), F32),
            pltpu.SemaphoreType.DMA((28,)),
        ],
        compiler_params=params(),
        name="inner",
    )(plane_e, plane_o, conform, *halos, conf_low, conf_high, low, high, post, velo_e, velo_o)


def touch_kernel(_, out_ref):
    out_ref[...] = jnp.zeros_like(out_ref)


def touch(value):
    return pl.pallas_call(
        touch_kernel,
        out_shape=jax.ShapeDtypeStruct((8, 128), F32),
        in_specs=[any_spec()],
        out_specs=vmem_spec(),
        compiler_params=params(),
        name="touch",
    )(value)


def targets_of(read_ref, plane):
    return [
        read_ref.at[jnp.where(plane == 1, MINUS[slot], PLUS[slot]), plane] for slot in range(5)
    ]


def finish_kernel(
    plane_e,
    plane_o,
    part_ref,
    conf_ref,
    got_e,
    sent_e,
    got_o,
    sent_o,
    _,
    __,
    read_ref,
    new_ref,
    read_tile,
    new_tile,
    sems,
):
    height = conf_ref.shape[2]
    faces = ((plane_o[0], got_o, sent_o), (plane_e[0], got_e, sent_e))
    copies = []

    def send(source, target):
        copies.append(pltpu.make_async_copy(source, target, sems.at[len(copies)]))
        copies[-1].start()

    for face, (plane, got, sent) in enumerate(faces):
        half_sign = jnp.where(plane == 1, 0.5, -0.5).astype(F32)
        tile = read_tile.at[face]
        targets = targets_of(read_ref, plane)
        send(got.at[3], targets[0])

        def rows(start, face=face, plane=plane, half_sign=half_sign, got=got):
            at = pl.ds(start, ROWS)
            slope = [half_sign * got[a, at, :] for a in range(3)]
            row = [conf_ref[f, plane, at, :] for f in (0, 3, 4)]
            for f in range(6):
                i, j = COMPONENT_PAIRS[f]
                if i == j:
                    term = 2.0 * (row[i] * slope[j])
                else:
                    term = row[i] * slope[j] + slope[i] * row[j]
                new_tile[face, f, at, :] = part_ref[f, plane, at, :] + term

        for_rows(height, rows)
        send(new_tile.at[face], new_ref.at[:, plane])
        tile[0, 1:height, :] = got[4, 0 : height - 1, :]
        tile[0, 0:1, :] = sent[5, 0:1, :]
        send(tile.at[0], targets[1])
        tile[1, 0 : height - 1, :] = got[5, 1:height, :]
        tile[1, height - 1 : height, :] = sent[4, height - 1 : height, :]
        send(tile.at[1], targets[2])
    for copy in copies:
        copy.wait()


def last_kernel(plane_e, plane_o, slant_e, slant_o, _, read_ref, sems):
    copies = []
    for plane, slant in ((plane_o[0], slant_o), (plane_e[0], slant_e)):
        targets = targets_of(read_ref, plane)
        for slot in (3, 4):
            copies.append(
                pltpu.make_async_copy(slant.at[slot - 3], targets[slot], sems.at[len(copies)])
            )
            copies[-1].start()
    for copy in copies:
        copy.wait()


def finish(plane_e, plane_o, part, conform, even, odd, slant_e, slant_o, read):
    height, width = conform.shape[2:]
    smem = pl.BlockSpec(memory_space=pltpu.SMEM)
    read_shape = jax.ShapeDtypeStruct(read.shape, F32)
    read, new = pl.pallas_call(
        finish_kernel,
        out_shape=(read_shape, jax.ShapeDtypeStruct(conform.shape, F32)),
        in_specs=[smem] * 2 + [vmem_spec()] * 6 + [any_spec()] * 2,
        out_specs=(any_spec(), any_spec()),
        scratch_shapes=[
            VMEM((2, 2, height, width), F32),
            VMEM((2, 6, height, width), F32),
            pltpu.SemaphoreType.DMA((8,)),
        ],
        input_output_aliases={8: 0},
        compiler_params=params(),
        name="finish",
    )(plane_e, plane_o, part, conform, *even, *odd, read, touch(even[0]))
    read = pl.pallas_call(
        last_kernel,
        out_shape=read_shape,
        in_specs=[smem] * 2 + [vmem_spec()] * 2 + [any_spec()],
        out_specs=any_spec(),
        scratch_shapes=[pltpu.SemaphoreType.DMA((4,))],
        input_output_aliases={4: 0},
        compiler_params=params(),
        name="last",
    )(plane_e, plane_o, slant_e, slant_o, read)
    return read, new


def body(popul, conform):
    wide = lax.axis_size("wide")
    narrow = lax.axis_size("narrow")
    odd = lax.rem(lax.axis_index("wide"), 2)
    plane_e = (1 - odd).astype(jnp.int32).reshape(1)
    plane_o = odd.astype(jnp.int32).reshape(1)
    even_pairs = [(i, i ^ 1) for i in range(wide)]
    odd_pairs = [(i, (i + 1) % wide if i % 2 else (i - 1) % wide) for i in range(wide)]
    up = [(i, (i + 1) % narrow) for i in range(narrow)]
    down = [(j, i) for i, j in up]

    conform, early, late = load(plane_e, conform)
    early_e = lax.ppermute(early, "wide", even_pairs)
    late_e = lax.ppermute(late, "wide", even_pairs)
    conf_up, conf_down = edges(conform)
    conf_low = lax.ppermute(conf_up, "narrow", up)
    conf_high = lax.ppermute(conf_down, "narrow", down)
    early, late = pick(plane_o, conform, conf_up)
    popul, sums = moments(popul, early)
    early_o = lax.ppermute(early, "wide", odd_pairs)
    late_o = lax.ppermute(late, "wide", odd_pairs)
    pre = prepare(conform, conf_low, conf_high)
    post, sent_e, slant_e, z_up, z_down = collide(plane_e, popul, sums, pre, early_e)
    got_e = lax.ppermute(sent_e, "wide", even_pairs)
    post, sent_o, slant_o, z_up, z_down = collide(
        plane_o, popul, sums, pre, early_o, (post, z_up, z_down, late_e)
    )
    got_o = lax.ppermute(sent_o, "wide", odd_pairs)
    low = lax.ppermute(z_up, "narrow", up)
    high = lax.ppermute(z_down, "narrow", down)
    slant_e, slant_o = slants(plane_e, plane_o, low, high, slant_e, slant_o)
    slant_e = lax.ppermute(slant_e, "wide", even_pairs)
    slant_o = lax.ppermute(slant_o, "wide", odd_pairs)
    read, part = inner(
        plane_e,
        plane_o,
        conform,
        (early_e, late_e, early_o, late_o),
        conf_low,
        conf_high,
        low,
        high,
        post,
        sent_e,
        sent_o,
    )
    even = (got_e, sent_e)
    odd = (got_o, sent_o)
    return finish(plane_e, plane_o, part, conform, even, odd, slant_e, slant_o, read)


def solution(mesh):
    placed = P(None, "wide", None, "narrow")
    return jax.shard_map(
        body, mesh=mesh, in_specs=(placed, placed), out_specs=(placed, placed), check_vma=False
    )
```
